32 devices in a mesh: fsdp: 4 (over y, x), rep: 8 (over z, core).
Axes of the slice: x: 2, y: 2, z: 4, core: 2. Of those that a mesh axis runs over, the one named last changes fastest.
Arguments:
- tokens: bfloat16 [8, 4096, 768], P('rep', 'fsdp'), may hold values from -6 to 6
- counts: int32 [8, 32], P('rep', 'fsdp'), may hold values from 1 to 128, as said below
- cotangent: bfloat16 [8, 4096, 768], P('rep', 'fsdp'), may hold values from -6 to 6
- swe_qkv: bfloat16 [768, 2304], P(('fsdp', 'rep')), may hold values from -0.21875 to 0.21875
- swe_out: bfloat16 [768, 768], P(('fsdp', 'rep')), may hold values from -2.5 to 2.5
- swe_up: bfloat16 [768, 3072], P(('fsdp', 'rep')), may hold values from -0.21875 to 0.21875
- swe_down: bfloat16 [3072, 768], P(('fsdp', 'rep')), may hold values from -0.109375 to 0.109375
- swe_gains: bfloat16 [2, 768], P(None, ('fsdp', 'rep')), may hold values from 0.099609375 to 1.8984375
- swe_biases: bfloat16 [2, 768], P(None, ('fsdp', 'rep')), may hold values from -1.796875 to 1.796875
- cse_qkv: bfloat16 [768, 2304], P(('fsdp', 'rep')), may hold values from -0.21875 to 0.21875
- cse_out: bfloat16 [768, 768], P(('fsdp', 'rep')), may hold values from -1.25 to 1.25
- cse_up: bfloat16 [768, 3072], P(('fsdp', 'rep')), may hold values from -0.21875 to 0.21875
- cse_down: bfloat16 [3072, 768], P(('fsdp', 'rep')), may hold values from -0.109375 to 0.109375
- cse_gains: bfloat16 [2, 768], P(None, ('fsdp', 'rep')), may hold values from 0.099609375 to 1.8984375
- cse_biases: bfloat16 [2, 768], P(None, ('fsdp', 'rep')), may hold values from -1.796875 to 1.796875
- positions: bfloat16 [32, 768], P(None, ('fsdp', 'rep')), may hold values from -6 to 6
Outputs:
- layer_out: bfloat16 [8, 4096, 768], P('rep', 'fsdp')
- token_grad: bfloat16 [8, 4096, 768], P('rep', 'fsdp')
- grad_swe_qkv: float32 [768, 2304], P('fsdp')
- grad_swe_out: float32 [768, 768], P('fsdp')
- grad_swe_up: float32 [768, 3072], P('fsdp')
- grad_swe_down: float32 [3072, 768], P('fsdp')
- grad_swe_gains: float32 [2, 768], P(None, 'fsdp')
- grad_swe_biases: float32 [2, 768], P(None, 'fsdp')
- grad_cse_qkv: float32 [768, 2304], P('fsdp')
- grad_cse_out: float32 [768, 768], P('fsdp')
- grad_cse_up: float32 [768, 3072], P('fsdp')
- grad_cse_down: float32 [3072, 768], P('fsdp')
- grad_cse_gains: float32 [2, 768], P(None, 'fsdp')
- grad_cse_biases: float32 [2, 768], P(None, 'fsdp')
- grad_positions: float32 [32, 768], P(None, 'fsdp')
The draws below stay inside these ranges and needn't reach their ends.
Inputs may be any that keep to these rules, and one draw needn't show every extreme that they name: counts[d, s] is the number of true tokens in segment s of document d: a document's true tokens fill its segments from the first, every segment before the one that holds its last true token is full, and every segment after it holds only its first token.
All inputs are finite; a program needn't handle non-finite values.
Results may differ from the reference program's by a relative error of at most 0.035.
Values may be sent and summed in bfloat16 or wider, within the bound.
No kernel may reach another device: no remote copies, remote signals or barrier semaphores. Data moves between devices by JAX's collectives and lax.ppermute only.
A program may use at most 256 MiB of HBM per device.

```python
import jax
import jax.numpy as jnp
from jax import lax

D = 768
HEAD = 64
FF = 3072
SEG = 128
SEGS = 32
DOCLEN = 4096
DOCS = 8


def draw_counts(key, part):
    doc_ends = jax.random.randint(key, (DOCS, 1), SEGS * SEG // 2, SEGS * SEG - SEG + 2, dtype=jnp.int32)
    seg_starts = jnp.arange(SEGS, dtype=jnp.int32)[None, :] * SEG
    return jnp.clip(doc_ends - seg_starts, 1, SEG).astype(jnp.int32)


def block_scale(key, shape, shards, least, high):
    def one(axis_at, parts):
        steps = jax.random.uniform(jax.random.fold_in(jax.random.fold_in(key, 6), axis_at), (parts,), jnp.float32, least / len(shards), high / len(shards))
        return jnp.repeat(jnp.exp(steps), shape[axis_at] // parts).reshape((-1,) + (1,) * (len(shape) - axis_at - 1))

    gain = one(*shards[0])
    for cut in shards[1:]:
        gain = gain * one(*cut)
    return gain


def scatter_about(key, dims, spread, bound, pieces=(), kind=jnp.bfloat16):
    entries = spread * jax.random.normal(key, dims, jnp.float32)
    if pieces:
        entries = entries * block_scale(key, dims, pieces, -0.22, 0.18)
    return jnp.clip(entries, -bound, bound).astype(kind)


def setup_inputs(seed: int = 0) -> dict:
    key_of = jax.random.split(jax.random.key(seed), 17)
    return {
        "tokens": scatter_about(key_of[0], (DOCS, DOCLEN, D), 1.0, 6.0, ((0, 8), (1, 4))),
        "counts": draw_counts(jax.random.fold_in(key_of[16], 71), 0),
        "cotangent": scatter_about(key_of[2], (DOCS, DOCLEN, D), 1.0, 6.0, ((0, 8), (1, 4))),
        "swe_qkv": scatter_about(key_of[3], (D, 3 * D), D ** -0.5, 0.21875, ((0, 32),)),
        "swe_out": scatter_about(key_of[4], (D, D), (D // SEG) ** -0.5, 2.5, ((0, 32),)),
        "swe_up": scatter_about(key_of[5], (D, FF), D ** -0.5, 0.21875, ((0, 32),)),
        "swe_down": scatter_about(key_of[6], (FF, D), FF ** -0.5, 0.109375, ((0, 32),)),
        "swe_gains": jnp.clip(1.0 + 0.18 * jax.random.normal(key_of[7], (2, D), jnp.float32), 0.099609375, 1.8984375).astype(jnp.bfloat16),
        "swe_biases": scatter_about(key_of[8], (2, D), 0.3, 1.796875, ((1, 32),)),
        "cse_qkv": scatter_about(key_of[9], (D, 3 * D), D ** -0.5, 0.21875, ((0, 32),)),
        "cse_out": scatter_about(key_of[10], (D, D), (D // SEGS) ** -0.5, 1.25, ((0, 32),)),
        "cse_up": scatter_about(key_of[11], (D, FF), D ** -0.5, 0.21875, ((0, 32),)),
        "cse_down": scatter_about(key_of[12], (FF, D), FF ** -0.5, 0.109375, ((0, 32),)),
        "cse_gains": jnp.clip(1.0 + 0.18 * jax.random.normal(key_of[13], (2, D), jnp.float32), 0.099609375, 1.8984375).astype(jnp.bfloat16),
        "cse_biases": scatter_about(key_of[14], (2, D), 0.3, 1.796875, ((1, 32),)),
        "positions": scatter_about(key_of[15], (SEGS, D), 1.0, 6.0, ((1, 32),)),
    }


@jax.custom_vjp
def low(v):
    return lax.optimization_barrier(v.astype(jnp.bfloat16)).astype(jnp.float32)

@jax.custom_vjp
def low_back(v):
    return v

def low_keep(v):
    return (low(v), None)

def low_pass(kept, grad):
    return (grad,)

def back_keep(v):
    return (v, None)

def back_low(kept, grad):
    return (low(grad),)
low.defvjp(low_keep, low_pass)
low_back.defvjp(back_keep, back_low)
norm_eps = 1e-05
masked_score = -1000000000.0

def layer_norm(summed_in, gain_row, bias_row):
    row_mean = lax.optimization_barrier(jnp.mean(summed_in, axis=-1, keepdims=True))
    centered = summed_in - row_mean
    variance = lax.optimization_barrier(jnp.mean(centered * centered, axis=-1, keepdims=True))
    return centered * lax.rsqrt(variance + norm_eps) * gain_row + bias_row

def block(seg_rows, key_mask, proj_qkv, proj_out, proj_up, proj_down, gain_rows, bias_rows):
    high = lax.Precision.HIGHEST
    groups, length, model_width = seg_rows.shape
    head_count = model_width // HEAD
    packed = low_back(low(jnp.einsum('gsd,de->gse', seg_rows, proj_qkv, precision=high)))
    packed = packed.reshape(groups, length, 3, head_count, HEAD)
    queries, key_rows, value_rows = (packed[:, :, 0], packed[:, :, 1], packed[:, :, 2])
    scores = low_back(jnp.einsum('gqhe,gkhe->ghqk', queries, key_rows, precision=high) * HEAD ** (-0.5))
    scores = jnp.where(key_mask[:, None, None, :], scores, masked_score)
    softmax_w = jax.nn.softmax(scores, axis=-1)
    mixed_heads = jnp.einsum('ghqk,gkhe->gqhe', low(softmax_w), value_rows, precision=high)
    mixed_flat = low_back(low(mixed_heads)).reshape(groups, length, model_width)
    attended = low_back(jnp.einsum('gsd,de->gse', mixed_flat, proj_out, precision=high))
    first_norm = layer_norm(seg_rows + attended, gain_rows[0], bias_rows[0])
    inner_pre = low_back(jnp.einsum('gsd,df->gsf', low(first_norm), proj_up, precision=high))
    activated = low(jax.nn.gelu(inner_pre, approximate=False))
    outer_out = low_back(jnp.einsum('gsf,fd->gsd', activated, proj_down, precision=high))
    return layer_norm(first_norm + outer_out, gain_rows[1], bias_rows[1])

def document(doc_pair, params):
    doc_tokens, doc_counts = doc_pair
    segments = doc_tokens.reshape(SEGS, SEG, D)
    is_valid = jnp.arange(SEG, dtype=jnp.int32)[None, :] < doc_counts[:, None]
    valid_f = is_valid.astype(jnp.float32)
    hidden = block(segments, is_valid, *params[0:6]) * valid_f[..., None]
    cls_in = low(hidden[:, 0, :] + params[12])
    cls_out = block(cls_in[None], jnp.ones((1, SEGS), dtype=jnp.bool_), *params[6:12])[0]
    return hidden.at[:, 0, :].set(cls_out).reshape(SEG * SEGS, D)

def reference(tokens, counts, cotangent, swe_qkv, swe_out, swe_up, swe_down, swe_gains, swe_biases, cse_qkv, cse_out, cse_up, cse_down, cse_gains, cse_biases, positions):
    params = tuple((arr.astype(jnp.float32) for arr in (swe_qkv, swe_out, swe_up, swe_down, swe_gains, swe_biases, cse_qkv, cse_out, cse_up, cse_down, cse_gains, cse_biases, positions)))

    def forward(inputs, weights_in):
        per_doc = jax.checkpoint(lambda doc_pair: document(doc_pair, weights_in))
        return lax.map(per_doc, (inputs, counts))
    outputs, pullback = jax.vjp(forward, tokens.astype(jnp.float32), params)
    input_grad, weight_grads = pullback(cotangent.astype(jnp.float32))
    return (outputs.astype(jnp.bfloat16), input_grad.astype(jnp.bfloat16), weight_grads[0], weight_grads[1], weight_grads[2], weight_grads[3], weight_grads[4], weight_grads[5], weight_grads[6], weight_grads[7], weight_grads[8], weight_grads[9], weight_grads[10], weight_grads[11], weight_grads[12])
```

```python
import math

import jax
import jax.numpy as jnp
from jax import lax
from jax.sharding import Mesh
from jax.sharding import PartitionSpec as P

HEAD = 64
norm_eps = 1e-05
masked_score = -1000000000.0
bf16, f32 = jnp.bfloat16, jnp.float32


def product(left_op, right_op, einsum_form):
    return jnp.einsum(einsum_form, left_op, right_op, preferred_element_type=f32)


def swap(value, axis, bit):
    size = lax.axis_size(axis)
    return lax.ppermute(value, axis, [(i, i ^ bit) for i in range(size)])


def bit_of(axis, bit):
    return (lax.axis_index(axis) // bit) % 2


def join(mine, other, side, axis):
    first = side == 0
    return jnp.stack([jnp.where(first, mine, other), jnp.where(first, other, mine)], axis=axis)


def part(value, side, axis):
    return lax.dynamic_index_in_dim(value, side, axis, keepdims=False)


def bits_down(size):
    return [1 << k for k in reversed(range(size.bit_length() - 1))]


def gather_z(value):
    size = lax.axis_size("z")
    inner = value.shape
    got = value[None]
    for level, bit in enumerate(bits_down(size)):
        other = swap(got, "z", bit)
        got = join(got, other, bit_of("z", bit), 1)
        got = got.reshape((2 ** (level + 1),) + inner)
    return got


def gather_c(value, axis):
    return join(value, swap(value, "c", 1), lax.axis_index("c"), axis)


def gather_rows(shard):
    rows, cols = shard.shape
    col_z = gather_z(shard)
    half = (cols // 256) * 128
    one, two = col_z[:, :, :half], col_z[:, :, half:]
    y, x = lax.axis_index("y"), lax.axis_index("x")
    one = join(one, swap(one, "x", 1), x, 0)
    two = join(two, swap(two, "y", 1), y, 0)
    one = join(one, swap(one, "y", 1), y, 0)
    two = join(two, swap(two, "x", 1), x, 1)
    both = jnp.concatenate([one, two], axis=-1)
    both = gather_c(both, 3)
    return both.reshape(-1, cols)


def swap_f(value, dist):
    count = lax.axis_size("y") * lax.axis_size("x")
    return lax.ppermute(value, ("y", "x"), [(i, i ^ dist) for i in range(count)])


def in_order(parts):
    y, x = lax.axis_index("y"), lax.axis_index("x")
    row0 = [jnp.where(x == 0, parts[0], parts[1]), jnp.where(x == 0, parts[1], parts[0])]
    row1 = [jnp.where(x == 0, parts[2], parts[3]), jnp.where(x == 0, parts[3], parts[2])]
    top, low = jnp.stack(row0), jnp.stack(row1)
    return jnp.concatenate([jnp.where(y == 0, top, low), jnp.where(y == 0, low, top)])


def gather_f(value):
    return in_order([value] + [swap_f(value, d) for d in (1, 2, 3)])


def sum_f(value):
    got = [value] + [swap_f(value, d) for d in (1, 2, 3)]
    return (got[0] + got[1]) + (got[2] + got[3])


def reduce_rows(grad):
    rows, cols = grad.shape
    zsize = lax.axis_size("z")
    count = lax.axis_size("y") * lax.axis_size("x")
    y, x, c = lax.axis_index("y"), lax.axis_index("x"), lax.axis_index("c")
    f = y * lax.axis_size("x") + x
    per = rows // count // 2
    halves = grad.reshape(count, 2, per, cols)
    other = swap(part(halves, 1 - c, 1), "c", 1)
    chip = (part(halves, c, 1).astype(f32) + other.astype(f32)).astype(bf16)
    got = [part(chip, f, 0)] + [swap_f(part(chip, f ^ d, 0), d) for d in (1, 2, 3)]
    got = [g.astype(f32) for g in got]
    plane = ((got[0] + got[1]) + (got[2] + got[3])).astype(bf16)
    left = plane.reshape(zsize, per // zsize, cols)
    bit = 1
    while bit < zsize:
        side = bit_of("z", bit)
        pairs = left.reshape((-1, 2) + left.shape[1:])
        other = swap(part(pairs, 1 - side, 1), "z", bit)
        left = (part(pairs, side, 1).astype(f32) + other.astype(f32)).astype(bf16)
        bit *= 2
    whole = gather_z(left[0]).reshape(per, cols)
    return gather_c(whole, 0).reshape(2 * per, cols)


def normalize(summed_in, gain_row, bias_row):
    row_mean = jnp.mean(summed_in, axis=-1, keepdims=True)
    centered = summed_in - row_mean
    inv_dev = lax.rsqrt(jnp.mean(centered * centered, axis=-1, keepdims=True) + norm_eps)
    unit_rows = centered * inv_dev
    return (unit_rows * gain_row + bias_row, unit_rows, inv_dev)


def norm_back(upstream, unit_rows, inv_dev, gain_row):
    scaled = upstream * gain_row
    grad_in = inv_dev * (
        scaled
        - jnp.mean(scaled, axis=-1, keepdims=True)
        - unit_rows * jnp.mean(scaled * unit_rows, axis=-1, keepdims=True)
    )
    sums = tuple(range(upstream.ndim - 1))
    return (grad_in, jnp.sum(upstream * unit_rows, axis=sums), jnp.sum(upstream, axis=sums))


def gelu_pair(inner_pre):
    cumul = 0.5 * (1.0 + lax.erf(inner_pre * 0.7071067811865476))
    return (
        inner_pre * cumul,
        cumul + inner_pre * jnp.exp(-0.5 * inner_pre * inner_pre) * 0.3989422804014327,
    )


def masked_scores(query_rows, key_rows, key_mask):
    raw_scores = product(query_rows, key_rows, "gqhe,gkhe->ghqk") * (1.0 / math.sqrt(HEAD))
    return jnp.where(key_mask[:, None, None, :], raw_scores, masked_score)


def attend(query_rows, key_rows, value_rows, key_mask):
    scores = masked_scores(query_rows, key_rows, key_mask)
    row_max = jnp.max(scores, axis=-1, keepdims=True)
    log_total = row_max + jnp.log(jnp.sum(jnp.exp(scores - row_max), axis=-1, keepdims=True))
    softmax_w = jnp.exp(scores - log_total).astype(bf16)
    mixed_heads = product(softmax_w, value_rows, "ghqk,gkhe->gqhe").astype(bf16)
    return (mixed_heads, log_total)


def attend_back(query_rows, key_rows, value_rows, key_mask, log_total, grad_mixed):
    scores = masked_scores(query_rows, key_rows, key_mask)
    softmax_w = jnp.exp(scores - log_total)
    grad_value = product(softmax_w.astype(bf16), grad_mixed, "ghqk,gqhe->gkhe")
    grad_probs = product(grad_mixed, value_rows, "gqhe,gkhe->ghqk")
    grad_scores = (
        softmax_w * (grad_probs - jnp.sum(softmax_w * grad_probs, axis=-1, keepdims=True))
    ).astype(bf16)
    inv_root = 1.0 / math.sqrt(HEAD)
    grad_query = product(grad_scores, key_rows, "ghqk,gkhe->gqhe") * inv_root
    grad_key = product(grad_scores, query_rows, "ghqk,gqhe->gkhe") * inv_root
    return (grad_query, grad_key, grad_value)


def split_heads(packed, head_count):
    stacked = packed.reshape(packed.shape[0], packed.shape[1], 3, head_count, HEAD)
    return (stacked[:, :, 0], stacked[:, :, 1], stacked[:, :, 2])


def finish(resid_in, mixed_flat, proj_out, proj_up, proj_down, gain_rows, bias_rows):
    attended = product(mixed_flat, proj_out, "gsd,de->gse")
    first_norm, unit_one, inv_one = normalize(resid_in + attended, gain_rows[0], bias_rows[0])
    first_low = first_norm.astype(bf16)
    inner_pre = product(first_low, proj_up, "gsd,df->gsf")
    activated, gelu_slope = gelu_pair(inner_pre)
    act_low = activated.astype(bf16)
    outer_out = product(act_low, proj_down, "gsf,fd->gsd")
    normed_out, unit_two, inv_two = normalize(first_norm + outer_out, gain_rows[1], bias_rows[1])
    return (normed_out, (unit_one, inv_one, first_low, gelu_slope, act_low, unit_two, inv_two))


def finish_back(upstream, mixed_flat, saved_parts, proj_out, proj_up, proj_down, gain_rows):
    unit_one, inv_one, first_low, gelu_slope, act_low, unit_two, inv_two = saved_parts
    grad_two, gain_two, bias_two = norm_back(upstream, unit_two, inv_two, gain_rows[1])
    grad_outer = grad_two.astype(bf16)
    grad_down = product(act_low, grad_outer, "gsf,gsd->fd")
    grad_inner = (product(grad_outer, proj_down, "gsd,fd->gsf") * gelu_slope).astype(bf16)
    grad_up = product(first_low, grad_inner, "gsd,gsf->df")
    grad_first = grad_two + product(grad_inner, proj_up, "gsf,df->gsd")
    grad_one, gain_one, bias_one = norm_back(grad_first, unit_one, inv_one, gain_rows[0])
    grad_attended = grad_one.astype(bf16)
    grad_out = product(mixed_flat, grad_attended, "gsd,gse->de")
    grad_mixed = product(grad_attended, proj_out, "gse,de->gsd").astype(bf16)
    return (grad_one, grad_mixed, grad_out, grad_up, grad_down, (gain_one, gain_two, bias_one, bias_two))


def cross_weights(cse_qkv, cse_out, cse_up, cse_down, fsize, f):
    rows, width = cse_qkv.shape[0], cse_out.shape[1]
    ff = cse_up.shape[1]
    slim = width // fsize
    cols = jnp.concatenate(
        [
            cse_qkv.reshape(rows, 3, fsize, slim).transpose(2, 0, 1, 3).reshape(fsize, rows, 3 * slim),
            cse_up.reshape(rows, fsize, ff // fsize).transpose(1, 0, 2),
        ],
        axis=-1,
    )
    mine = in_order([part(cols, f, 0)] + [swap_f(part(cols, f ^ d, 0), d) for d in (1, 2, 3)])
    flat = mine.reshape(fsize * rows, -1)
    frows = cse_down.shape[0]
    out_flat = cse_out.reshape(frows, -1)
    message = jnp.concatenate([flat, cse_down, out_flat], axis=-1)
    whole = gather_c(gather_z(message), 1)
    reps = whole.shape[0] * whole.shape[1]
    whole = whole.reshape(reps, frows, -1)
    a, b = 3 * slim, 3 * slim + ff // fsize
    by_row = whole[:, :, :b].reshape(reps, fsize, rows, b).transpose(1, 0, 2, 3).reshape(-1, b)
    qkv = by_row[:, :a]
    up = by_row[:, a:]
    down = whole[:, :, b : b + width].reshape(-1, width)
    out = whole[:, :, b + width :].reshape(-1, width)
    return qkv, out, up, down


def cross_block(cls_in, cotan, weights, gains, biases, fsize, f):
    qkv, out, up, down = weights
    segs, width = cls_in.shape
    slim = width // fsize
    heads = slim // HEAD
    packed = product(cls_in[None], qkv, "gsd,de->gse").astype(bf16)
    queries, keys, values = split_heads(packed, heads)
    every = jnp.ones((1, segs), jnp.bool_)
    mixed, log_total = attend(queries, keys, values, every)
    mixed = mixed.reshape(segs, slim)
    attended = sum_f(product(mixed, out, "sd,de->se"))
    first, unit_one, inv_one = normalize(cls_in.astype(f32) + attended, gains[0], biases[0])
    first_low = first.astype(bf16)
    activated, slope = gelu_pair(product(first_low, up, "sd,df->sf"))
    act_low = activated.astype(bf16)
    outer = sum_f(product(act_low, down, "sf,fd->sd"))
    cls_out, unit_two, inv_two = normalize(first + outer, gains[1], biases[1])

    grad_two, gain_two, bias_two = norm_back(cotan, unit_two, inv_two, gains[1])
    grad_outer = grad_two.astype(bf16)
    grad_inner = (product(grad_outer, down, "sd,fd->sf") * slope).astype(bf16)
    grad_first = grad_two + sum_f(product(grad_inner, up, "sf,df->sd"))
    grad_one, gain_one, bias_one = norm_back(grad_first, unit_one, inv_one, gains[0])
    grad_attended = grad_one.astype(bf16)
    grad_mixed = product(grad_attended, out, "se,de->sd").astype(bf16)
    grad_q, grad_k, grad_v = attend_back(
        queries, keys, values, every, log_total, grad_mixed.reshape(1, segs, heads, HEAD)
    )
    grad_packed = jnp.concatenate(
        [grad_q.reshape(segs, slim), grad_k.reshape(segs, slim), grad_v.reshape(segs, slim)], axis=-1
    ).astype(bf16)
    grad_in = grad_one + sum_f(product(grad_packed, qkv, "se,de->sd"))

    def own(value):
        return lax.dynamic_slice_in_dim(value, f * slim, slim, value.ndim - 1)

    sums = jnp.stack([gain_one, gain_two, bias_one, bias_two])
    sums = jnp.pad(own(sums), ((0, segs - 4), (0, 0)))
    spread = gather_f(jnp.concatenate([grad_packed, grad_inner], axis=-1))
    qkv_cols = spread[:, :, : 3 * slim].reshape(fsize, segs, 3, slim).transpose(1, 2, 0, 3)
    up_cols = spread[:, :, 3 * slim :].transpose(1, 0, 2)
    pieces = [
        qkv_cols.reshape(segs, 3 * width),
        up_cols.reshape(segs, -1),
        act_low,
        grad_outer,
        grad_attended,
        mixed,
        own(cls_in),
        own(first_low),
        own(grad_in).astype(bf16),
        sums.astype(bf16),
    ]
    ends, at = [], 0
    for piece in pieces:
        ends.append((at, at + piece.shape[1]))
        at += piece.shape[1]
    docs = gather_c(gather_z(jnp.concatenate(pieces, axis=-1)), 1)
    docs = docs.reshape(-1, segs, at)
    flat = docs.reshape(-1, at)
    cut = [flat[:, a:b] for a, b in ends]
    g_qkv = product(cut[6], cut[0], "rd,re->de")
    g_out = product(cut[5], cut[4], "rd,re->de")
    g_up = product(cut[7], cut[1], "rd,re->de")
    g_down = product(cut[2], cut[3], "rd,re->de")
    g_pos = jnp.sum(docs[:, :, ends[8][0] : ends[8][1]].astype(f32), axis=0)
    g_sums = jnp.sum(docs[:, :4, ends[9][0] : ends[9][1]].astype(f32), axis=0)
    return cls_out, grad_in, (g_qkv, g_out, g_up, g_down, g_sums[0:2], g_sums[2:4], g_pos)


def per_device(
    tokens, counts, cotangent,
    swe_qkv, swe_out, swe_up, swe_down, swe_gains, swe_biases,
    cse_qkv, cse_out, cse_up, cse_down, cse_gains, cse_biases, positions,
):
    docs_here, local_len, width = tokens.shape
    seg_here = counts.shape[1]
    seg_len = local_len // seg_here
    groups = docs_here * seg_here
    head_count = width // HEAD
    fsize = lax.axis_size("y") * lax.axis_size("x")
    f = lax.axis_index("y") * lax.axis_size("x") + lax.axis_index("x")
    segs = fsize * seg_here

    small = jnp.concatenate([swe_gains, swe_biases, cse_gains, cse_biases, positions], axis=0)
    count_small = small.shape[0]
    small = jnp.pad(small.T, ((0, 0), (0, -count_small % 128)))
    first_group = gather_rows(jnp.concatenate([swe_qkv, swe_out, small], axis=-1))
    w_qkv = first_group[:, : 3 * width]
    w_out = first_group[:, 3 * width : 4 * width]
    rows = first_group[:, 4 * width : 4 * width + count_small].T.astype(f32)
    gains, biases, cross_gains, cross_biases, pos = (
        rows[0:2], rows[2:4], rows[4:6], rows[6:8], rows[8:]
    )
    w_up = gather_rows(swe_up)
    w_down = gather_rows(swe_down)
    cross = cross_weights(cse_qkv, cse_out, cse_up, cse_down, fsize, f)

    seg_rows = tokens.reshape(groups, seg_len, width)
    is_valid = jnp.arange(seg_len, dtype=jnp.int32)[None, :] < counts.reshape(groups, 1)
    valid_f = is_valid.astype(f32)[..., None]
    packed = product(seg_rows, w_qkv, "gsd,de->gse").astype(bf16)
    queries, keys, values = split_heads(packed, head_count)
    mixed, log_total = attend(queries, keys, values, is_valid)
    mixed = mixed.reshape(groups, seg_len, width)
    normed, saved = finish(seg_rows.astype(f32), mixed, w_out, w_up, w_down, gains, biases)
    hidden = normed * valid_f

    pos_here = lax.dynamic_slice_in_dim(pos, f * seg_here, seg_here, 0)
    cls_here = (hidden[:, 0, :] + pos_here).astype(bf16)
    upstream = cotangent.reshape(groups, seg_len, width)
    both = gather_f(jnp.concatenate([cls_here, upstream[:, 0, :]], axis=-1)).reshape(segs, 2 * width)
    cls_out, cls_grad, cross_grads = cross_block(
        both[:, :width], both[:, width:].astype(f32), cross, cross_gains, cross_biases, fsize, f
    )
    cls_out = lax.dynamic_slice_in_dim(cls_out, f * seg_here, seg_here, 0)
    cls_grad = lax.dynamic_slice_in_dim(cls_grad, f * seg_here, seg_here, 0)
    layer_out = hidden.at[:, 0, :].set(cls_out).astype(bf16).reshape(tokens.shape)

    grad_hidden = upstream.astype(f32).at[:, 0, :].set(cls_grad) * valid_f
    resid, grad_mixed, grad_out, grad_up, grad_down, sums = finish_back(
        grad_hidden, mixed, saved, w_out, w_up, w_down, gains
    )
    sums = jnp.pad(jnp.stack(sums, axis=1), ((0, 0), (0, 124)))
    red_down = reduce_rows(grad_down.astype(bf16))
    red_up = reduce_rows(grad_up.astype(bf16))
    grad_q, grad_k, grad_v = attend_back(
        queries, keys, values, is_valid, log_total,
        grad_mixed.reshape(groups, seg_len, head_count, HEAD),
    )
    grad_packed = jnp.concatenate(
        [g.reshape(groups, seg_len, width) for g in (grad_q, grad_k, grad_v)], axis=2
    ).astype(bf16)
    grad_qkv = product(seg_rows, grad_packed, "gsd,gse->de")
    last = reduce_rows(jnp.concatenate([grad_qkv, grad_out, sums], axis=-1).astype(bf16)).astype(f32)
    token_grad = (resid + product(grad_packed, w_qkv, "gse,de->gsd")).astype(bf16)
    small_grads = last[:, 4 * width : 4 * width + 4].T
    return (
        layer_out,
        token_grad.reshape(tokens.shape),
        last[:, : 3 * width],
        last[:, 3 * width : 4 * width],
        red_up.astype(f32),
        red_down.astype(f32),
        small_grads[0:2],
        small_grads[2:4],
    ) + cross_grads


def solution(mesh):
    fsize, rsize = mesh.shape["fsdp"], mesh.shape["rep"]
    fine = Mesh(mesh.devices.reshape(2, fsize // 2, rsize // 2, 2), ("y", "x", "z", "c"))
    fs, rep = ("y", "x"), ("z", "c")
    every = fs + rep
    by_rows, by_cols = P(every, None), P(None, every)
    block = (by_rows,) * 4 + (by_cols,) * 2
    grads = (P(fs, None),) * 4 + (P(None, fs),) * 2
    return jax.shard_map(
        per_device,
        mesh=fine,
        in_specs=(P(rep, fs, None), P(rep, fs), P(rep, fs, None)) + block + block + (by_cols,),
        out_specs=(P(rep, fs, None),) * 2 + grads + grads + (P(None, fs),),
        check_vma=False,
    )
```

```python
import functools
import math

import jax
import jax.numpy as jnp
from jax import lax
from jax.experimental import pallas as pl
from jax.experimental.pallas import tpu as pltpu
from jax.sharding import Mesh
from jax.sharding import PartitionSpec as P

HEAD = 64
norm_eps = 1e-05
masked_score = -1000000000.0
bf16, f32 = jnp.bfloat16, jnp.float32
VMEM_CAP = 56 << 20


def tie(values, *after):
    return lax.optimization_barrier((values, after))[0]


def swap(value, axis, bit, then=()):
    size = lax.axis_size(axis)
    got = lax.ppermute(value, axis, [(i, i ^ bit) for i in range(size)])
    return tie(got, then) if then else got


def bit_of(axis, bit):
    return (lax.axis_index(axis) // bit) % 2


def join(mine, other, side, axis):
    first = side == 0
    return jnp.stack([jnp.where(first, mine, other), jnp.where(first, other, mine)], axis=axis)


def side_by_side(mine, other, side):
    both = jnp.concatenate([other, other], axis=-1)
    return lax.dynamic_update_slice_in_dim(both, mine, side * mine.shape[-1], axis=-1)


def part(value, side, axis):
    return lax.dynamic_index_in_dim(value, side, axis, keepdims=False)


def bits_down(size):
    return [1 << k for k in reversed(range(size.bit_length() - 1))]


class RowGather:
    def __init__(self, shard):
        rows, cols = shard.shape
        half = cols // 2
        c = lax.axis_index("c")
        keep = lax.dynamic_slice_in_dim(shard, c * half, half, 1)
        send = lax.dynamic_slice_in_dim(shard, (1 - c) * half, half, 1)
        self.state = join(keep, swap(send, "c", 1), c, 0).reshape(1, 2 * rows, half)

    def after(self, *others):
        self.state = tie(self.state, others)

    def far_z(self, *then):
        bits = bits_down(lax.axis_size("z"))
        for bit in bits[:-1]:
            self._along_z(bit, then)

    def near_z(self, *then):
        self._along_z(1, then)

    def _along_z(self, bit, then=()):
        got = self.state
        got = join(got, swap(got, "z", bit, then), bit_of("z", bit), 1)
        self.state = got.reshape((-1,) + got.shape[2:])

    def plane_first(self, *then):
        zhalf = self.state.shape[0] // 2
        one, two = self.state[:zhalf], self.state[zhalf:]
        got_one, got_two = swap(one, "x", 1, then), swap(two, "y", 1, then)
        self.state = join(one, got_one, lax.axis_index("x"), 0), join(two, got_two, lax.axis_index("y"), 0)

    def plane_second(self, *then):
        one, two = self.state
        got_one, got_two = swap(one, "y", 1, then), swap(two, "x", 1, then)
        one = join(one, got_one, lax.axis_index("y"), 0)
        two = join(two, got_two, lax.axis_index("x"), 1)
        both = jnp.concatenate([one, two], axis=2)
        self.state = both.reshape(-1, both.shape[-1])

    def sibling(self, *then):
        self.state = self.state, swap(self.state, "c", 1, then)


class RepGather:
    def __init__(self, message):
        self.state = message[None]

    far_z = RowGather.far_z
    near_z = RowGather.near_z
    after = RowGather.after

    def _along_z(self, bit, then=()):
        got = self.state
        got = join(got, swap(got, "z", bit, then), bit_of("z", bit), 1)
        self.state = got.reshape((-1,) + got.shape[2:])

    def sibling(self, *then):
        self.state = join(self.state, swap(self.state, "c", 1, then), lax.axis_index("c"), 1)


def swap_f(value, dist, then=()):
    count = lax.axis_size("y") * lax.axis_size("x")
    got = lax.ppermute(value, ("y", "x"), [(i, i ^ dist) for i in range(count)])
    return tie(got, then) if then else got


def in_order(parts):
    y, x = lax.axis_index("y"), lax.axis_index("x")
    row0 = [jnp.where(x == 0, parts[0], parts[1]), jnp.where(x == 0, parts[1], parts[0])]
    row1 = [jnp.where(x == 0, parts[2], parts[3]), jnp.where(x == 0, parts[3], parts[2])]
    top, low = jnp.stack(row0), jnp.stack(row1)
    return jnp.concatenate([jnp.where(y == 0, top, low), jnp.where(y == 0, low, top)])


def gather_f(value, *then):
    return in_order([value] + [swap_f(value, d, then) for d in (1, 2, 3)])


def sum_f(value):
    got = [value] + [swap_f(value, d) for d in (1, 2, 3)]
    return (got[0] + got[1]) + (got[2] + got[3])


def add(*terms):
    total = terms[0].astype(f32)
    for term in terms[1:]:
        total = total + term.astype(f32)
    return total.astype(bf16)


class RowReduce:
    def __init__(self):
        self.parts = []

    def after(self, *others):
        self.state = tie(self.state, others)

    def core(self, pair, *then):
        self.parts.append((pair[0], swap(pair[1], "c", 1, then)))

    def after_core(self, *others):
        self.parts = tie(self.parts, others)

    def chip_direct(self):
        count = lax.axis_size("y") * lax.axis_size("x")
        mine, got = (p.reshape((count, -1) + p.shape[-1:]) for p in self.parts[0])
        self.state = [add(mine[d], got[d]) for d in range(count)]

    def plane_direct(self, *then):
        got = [swap_f(self.state[d], d, then) for d in (1, 2, 3)]
        plane = add(self.state[0], *got)
        zsize = lax.axis_size("z")
        self.state = plane.reshape(zsize, plane.shape[0] // zsize, plane.shape[1])

    def chip(self):
        count = lax.axis_size("y") * lax.axis_size("x")

        def some(blocks, right):
            out = []
            for d in blocks:
                cuts = []
                for mine, got in self.parts:
                    half = (mine.shape[-1] // 256) * 128
                    cut = slice(half, None) if right else slice(None, half)
                    mine = mine.reshape((count, -1) + mine.shape[-1:])
                    got = got.reshape(mine.shape)
                    cuts.append(add(mine[d][:, cut], got[d][:, cut]))
                out.append(jnp.concatenate(cuts, axis=-1))
            return jnp.stack(out)

        self.state = some((0, 2), False), some((1, 3), False), some((0, 1), True), some((2, 3), True)

    def plane_first(self, *then):
        keep_left, send_left, keep_right, send_right = self.state
        got_left, got_right = swap(send_left, "x", 1, then), swap(send_right, "y", 1, then)
        self.state = (
            add(keep_left[0], got_left[0]), add(keep_left[1], got_left[1]),
            add(keep_right[0], got_right[0]), add(keep_right[1], got_right[1]),
        )

    def plane_second(self, *then):
        keep_left, send_left, keep_right, send_right = self.state
        got_left, got_right = swap(send_left, "y", 1, then), swap(send_right, "x", 1, then)
        plane = jnp.concatenate([add(keep_left, got_left), add(keep_right, got_right)], axis=-1)
        zsize = lax.axis_size("z")
        self.state = plane.reshape(zsize, plane.shape[0] // zsize, plane.shape[1])

    def near_z(self, *then):
        self._along_z(1, then)

    def far_z(self, *then):
        for bit in reversed(bits_down(lax.axis_size("z"))[:-1]):
            self._along_z(bit, then)

    def _along_z(self, bit, then=()):
        side = bit_of("z", bit)
        pairs = self.state.reshape((-1, 2) + self.state.shape[1:])
        other = swap(part(pairs, 1 - side, 1), "z", bit, then)
        self.state = add(part(pairs, side, 1), other)

    def back_far(self, *then):
        self.back = RepGather(self.state[0])
        self.back.far_z(*then)
        self.state = self.back.state

    def back_near(self, *then):
        self.back.state = self.state
        self.back.near_z(*then)
        self.state = self.back.state

    def back_core(self, *then):
        mine = self.state.reshape(-1, self.state.shape[-1])
        both = join(mine, swap(mine, "c", 1, then), lax.axis_index("c"), 0)
        self.state = both.reshape(-1, both.shape[-1])


def ungroup(reduced, sizes):
    halves = [(size // 256) * 128 for size in sizes]
    left, right, arrays = 0, sum(halves), []
    for size, half in zip(sizes, halves, strict=True):
        arrays.append(jnp.concatenate([reduced[:, left : left + half], reduced[:, right : right + size - half]], axis=-1))
        left, right = left + half, right + size - half
    return arrays


def product(left_op, right_op, einsum_form):
    return jnp.einsum(einsum_form, left_op, right_op, preferred_element_type=f32)


def normalize(summed_in, gain_row, bias_row):
    row_mean = jnp.mean(summed_in, axis=-1, keepdims=True)
    centered = summed_in - row_mean
    inv_dev = lax.rsqrt(jnp.mean(centered * centered, axis=-1, keepdims=True) + norm_eps)
    unit_rows = centered * inv_dev
    return (unit_rows * gain_row + bias_row, unit_rows, inv_dev)


def norm_back(upstream, unit_rows, inv_dev, gain_row):
    scaled = upstream * gain_row
    grad_in = inv_dev * (
        scaled
        - jnp.mean(scaled, axis=-1, keepdims=True)
        - unit_rows * jnp.mean(scaled * unit_rows, axis=-1, keepdims=True)
    )
    sums = tuple(range(upstream.ndim - 1))
    return (grad_in, jnp.sum(upstream * unit_rows, axis=sums), jnp.sum(upstream, axis=sums))


def gelu_pair(inner_pre):
    cumul = 0.5 * (1.0 + lax.erf(inner_pre * 0.7071067811865476))
    return (
        inner_pre * cumul,
        cumul + inner_pre * jnp.exp(-0.5 * inner_pre * inner_pre) * 0.3989422804014327,
    )


def masked_scores(query_rows, key_rows, key_mask):
    raw_scores = product(query_rows, key_rows, "gqhe,gkhe->ghqk") * (1.0 / math.sqrt(HEAD))
    return jnp.where(key_mask[:, None, None, :], raw_scores, masked_score)


def attend(query_rows, key_rows, value_rows, key_mask):
    scores = masked_scores(query_rows, key_rows, key_mask)
    row_max = jnp.max(scores, axis=-1, keepdims=True)
    log_total = row_max + jnp.log(jnp.sum(jnp.exp(scores - row_max), axis=-1, keepdims=True))
    softmax_w = jnp.exp(scores - log_total).astype(bf16)
    mixed_heads = product(softmax_w, value_rows, "ghqk,gkhe->gqhe").astype(bf16)
    return (mixed_heads, log_total)


def attend_back(query_rows, key_rows, value_rows, key_mask, log_total, grad_mixed):
    scores = masked_scores(query_rows, key_rows, key_mask)
    softmax_w = jnp.exp(scores - log_total)
    grad_value = product(softmax_w.astype(bf16), grad_mixed, "ghqk,gqhe->gkhe")
    grad_probs = product(grad_mixed, value_rows, "gqhe,gkhe->ghqk")
    grad_scores = (
        softmax_w * (grad_probs - jnp.sum(softmax_w * grad_probs, axis=-1, keepdims=True))
    ).astype(bf16)
    inv_root = 1.0 / math.sqrt(HEAD)
    grad_query = product(grad_scores, key_rows, "ghqk,gkhe->gqhe") * inv_root
    grad_key = product(grad_scores, query_rows, "ghqk,gqhe->gkhe") * inv_root
    return (grad_query, grad_key, grad_value)


def split_heads(packed, head_count):
    stacked = packed.reshape(packed.shape[0], packed.shape[1], 3, head_count, HEAD)
    return (stacked[:, :, 0], stacked[:, :, 1], stacked[:, :, 2])


def dot(a, b):
    return lax.dot_general(a, b, (((1,), (0,)), ((), ())), preferred_element_type=f32)


def dot_nt(a, b):
    return lax.dot_general(a, b, (((1,), (1,)), ((), ())), preferred_element_type=f32)


def dot_tn(a, b):
    return lax.dot_general(a, b, (((0,), (0,)), ((), ())), preferred_element_type=f32)


def norm_back_rows(upstream, unit_rows, inv_dev, gain_row):
    scaled = upstream * gain_row
    return inv_dev * (
        scaled
        - jnp.mean(scaled, axis=-1, keepdims=True)
        - unit_rows * jnp.mean(scaled * unit_rows, axis=-1, keepdims=True)
    )


def pair_of(value, low_half):
    zero = jnp.zeros_like(value)
    return jnp.concatenate([jnp.where(low_half, value, zero), jnp.where(low_half, zero, value)], axis=0)


def pair_probs(keys, queries_two, key_ok):
    scores = jnp.where(key_ok, dot_nt(keys, queries_two), masked_score)
    e = jnp.exp(scores - jnp.max(scores, axis=0, keepdims=True))
    return e * (1.0 / jnp.sum(e, axis=0, keepdims=True))


def cost(flops, moved):
    return pl.CostEstimate(flops=flops, bytes_accessed=moved, transcendentals=0)


def attend_kernel(counts_ref, x_ref, w_ref, packed_ref, mixed_ref, *, seg):
    step = pl.program_id(0)
    rows, width = x_ref.shape
    packed_ref[...] = dot(x_ref[...], w_ref[...]).astype(bf16)
    low_half = lax.broadcasted_iota(jnp.int32, (seg, 2 * HEAD), 1) < HEAD
    key_at = lax.broadcasted_iota(jnp.int32, (seg, 2 * seg), 0)
    for s in range(rows // seg):
        key_ok = key_at < counts_ref[step * (rows // seg) + s]
        r = pl.ds(s * seg, seg)
        for p in range(width // (2 * HEAD)):
            col = p * 2 * HEAD
            q = packed_ref[r, pl.ds(col, 2 * HEAD)] * jnp.asarray(HEAD**-0.5, bf16)
            k = packed_ref[r, pl.ds(width + col, 2 * HEAD)]
            v = packed_ref[r, pl.ds(2 * width + col, 2 * HEAD)]
            probs = pair_probs(k, pair_of(q, low_half), key_ok).astype(bf16)
            both = dot_tn(probs, v)
            mixed_ref[r, pl.ds(col, 2 * HEAD)] = jnp.where(low_half, both[:seg], both[seg:]).astype(bf16)


def attend_call(counts, x, w_qkv, rows=256):
    total, width = x.shape
    return pl.pallas_call(
        functools.partial(attend_kernel, seg=total // counts.shape[0]),
        grid_spec=pltpu.PrefetchScalarGridSpec(
            num_scalar_prefetch=1,
            grid=(total // rows,),
            in_specs=[
                pl.BlockSpec((rows, width), lambda i, n: (i, 0)),
                pl.BlockSpec((width, 3 * width), lambda i, n: (0, 0)),
            ],
            out_specs=[
                pl.BlockSpec((rows, 3 * width), lambda i, n: (i, 0)),
                pl.BlockSpec((rows, width), lambda i, n: (i, 0)),
            ],
        ),
        out_shape=[
            jax.ShapeDtypeStruct((total, 3 * width), bf16),
            jax.ShapeDtypeStruct((total, width), bf16),
        ],
        compiler_params=pltpu.CompilerParams(vmem_limit_bytes=VMEM_CAP),
        cost_estimate=cost(8 * total * width * width, 16 << 20),
        name="attend",
    )(counts, x, w_qkv)


def attend_back_kernel(counts_ref, packed_ref, grad_ref, out_ref, *, seg):
    step = pl.program_id(0)
    rows, width = grad_ref.shape
    low_half = lax.broadcasted_iota(jnp.int32, (seg, 2 * HEAD), 1) < HEAD
    key_at = lax.broadcasted_iota(jnp.int32, (seg, 2 * seg), 0)
    root = jnp.asarray(HEAD**-0.5, bf16)
    for s in range(rows // seg):
        key_ok = key_at < counts_ref[step * (rows // seg) + s]
        r = pl.ds(s * seg, seg)
        for p in range(width // (2 * HEAD)):
            col = p * 2 * HEAD
            q_two = pair_of(packed_ref[r, pl.ds(col, 2 * HEAD)] * root, low_half)
            k = packed_ref[r, pl.ds(width + col, 2 * HEAD)]
            v = packed_ref[r, pl.ds(2 * width + col, 2 * HEAD)]
            g_two = pair_of(grad_ref[r, pl.ds(col, 2 * HEAD)], low_half)
            probs = pair_probs(k, q_two, key_ok)
            grad_v = dot(probs.astype(bf16), g_two)
            grad_p = dot_nt(v, g_two)
            weighted = probs * grad_p
            grad_s = (weighted - probs * jnp.sum(weighted, axis=0, keepdims=True)).astype(bf16)
            grad_k = dot(grad_s, q_two)
            both = dot_tn(grad_s, k) * (HEAD**-0.5)
            out_ref[r, pl.ds(col, 2 * HEAD)] = jnp.where(low_half, both[:seg], both[seg:]).astype(bf16)
            out_ref[r, pl.ds(width + col, 2 * HEAD)] = grad_k.astype(bf16)
            out_ref[r, pl.ds(2 * width + col, 2 * HEAD)] = grad_v.astype(bf16)


def attend_back_call(counts, packed, grad_mixed, rows=256):
    total, width = grad_mixed.shape
    return pl.pallas_call(
        functools.partial(attend_back_kernel, seg=total // counts.shape[0]),
        grid_spec=pltpu.PrefetchScalarGridSpec(
            num_scalar_prefetch=1,
            grid=(total // rows,),
            in_specs=[
                pl.BlockSpec((rows, 3 * width), lambda i, n: (i, 0)),
                pl.BlockSpec((rows, width), lambda i, n: (i, 0)),
            ],
            out_specs=pl.BlockSpec((rows, 3 * width), lambda i, n: (i, 0)),
        ),
        out_shape=jax.ShapeDtypeStruct((total, 3 * width), bf16),
        compiler_params=pltpu.CompilerParams(vmem_limit_bytes=VMEM_CAP),
        cost_estimate=cost(16 * total * width * width, 16 << 20),
        name="attend_back",
    )(counts, packed, grad_mixed)


def whole(shape):
    return pl.BlockSpec(shape, lambda *i: (0,) * len(shape))


def rows_of(rows, cols):
    return pl.BlockSpec((rows, cols), lambda i, *n: (i, 0))


def finish_kernel(counts_ref, x_ref, mixed_ref, out_ref, up_ref, down_ref, rows_ref,
                  z1_ref, z2_ref, act_ref, slope_ref, hidden_ref, cls_ref, *, tile, seg):
    step = pl.program_id(0)
    rows, width = x_ref.shape
    z1 = x_ref[...].astype(f32) + dot(mixed_ref[...], out_ref[...])
    z1_ref[...] = z1
    first, _, _ = normalize(z1, rows_ref[0:1], rows_ref[2:3])
    low = first.astype(bf16)
    total = first
    for t in range(up_ref.shape[1] // tile):
        cols = pl.ds(t * tile, tile)
        act, slope = gelu_pair(dot(low, up_ref[:, cols]))
        act = act.astype(bf16)
        act_ref[:, cols] = act
        slope_ref[:, cols] = slope.astype(bf16)
        total = total + dot(act, down_ref[cols, :])
    z2_ref[...] = total
    normed = normalize(total, rows_ref[1:2], rows_ref[3:4])[0]
    at = lax.broadcasted_iota(jnp.int32, (seg, width), 0)
    for s in range(rows // seg):
        here = step * (rows // seg) + s
        block = normed[s * seg : (s + 1) * seg]
        cls_ref[pl.ds(here, 1), :] = block[0:1]
        hidden_ref[s * seg : (s + 1) * seg] = jnp.where(at < counts_ref[here], block, 0.0).astype(bf16)


def pack_kernel(wide_ref, *refs):
    small, o_ref = refs[:-1], refs[-1]
    cols = wide_ref.shape[1]
    o_ref[:, :cols] = wide_ref[...]
    turned, at = 0.0, 0
    for ref in small:
        count = ref.shape[0]
        shape = (count, 128)
        one = lax.broadcasted_iota(jnp.int32, shape, 1) == lax.broadcasted_iota(jnp.int32, shape, 0) + at
        turned = turned + dot_tn(ref[...], one.astype(bf16))
        at += count
    o_ref[:, cols:] = turned.astype(bf16)


def pack_call(wide, small):
    return pl.pallas_call(
        pack_kernel,
        out_shape=jax.ShapeDtypeStruct((wide.shape[0], wide.shape[1] + 128), bf16),
        name="pack",
    )(wide, *small)


def turn_kernel(w_ref, o_ref):
    o_ref[...] = w_ref[...].astype(f32).T


def turn_call(w, at):
    return pl.pallas_call(
        turn_kernel,
        grid=(1,),
        in_specs=[pl.BlockSpec((w.shape[0], 128), lambda i: (0, at))],
        out_specs=whole((128, w.shape[0])),
        out_shape=jax.ShapeDtypeStruct((128, w.shape[0]), f32),
        name="turn",
    )(w)


def up_out_specs(width, ff):
    return [
        pl.BlockSpec((width, width), lambda i, *n: (0, 3)),
        pl.BlockSpec((width, ff), lambda i, *n: (0, 0)),
    ]


def finish_call(counts, x, mixed, w_first, w_up, w_down, small, rows=256, tile=768):
    total, width = x.shape
    ff = w_down.shape[0]
    groups = counts.shape[0]
    narrow, wide = rows_of(rows, width), rows_of(rows, ff)
    return pl.pallas_call(
        functools.partial(finish_kernel, tile=tile, seg=total // groups),
        grid_spec=pltpu.PrefetchScalarGridSpec(
            num_scalar_prefetch=1,
            grid=(total // rows,),
            in_specs=[
                narrow, narrow,
                *up_out_specs(width, ff), whole(w_down.shape),
                whole(small.shape),
            ],
            out_specs=[narrow, narrow, wide, wide, narrow, whole((groups, width))],
        ),
        out_shape=[
            jax.ShapeDtypeStruct((total, width), f32),
            jax.ShapeDtypeStruct((total, width), f32),
            jax.ShapeDtypeStruct((total, ff), bf16),
            jax.ShapeDtypeStruct((total, ff), bf16),
            jax.ShapeDtypeStruct((total, width), bf16),
            jax.ShapeDtypeStruct((groups, width), f32),
        ],
        compiler_params=pltpu.CompilerParams(vmem_limit_bytes=VMEM_CAP),
        cost_estimate=cost(2 * total * width * (width + 2 * ff), 40 << 20),
        name="finish",
    )(counts, x, mixed, w_first, w_up, w_down, small)


def finish_back_kernel(counts_ref, cot_ref, cls_ref, z1_ref, z2_ref, slope_ref, out_ref, up_ref, down_ref,
                       rows_ref,
                       outer_ref, inner_ref, resid_ref, attended_ref, mixed_ref, low_ref, sums_ref, *, tile, seg):
    step = pl.program_id(0)
    rows, width = cot_ref.shape

    @pl.when(step == 0)
    def _():
        sums_ref[...] = jnp.zeros_like(sums_ref)

    at = lax.broadcasted_iota(jnp.int32, (seg, width), 0)
    parts = []
    for s in range(rows // seg):
        here = step * (rows // seg) + s
        block = cot_ref[s * seg : (s + 1) * seg].astype(f32)
        block = jnp.where(at == 0, cls_ref[pl.ds(here, 1), :], block)
        parts.append(jnp.where(at < counts_ref[here], block, 0.0))
    g = jnp.concatenate(parts, axis=0)
    _, unit_two, inv_two = normalize(z2_ref[...], rows_ref[1:2], rows_ref[3:4])
    grad_two = norm_back_rows(g, unit_two, inv_two, rows_ref[1:2])
    outer = grad_two.astype(bf16)
    outer_ref[...] = outer
    sums_ref[1:2] += jnp.sum(g * unit_two, axis=0, keepdims=True)
    sums_ref[3:4] += jnp.sum(g, axis=0, keepdims=True)
    first_grad = grad_two
    for t in range(up_ref.shape[1] // tile):
        cols = pl.ds(t * tile, tile)
        inner = (dot_nt(outer, down_ref[cols, :]) * slope_ref[:, cols].astype(f32)).astype(bf16)
        inner_ref[:, cols] = inner
        first_grad = first_grad + dot_nt(inner, up_ref[:, cols])
    first, unit_one, inv_one = normalize(z1_ref[...], rows_ref[0:1], rows_ref[2:3])
    low_ref[...] = first.astype(bf16)
    grad_one = norm_back_rows(first_grad, unit_one, inv_one, rows_ref[0:1])
    resid_ref[...] = grad_one
    sums_ref[0:1] += jnp.sum(first_grad * unit_one, axis=0, keepdims=True)
    sums_ref[2:3] += jnp.sum(first_grad, axis=0, keepdims=True)
    attended = grad_one.astype(bf16)
    attended_ref[...] = attended
    mixed_ref[...] = dot_nt(attended, out_ref[...]).astype(bf16)


def finish_back_call(counts, cot, cls_grad, z1, z2, slope, w_first, w_up, w_down, small, rows=256, tile=768):
    total, width = cot.shape
    ff = w_down.shape[0]
    groups = counts.shape[0]
    narrow, wide = rows_of(rows, width), rows_of(rows, ff)
    return pl.pallas_call(
        functools.partial(finish_back_kernel, tile=tile, seg=total // groups),
        grid_spec=pltpu.PrefetchScalarGridSpec(
            num_scalar_prefetch=1,
            grid=(total // rows,),
            in_specs=[
                narrow, whole((groups, width)), narrow, narrow, wide,
                *up_out_specs(width, ff), whole(w_down.shape),
                whole(small.shape),
            ],
            out_specs=[narrow, wide, narrow, narrow, narrow, narrow, whole((16, width))],
        ),
        out_shape=[
            jax.ShapeDtypeStruct((total, width), bf16),
            jax.ShapeDtypeStruct((total, ff), bf16),
            jax.ShapeDtypeStruct((total, width), f32),
            jax.ShapeDtypeStruct((total, width), bf16),
            jax.ShapeDtypeStruct((total, width), bf16),
            jax.ShapeDtypeStruct((total, width), bf16),
            jax.ShapeDtypeStruct((16, width), f32),
        ],
        compiler_params=pltpu.CompilerParams(vmem_limit_bytes=VMEM_CAP),
        cost_estimate=cost(2 * total * width * (width + 2 * ff), 40 << 20),
        name="finish_back",
    )(counts, cot, cls_grad, z1, z2, slope, w_first, w_up, w_down, small)


def row_blocks_kernel(ids_ref, a_ref, b_ref, *refs, count):
    extra, (mine_ref, send_ref, turned_ref) = refs[:-3], refs[-3:]
    c, f = ids_ref[0], ids_ref[1]
    half = turned_ref.shape[0] // 2
    unit = half // count

    def place(ref, value):
        for block in range(count):
            for h in range(2):
                to = pl.multiple_of((h ^ c) * half + (block ^ f) * unit, 16)
                ref[pl.ds(to, unit), :] = value[(block * 2 + h) * unit : (block * 2 + h + 1) * unit]

    @pl.when(pl.program_id(0) == 0)
    def _():
        place(turned_ref, a_ref[...].T)

    tile = b_ref.shape[1]
    result = dot(turned_ref[...], b_ref[...]).astype(bf16)
    mine_ref[:, :tile] = result[:half]
    send_ref[:, :tile] = result[half:]
    if extra:
        sums_ref, = extra
        low = sums_ref[...].astype(bf16)
        lanes = lax.broadcasted_iota(jnp.int32, (low.shape[0], 128), 1)
        eye = (lax.broadcasted_iota(jnp.int32, (low.shape[0], 128), 0) == lanes).astype(bf16)
        turned = dot_tn(low, eye).astype(bf16)
        for block in range(count):
            for h in range(2):
                value = turned[(block * 2 + h) * unit : (block * 2 + h + 1) * unit]
                to = pl.multiple_of((block ^ f) * unit, 16)

                @pl.when(h == c)
                def _():
                    mine_ref[pl.ds(to, unit), tile:] = value

                @pl.when(h != c)
                def _():
                    send_ref[pl.ds(to, unit), tile:] = value


def row_blocks_call(ids, a, b, count, sums=None, tile=768):
    total, width = a.shape
    cols = b.shape[1]
    full = cols if sums is None else cols + 128
    step = tile if sums is None else full
    out = pl.BlockSpec((width // 2, step), lambda i, n: (0, i))
    more = [] if sums is None else [sums]
    return pl.pallas_call(
        functools.partial(row_blocks_kernel, count=count),
        grid_spec=pltpu.PrefetchScalarGridSpec(
            num_scalar_prefetch=1,
            grid=(cols // tile,),
            in_specs=[whole(a.shape), pl.BlockSpec((total, tile), lambda i, n: (0, i))] + [whole(m.shape) for m in more],
            out_specs=[out, out],
            scratch_shapes=[pltpu.VMEM((width, total), bf16)],
        ),
        out_shape=[jax.ShapeDtypeStruct((width // 2, full), bf16)] * 2,
        compiler_params=pltpu.CompilerParams(vmem_limit_bytes=VMEM_CAP),
        cost_estimate=cost(2 * total * width * cols * 2, 16 << 20),
        name="row_blocks",
    )(ids, a, b, *more)


def wide_blocks_kernel(ids_ref, a_ref, b_ref, mine_ref, send_ref):
    c = ids_ref[0]
    half = b_ref.shape[1] // 2

    def rows_at(h):
        at = pl.multiple_of(h * half, 128)
        return dot_tn(b_ref[:, pl.ds(at, half)], a_ref[...]).astype(bf16)

    mine_ref[0] = rows_at(c)
    send_ref[0] = rows_at(1 - c)


def wide_blocks_call(ids, a, b, count):
    total, width = a.shape
    block = b.shape[1] // count
    out = pl.BlockSpec((1, block // 2, width), lambda i, n: (i ^ n[1], 0, 0))
    return pl.pallas_call(
        wide_blocks_kernel,
        grid_spec=pltpu.PrefetchScalarGridSpec(
            num_scalar_prefetch=1,
            grid=(count,),
            in_specs=[whole(a.shape), pl.BlockSpec((total, block), lambda i, n: (0, i))],
            out_specs=[out, out],
        ),
        out_shape=[jax.ShapeDtypeStruct((count, block // 2, width), bf16)] * 2,
        compiler_params=pltpu.CompilerParams(vmem_limit_bytes=VMEM_CAP),
        cost_estimate=cost(2 * total * width * b.shape[1] * 2, 16 << 20),
        name="wide_blocks",
    )(ids, a, b)


def token_grad_kernel(resid_ref, g_ref, w_ref, o_ref):
    o_ref[...] = (resid_ref[...] + dot_nt(g_ref[...], w_ref[...])).astype(bf16)


def token_grad_call(resid, g, w_qkv, rows=256):
    total, width = resid.shape
    return pl.pallas_call(
        token_grad_kernel,
        grid=(total // rows,),
        in_specs=[rows_of(rows, width), rows_of(rows, 3 * width), whole((width, 3 * width))],
        out_specs=rows_of(rows, width),
        out_shape=jax.ShapeDtypeStruct((total, width), bf16),
        compiler_params=pltpu.CompilerParams(vmem_limit_bytes=VMEM_CAP),
        cost_estimate=cost(12 * total * width * width, 16 << 20),
        name="token_grad",
    )(resid, g, w_qkv)


def cross_message(cse_qkv, cse_out, cse_up, cse_down, fsize, f):
    rows, width = cse_qkv.shape[0], cse_out.shape[1]
    ff = cse_up.shape[1]
    slim = width // fsize
    cols = jnp.concatenate(
        [
            cse_qkv.reshape(rows, 3, fsize, slim).transpose(2, 0, 1, 3).reshape(fsize, rows, 3 * slim),
            cse_up.reshape(rows, fsize, ff // fsize).transpose(1, 0, 2),
        ],
        axis=-1,
    )
    mine = in_order([part(cols, f, 0)] + [swap_f(part(cols, f ^ d, 0), d) for d in (1, 2, 3)])
    flat = mine.reshape(fsize * rows, -1)
    frows = cse_down.shape[0]
    out_flat = jnp.concatenate([cse_out[:, k * slim : (k + 1) * slim] for k in range(fsize)], axis=0)
    return jnp.concatenate([flat, cse_down, out_flat], axis=-1)


def unpack_kernel(m_ref, qkv_ref, out_ref, up_ref, down_ref, *, fsize):
    reps, frows, _ = m_ref.shape
    rows = frows // fsize
    width, a = qkv_ref.shape
    b, slim = a + up_ref.shape[1], width // fsize
    for r in range(reps):
        for k in range(fsize):
            at, here = k * reps * rows + r * rows, slice(k * rows, (k + 1) * rows)
            qkv_ref[at : at + rows, :] = m_ref[r, here, :a]
            up_ref[at : at + rows, :] = m_ref[r, here, a:b]
        down_ref[r * frows : (r + 1) * frows, :] = m_ref[r, :, b : b + width]
        out = [m_ref[r, k * rows : (k + 1) * rows, b + width :] for k in range(fsize)]
        out_ref[r * rows : (r + 1) * rows, :] = jnp.concatenate(out, axis=-1)


def cross_unpack(gathered, width, ff, fsize):
    reps, frows = gathered.shape[:2]
    slim = width // fsize
    if frows // fsize % 8:
        return cross_unpack_small(gathered, width, ff, fsize)
    shapes = [(width, 3 * slim), (slim, width), (width, ff // fsize), (ff // fsize, width)]
    return pl.pallas_call(
        functools.partial(unpack_kernel, fsize=fsize),
        out_shape=[jax.ShapeDtypeStruct(shape, bf16) for shape in shapes],
        compiler_params=pltpu.CompilerParams(vmem_limit_bytes=VMEM_CAP),
        name="unpack",
    )(gathered)


def cross_unpack_small(gathered, width, ff, fsize):
    slim = width // fsize
    reps, frows = gathered.shape[:2]
    rows = frows // fsize
    a, b = 3 * slim, 3 * slim + ff // fsize
    by_row = gathered[:, :, :b].reshape(reps, fsize, rows, b).transpose(1, 0, 2, 3).reshape(-1, b)
    qkv = by_row[:, :a]
    up = by_row[:, a:]
    down = gathered[:, :, b : b + width].reshape(-1, width)
    out = gathered[:, :, b + width :].reshape(reps, fsize, rows, slim).transpose(0, 2, 1, 3).reshape(-1, width)
    return qkv, out, up, down


def cross_block(cls_in, cotan, weights, gains, biases, fsize, f):
    qkv, out, up, down = weights
    segs, width = cls_in.shape
    slim = width // fsize
    heads = slim // HEAD
    packed = product(cls_in[None], qkv, "gsd,de->gse").astype(bf16)
    queries, keys, values = split_heads(packed, heads)
    every = jnp.ones((1, segs), jnp.bool_)
    mixed, log_total = attend(queries, keys, values, every)
    mixed = mixed.reshape(segs, slim)
    attended = sum_f(product(mixed, out, "sd,de->se"))
    first, unit_one, inv_one = normalize(cls_in.astype(f32) + attended, gains[0], biases[0])
    first_low = first.astype(bf16)
    activated, slope = gelu_pair(product(first_low, up, "sd,df->sf"))
    act_low = activated.astype(bf16)
    outer = sum_f(product(act_low, down, "sf,fd->sd"))
    cls_out, unit_two, inv_two = normalize(first + outer, gains[1], biases[1])

    grad_two, gain_two, bias_two = norm_back(cotan, unit_two, inv_two, gains[1])
    grad_outer = grad_two.astype(bf16)
    grad_inner = (product(grad_outer, down, "sd,fd->sf") * slope).astype(bf16)
    grad_first = grad_two + sum_f(product(grad_inner, up, "sf,df->sd"))
    grad_one, gain_one, bias_one = norm_back(grad_first, unit_one, inv_one, gains[0])
    grad_attended = grad_one.astype(bf16)
    grad_mixed = product(grad_attended, out, "se,de->sd").astype(bf16)
    grad_q, grad_k, grad_v = attend_back(
        queries, keys, values, every, log_total, grad_mixed.reshape(1, segs, heads, HEAD)
    )
    grad_packed = jnp.concatenate(
        [grad_q.reshape(segs, slim), grad_k.reshape(segs, slim), grad_v.reshape(segs, slim)], axis=-1
    ).astype(bf16)
    grad_in = grad_one + sum_f(product(grad_packed, qkv, "se,de->sd"))

    def own(value):
        return lax.dynamic_slice_in_dim(value, f * slim, slim, value.ndim - 1)

    sums = jnp.stack([gain_one, gain_two, bias_one, bias_two])
    pieces = {
        "packed": grad_packed,
        "inner": grad_inner,
        "act": act_low,
        "outer": grad_outer,
        "attended": grad_attended,
        "mixed": mixed,
        "own_in": own(cls_in),
        "own_low": own(first_low),
        "own_grad": own(grad_in).astype(bf16),
        "sums": jnp.pad(own(sums), ((0, segs - 4), (0, 0))).astype(bf16),
    }
    return cls_out, grad_in, pieces


def doc_message(spread, pieces, fsize, width):
    segs = spread.shape[1]
    slim = width // fsize
    qkv_cols = spread[:, :, : 3 * slim].reshape(fsize, segs, 3, slim).transpose(1, 2, 0, 3)
    parts = {"packed": qkv_cols.reshape(segs, 3 * width), "inner": spread[:, :, 3 * slim :].transpose(1, 0, 2).reshape(segs, -1)}
    parts = {**pieces, **parts}
    ends, at = {}, 0
    for name, value in parts.items():
        ends[name] = (at, at + value.shape[1])
        at += value.shape[1] + -value.shape[1] % 128
    parts = {k: jnp.pad(v, ((0, 0), (0, -v.shape[1] % 128))) for k, v in parts.items()}
    return jnp.concatenate(list(parts.values()), axis=-1), ends


def cross_grads(docs, ends):
    flat = docs.reshape(-1, docs.shape[-1])
    cut = {name: flat[:, a:b] for name, (a, b) in ends.items()}
    g_qkv = product(cut["own_in"], cut["packed"], "rd,re->de")
    g_out = product(cut["mixed"], cut["attended"], "rd,re->de")
    g_up = product(cut["own_low"], cut["inner"], "rd,re->de")
    g_down = product(cut["act"], cut["outer"], "rd,re->de")
    part_of = {name: docs[:, :, ends[name][0] : ends[name][1]].astype(f32) for name in ("own_grad", "sums")}
    g_pos = jnp.sum(part_of["own_grad"], axis=0)
    g_sums = jnp.sum(part_of["sums"][:, :4], axis=0)
    return g_qkv, g_out, g_up, g_down, g_sums[0:2], g_sums[2:4], g_pos


def per_device(
    tokens, counts, cotangent,
    swe_qkv, swe_out, swe_up, swe_down, swe_gains, swe_biases,
    cse_qkv, cse_out, cse_up, cse_down, cse_gains, cse_biases, positions,
):
    docs_here, local_len, width = tokens.shape
    ff = swe_up.shape[1]
    seg_here = counts.shape[1]
    groups = docs_here * seg_here
    fsize = lax.axis_size("y") * lax.axis_size("x")
    f = lax.axis_index("y") * lax.axis_size("x") + lax.axis_index("x")
    c = lax.axis_index("c")
    ids = jnp.stack([c, f])
    segs = fsize * seg_here
    x = tokens.reshape(-1, width)
    cot = cotangent.reshape(-1, width)
    lens = counts.reshape(groups)

    small = [swe_gains, swe_biases, cse_gains, cse_biases, positions]
    count_small = sum(v.shape[0] for v in small)
    packed_up = pack_call(swe_up, small)
    w_up = lax.all_gather(packed_up, ("y", "x", "z", "c"), axis=0, tiled=True)
    first = RowGather(tie(jnp.concatenate([swe_qkv, swe_out], axis=-1), packed_up))
    first.far_z()
    down = RowGather(tie(swe_down, first.state))
    first.near_z()
    first.after(down.state)
    down.after(first.state)
    turned = first.state
    first.plane_first()
    down.far_z()
    message = cross_message(*tie((cse_qkv, cse_out, cse_up, cse_down), turned), fsize, f)
    down.after(first.state)
    first.after(down.state, message)
    first.plane_second()
    down.near_z()
    first.after(down.state)
    down.after(first.state)
    first.sibling()
    w_first = side_by_side(*first.state, c)
    down.plane_first(w_first)
    packed, mixed = attend_call(lens, x, tie(w_first, down.state))
    down.plane_second(packed)
    w_up = tie(w_up, packed, down.state)
    down.after(w_up)
    cross = lax.all_gather(tie(message, w_up), ("z", "c"), axis=0)
    down.sibling()
    w_down = side_by_side(*down.state, c)
    rows = turn_call(w_up, ff // 128)
    gains, biases, cross_gains, cross_biases, pos = (
        rows[0:2], rows[2:4], rows[4:6], rows[6:8], rows[8:count_small]
    )
    z1, z2, act, slope, hidden, cls_rows = finish_call(lens, x, mixed, w_first, w_up, w_down, rows)
    cross_w = cross_unpack(cross, width, ff, fsize)

    pos_here = lax.dynamic_slice_in_dim(pos, f * seg_here, seg_here, 0)
    cls_here = (cls_rows + pos_here).astype(bf16)
    cls_cot = cot.reshape(groups, -1, width)[:, 0]
    both = gather_f(jnp.concatenate([cls_here, cls_cot], axis=-1), cross_w).reshape(segs, 2 * width)
    cls_out, cls_grad, pieces = cross_block(
        both[:, :width], both[:, width:].astype(f32), cross_w, cross_gains, cross_biases, fsize, f,
    )
    cls_out = lax.dynamic_slice_in_dim(cls_out, f * seg_here, seg_here, 0)
    cls_here_grad = lax.dynamic_slice_in_dim(cls_grad, f * seg_here, seg_here, 0)

    spread = tie(jnp.concatenate([pieces["packed"], pieces["inner"]], axis=-1), cls_grad)
    outer, inner, resid, attended, grad_mixed, low, sums = finish_back_call(
        lens, cot, tie(cls_here_grad, spread), z1, z2, slope, w_first, w_up, w_down, rows
    )
    spread = gather_f(spread, outer)
    layer_out = hidden.reshape(groups, -1, width).at[:, 0].set(tie(cls_out.astype(bf16), outer))
    message, ends = doc_message(tie(spread, outer), pieces, fsize, width)
    docs = lax.all_gather(message, ("z", "c"), axis=0)
    red_down, red_up, red_qkv = RowReduce(), RowReduce(), RowReduce()
    g_down = wide_blocks_call(ids, tie(outer, message), act, fsize)
    g_out = row_blocks_call(ids, tie(mixed, g_down), attended, fsize, sums)
    red_down.core(g_down, g_out)
    red_down.chip()
    g_up = row_blocks_call(ids, tie(low, red_down.state), inner, fsize)
    red_down.plane_first(g_up)
    red_up.core(g_out, g_up)
    red_up.core(tie(g_up, red_down.state))
    red_up.chip()
    red_down.after(red_up.state)
    grad_packed = attend_back_call(lens, packed, tie(grad_mixed, red_up.state, red_down.state))
    red_down.plane_second(grad_packed)
    red_up.plane_first(grad_packed)
    red_down.after(grad_packed, red_up.state)
    red_up.after(red_down.state)
    g_qkv = row_blocks_call(ids, x, tie(grad_packed, red_up.state, red_down.state), fsize)
    red_up.plane_second(g_qkv)
    red_down.near_z(g_qkv)
    red_qkv.core(tie(g_qkv, red_up.state, red_down.state))
    red_qkv.chip_direct()
    red_down.far_z(red_qkv.state)
    red_up.near_z(red_qkv.state)
    red_up.after(red_qkv.state, red_down.state)
    red_down.after(red_up.state)
    token_grad = token_grad_call(tie(resid, red_qkv.state, red_down.state, red_up.state), grad_packed, w_first)
    red_down.back_far(token_grad)
    red_up.far_z(token_grad)
    others = cross_grads(tie(docs, token_grad), ends)
    red_qkv.plane_direct(token_grad)
    red_down.back_near()
    red_up.back_far()

    def step(*moves):
        states = lax.optimization_barrier([r.state for r in (red_qkv, red_up, red_down)])
        for r, state in zip((red_qkv, red_up, red_down), states, strict=True):
            r.state = state
        for move in moves:
            move()

    red_qkv.near_z()
    step(red_qkv.far_z, red_up.back_near, red_down.back_core)
    red_qkv.back_far()
    step(red_qkv.back_near, red_up.back_core)
    done_out, done_up = ungroup(red_up.state.astype(f32), (width + 128, ff))
    done_down = red_down.state.astype(f32)
    red_qkv.back_core(layer_out, done_out, done_up, done_down)
    done_qkv = red_qkv.state.astype(f32)
    small_grads = done_out[:, width : width + 4].T
    return (
        layer_out.reshape(tokens.shape),
        token_grad.reshape(tokens.shape),
        done_qkv,
        done_out[:, :width],
        done_up,
        done_down,
        small_grads[0:2],
        small_grads[2:4],
    ) + others


def solution(mesh):
    fsize, rsize = mesh.shape["fsdp"], mesh.shape["rep"]
    fine = Mesh(mesh.devices.reshape(2, fsize // 2, rsize // 2, 2), ("y", "x", "z", "c"))
    fs, rep = ("y", "x"), ("z", "c")
    every = fs + rep
    by_rows, by_cols = P(every, None), P(None, every)
    block = (by_rows,) * 4 + (by_cols,) * 2
    grads = (P(fs, None),) * 4 + (P(None, fs),) * 2
    return jax.shard_map(
        per_device,
        mesh=fine,
        in_specs=(P(rep, fs, None), P(rep, fs), P(rep, fs, None)) + block + block + (by_cols,),
        out_specs=(P(rep, fs, None),) * 2 + grads + grads + (P(None, fs),),
        check_vma=False,
    )
```

```python
import functools
import math

import jax
import jax.numpy as jnp
from jax import lax
from jax.experimental import pallas as pl
from jax.experimental.pallas import tpu as pltpu
from jax.sharding import Mesh
from jax.sharding import PartitionSpec as P

HEAD = 64
norm_eps = 1e-05
masked_score = -1000000000.0
bf16, f32 = jnp.bfloat16, jnp.float32
VMEM_CAP = 56 << 20


def tie(values, *after):
    return lax.optimization_barrier((values, after))[0]


def swap(value, axis, bit, then=()):
    size = lax.axis_size(axis)
    got = lax.ppermute(value, axis, [(i, i ^ bit) for i in range(size)])
    return tie(got, then) if then else got


def bit_of(axis, bit):
    return (lax.axis_index(axis) // bit) % 2


def join(mine, other, side, axis):
    first = side == 0
    return jnp.stack([jnp.where(first, mine, other), jnp.where(first, other, mine)], axis=axis)


def side_by_side(mine, other, side):
    both = jnp.concatenate([other, other], axis=-1)
    return lax.dynamic_update_slice_in_dim(both, mine, side * mine.shape[-1], axis=-1)


def part(value, side, axis):
    return lax.dynamic_index_in_dim(value, side, axis, keepdims=False)


def bits_down(size):
    return [1 << k for k in reversed(range(size.bit_length() - 1))]


class RowGather:
    def __init__(self, shard):
        rows, cols = shard.shape
        half = cols // 2
        c = lax.axis_index("c")
        keep = lax.dynamic_slice_in_dim(shard, c * half, half, 1)
        send = lax.dynamic_slice_in_dim(shard, (1 - c) * half, half, 1)
        self.state = join(keep, swap(send, "c", 1), c, 0).reshape(1, 2 * rows, half)

    def after(self, *others):
        self.state = tie(self.state, others)

    def far_z(self, *then):
        bits = bits_down(lax.axis_size("z"))
        for bit in bits[:-1]:
            self._along_z(bit, then)

    def near_z(self, *then):
        self._along_z(1, then)

    def _along_z(self, bit, then=()):
        got = self.state
        got = join(got, swap(got, "z", bit, then), bit_of("z", bit), 1)
        self.state = got.reshape((-1,) + got.shape[2:])

    def plane_first(self, *then):
        zhalf = self.state.shape[0] // 2
        one, two = self.state[:zhalf], self.state[zhalf:]
        got_one, got_two = swap(one, "x", 1, then), swap(two, "y", 1, then)
        self.state = join(one, got_one, lax.axis_index("x"), 0), join(two, got_two, lax.axis_index("y"), 0)

    def plane_second(self, *then):
        one, two = self.state
        got_one, got_two = swap(one, "y", 1, then), swap(two, "x", 1, then)
        one = join(one, got_one, lax.axis_index("y"), 0)
        two = join(two, got_two, lax.axis_index("x"), 1)
        both = jnp.concatenate([one, two], axis=2)
        self.state = both.reshape(-1, both.shape[-1])

    def sibling(self, *then):
        self.state = self.state, swap(self.state, "c", 1, then)


class RepGather:
    def __init__(self, message):
        self.state = message[None]

    far_z = RowGather.far_z
    near_z = RowGather.near_z
    after = RowGather.after

    def _along_z(self, bit, then=()):
        got = self.state
        got = join(got, swap(got, "z", bit, then), bit_of("z", bit), 1)
        self.state = got.reshape((-1,) + got.shape[2:])

    def sibling(self, *then):
        self.state = join(self.state, swap(self.state, "c", 1, then), lax.axis_index("c"), 1)


def swap_f(value, dist, then=()):
    count = lax.axis_size("y") * lax.axis_size("x")
    got = lax.ppermute(value, ("y", "x"), [(i, i ^ dist) for i in range(count)])
    return tie(got, then) if then else got


def in_order(parts):
    y, x = lax.axis_index("y"), lax.axis_index("x")
    row0 = [jnp.where(x == 0, parts[0], parts[1]), jnp.where(x == 0, parts[1], parts[0])]
    row1 = [jnp.where(x == 0, parts[2], parts[3]), jnp.where(x == 0, parts[3], parts[2])]
    top, low = jnp.stack(row0), jnp.stack(row1)
    return jnp.concatenate([jnp.where(y == 0, top, low), jnp.where(y == 0, low, top)])


def gather_f(value, *then):
    return in_order([value] + [swap_f(value, d, then) for d in (1, 2, 3)])


def sum_f(value):
    got = [value] + [swap_f(value, d) for d in (1, 2, 3)]
    return (got[0] + got[1]) + (got[2] + got[3])


def add(*terms):
    total = terms[0].astype(f32)
    for term in terms[1:]:
        total = total + term.astype(f32)
    return total.astype(bf16)


class RowReduce:
    def __init__(self):
        self.parts = []

    def after(self, *others):
        self.state = tie(self.state, others)

    def core(self, pair, *then):
        self.parts.append((pair[0], swap(pair[1], "c", 1, then)))

    def after_core(self, *others):
        self.parts = tie(self.parts, others)

    def chip_direct(self):
        count = lax.axis_size("y") * lax.axis_size("x")
        mine, got = (p.reshape((count, -1) + p.shape[-1:]) for p in self.parts[0])
        self.state = [add(mine[d], got[d]) for d in range(count)]

    def plane_direct(self, *then):
        got = [swap_f(self.state[d], d, then) for d in (1, 2, 3)]
        plane = add(self.state[0], *got)
        zsize = lax.axis_size("z")
        self.state = plane.reshape(zsize, plane.shape[0] // zsize, plane.shape[1])

    def chip(self):
        count = lax.axis_size("y") * lax.axis_size("x")

        def some(blocks, lower):
            out = []
            for d in blocks:
                cuts = []
                for mine, got in self.parts:
                    mine = mine.reshape((count, -1) + mine.shape[-1:])
                    got = got.reshape(mine.shape)
                    half = mine.shape[1] // 2
                    cut = slice(half, None) if lower else slice(None, half)
                    cuts.append(add(mine[d, cut], got[d, cut]))
                out.append(jnp.concatenate(cuts, axis=-1))
            return jnp.stack(out)

        self.state = some((0, 2), False), some((1, 3), False), some((0, 1), True), some((2, 3), True)

    def plane_first(self, *then):
        keep_upper, send_upper, keep_lower, send_lower = self.state
        got_upper, got_lower = swap(send_upper, "x", 1, then), swap(send_lower, "y", 1, then)
        self.state = (
            add(keep_upper[0], got_upper[0]), add(keep_upper[1], got_upper[1]),
            add(keep_lower[0], got_lower[0]), add(keep_lower[1], got_lower[1]),
        )

    def plane_second(self, *then):
        keep_upper, send_upper, keep_lower, send_lower = self.state
        got_upper, got_lower = swap(send_upper, "y", 1, then), swap(send_lower, "x", 1, then)
        plane = jnp.concatenate([add(keep_upper, got_upper), add(keep_lower, got_lower)], axis=0)
        zsize = lax.axis_size("z")
        self.state = plane.reshape(zsize, plane.shape[0] // zsize, plane.shape[1])

    def near_z(self, *then):
        self._along_z(1, then)

    def far_z(self, *then):
        for bit in reversed(bits_down(lax.axis_size("z"))[:-1]):
            self._along_z(bit, then)

    def _along_z(self, bit, then=()):
        side = bit_of("z", bit)
        pairs = self.state.reshape((-1, 2) + self.state.shape[1:])
        other = swap(part(pairs, 1 - side, 1), "z", bit, then)
        self.state = add(part(pairs, side, 1), other)

    def back_far(self, *then):
        self.back = RepGather(self.state[0])
        self.back.far_z(*then)
        self.state = self.back.state

    def back_near(self, *then):
        self.back.state = self.state
        self.back.near_z(*then)
        self.state = self.back.state

    def back_core(self, *then):
        mine = self.state.reshape(-1, self.state.shape[-1])
        both = join(mine, swap(mine, "c", 1, then), lax.axis_index("c"), 0)
        self.state = both.reshape(-1, both.shape[-1])


def product(left_op, right_op, einsum_form):
    return jnp.einsum(einsum_form, left_op, right_op, preferred_element_type=f32)


def normalize(summed_in, gain_row, bias_row):
    row_mean = jnp.mean(summed_in, axis=-1, keepdims=True)
    centered = summed_in - row_mean
    inv_dev = lax.rsqrt(jnp.mean(centered * centered, axis=-1, keepdims=True) + norm_eps)
    unit_rows = centered * inv_dev
    return (unit_rows * gain_row + bias_row, unit_rows, inv_dev)


def norm_back(upstream, unit_rows, inv_dev, gain_row):
    scaled = upstream * gain_row
    grad_in = inv_dev * (
        scaled
        - jnp.mean(scaled, axis=-1, keepdims=True)
        - unit_rows * jnp.mean(scaled * unit_rows, axis=-1, keepdims=True)
    )
    sums = tuple(range(upstream.ndim - 1))
    return (grad_in, jnp.sum(upstream * unit_rows, axis=sums), jnp.sum(upstream, axis=sums))


def gelu_pair(inner_pre):
    cumul = 0.5 * (1.0 + lax.erf(inner_pre * 0.7071067811865476))
    return (
        inner_pre * cumul,
        cumul + inner_pre * jnp.exp(-0.5 * inner_pre * inner_pre) * 0.3989422804014327,
    )


def masked_scores(query_rows, key_rows, key_mask):
    raw_scores = product(query_rows, key_rows, "gqhe,gkhe->ghqk") * (1.0 / math.sqrt(HEAD))
    return jnp.where(key_mask[:, None, None, :], raw_scores, masked_score)


def attend(query_rows, key_rows, value_rows, key_mask):
    scores = masked_scores(query_rows, key_rows, key_mask)
    row_max = jnp.max(scores, axis=-1, keepdims=True)
    log_total = row_max + jnp.log(jnp.sum(jnp.exp(scores - row_max), axis=-1, keepdims=True))
    softmax_w = jnp.exp(scores - log_total).astype(bf16)
    mixed_heads = product(softmax_w, value_rows, "ghqk,gkhe->gqhe").astype(bf16)
    return (mixed_heads, log_total)


def attend_back(query_rows, key_rows, value_rows, key_mask, log_total, grad_mixed):
    scores = masked_scores(query_rows, key_rows, key_mask)
    softmax_w = jnp.exp(scores - log_total)
    grad_value = product(softmax_w.astype(bf16), grad_mixed, "ghqk,gqhe->gkhe")
    grad_probs = product(grad_mixed, value_rows, "gqhe,gkhe->ghqk")
    grad_scores = (
        softmax_w * (grad_probs - jnp.sum(softmax_w * grad_probs, axis=-1, keepdims=True))
    ).astype(bf16)
    inv_root = 1.0 / math.sqrt(HEAD)
    grad_query = product(grad_scores, key_rows, "ghqk,gkhe->gqhe") * inv_root
    grad_key = product(grad_scores, query_rows, "ghqk,gqhe->gkhe") * inv_root
    return (grad_query, grad_key, grad_value)


def split_heads(packed, head_count):
    stacked = packed.reshape(packed.shape[0], packed.shape[1], 3, head_count, HEAD)
    return (stacked[:, :, 0], stacked[:, :, 1], stacked[:, :, 2])


def dot(a, b):
    return lax.dot_general(a, b, (((1,), (0,)), ((), ())), preferred_element_type=f32)


def dot_nt(a, b):
    return lax.dot_general(a, b, (((1,), (1,)), ((), ())), preferred_element_type=f32)


def dot_tn(a, b):
    return lax.dot_general(a, b, (((0,), (0,)), ((), ())), preferred_element_type=f32)


def norm_back_rows(upstream, unit_rows, inv_dev, gain_row):
    scaled = upstream * gain_row
    return inv_dev * (
        scaled
        - jnp.mean(scaled, axis=-1, keepdims=True)
        - unit_rows * jnp.mean(scaled * unit_rows, axis=-1, keepdims=True)
    )


def pair_of(value, low_half):
    zero = jnp.zeros_like(value)
    return jnp.concatenate([jnp.where(low_half, value, zero), jnp.where(low_half, zero, value)], axis=0)


def pair_probs(keys, queries_two, key_ok):
    scores = jnp.where(key_ok, dot_nt(keys, queries_two), masked_score)
    e = jnp.exp(scores - jnp.max(scores, axis=0, keepdims=True))
    return e * (1.0 / jnp.sum(e, axis=0, keepdims=True))


def cost(flops, moved):
    return pl.CostEstimate(flops=flops, bytes_accessed=moved, transcendentals=0)


def attend_kernel(counts_ref, x_ref, w_ref, packed_ref, mixed_ref, *, seg):
    step = pl.program_id(0)
    rows, width = x_ref.shape
    packed_ref[...] = dot(x_ref[...], w_ref[...]).astype(bf16)
    low_half = lax.broadcasted_iota(jnp.int32, (seg, 2 * HEAD), 1) < HEAD
    key_at = lax.broadcasted_iota(jnp.int32, (seg, 2 * seg), 0)
    for s in range(rows // seg):
        key_ok = key_at < counts_ref[step * (rows // seg) + s]
        r = pl.ds(s * seg, seg)
        for p in range(width // (2 * HEAD)):
            col = p * 2 * HEAD
            q = packed_ref[r, pl.ds(col, 2 * HEAD)] * jnp.asarray(HEAD**-0.5, bf16)
            k = packed_ref[r, pl.ds(width + col, 2 * HEAD)]
            v = packed_ref[r, pl.ds(2 * width + col, 2 * HEAD)]
            probs = pair_probs(k, pair_of(q, low_half), key_ok).astype(bf16)
            both = dot_tn(probs, v)
            mixed_ref[r, pl.ds(col, 2 * HEAD)] = jnp.where(low_half, both[:seg], both[seg:]).astype(bf16)


def attend_call(counts, x, w_qkv, rows=256):
    total, width = x.shape
    return pl.pallas_call(
        functools.partial(attend_kernel, seg=total // counts.shape[0]),
        grid_spec=pltpu.PrefetchScalarGridSpec(
            num_scalar_prefetch=1,
            grid=(total // rows,),
            in_specs=[
                pl.BlockSpec((rows, width), lambda i, n: (i, 0)),
                pl.BlockSpec((width, 3 * width), lambda i, n: (0, 0)),
            ],
            out_specs=[
                pl.BlockSpec((rows, 3 * width), lambda i, n: (i, 0)),
                pl.BlockSpec((rows, width), lambda i, n: (i, 0)),
            ],
        ),
        out_shape=[
            jax.ShapeDtypeStruct((total, 3 * width), bf16),
            jax.ShapeDtypeStruct((total, width), bf16),
        ],
        compiler_params=pltpu.CompilerParams(vmem_limit_bytes=VMEM_CAP),
        cost_estimate=cost(8 * total * width * width, 16 << 20),
        name="attend",
    )(counts, x, w_qkv)


def attend_back_kernel(counts_ref, packed_ref, grad_ref, out_ref, *, seg):
    step = pl.program_id(0)
    rows, width = grad_ref.shape
    low_half = lax.broadcasted_iota(jnp.int32, (seg, 2 * HEAD), 1) < HEAD
    key_at = lax.broadcasted_iota(jnp.int32, (seg, 2 * seg), 0)
    root = jnp.asarray(HEAD**-0.5, bf16)
    for s in range(rows // seg):
        key_ok = key_at < counts_ref[step * (rows // seg) + s]
        r = pl.ds(s * seg, seg)
        for p in range(width // (2 * HEAD)):
            col = p * 2 * HEAD
            q_two = pair_of(packed_ref[r, pl.ds(col, 2 * HEAD)] * root, low_half)
            k = packed_ref[r, pl.ds(width + col, 2 * HEAD)]
            v = packed_ref[r, pl.ds(2 * width + col, 2 * HEAD)]
            g_two = pair_of(grad_ref[r, pl.ds(col, 2 * HEAD)], low_half)
            probs = pair_probs(k, q_two, key_ok)
            grad_v = dot(probs.astype(bf16), g_two)
            grad_p = dot_nt(v, g_two)
            weighted = probs * grad_p
            grad_s = (weighted - probs * jnp.sum(weighted, axis=0, keepdims=True)).astype(bf16)
            grad_k = dot(grad_s, q_two)
            both = dot_tn(grad_s, k) * (HEAD**-0.5)
            out_ref[r, pl.ds(col, 2 * HEAD)] = jnp.where(low_half, both[:seg], both[seg:]).astype(bf16)
            out_ref[r, pl.ds(width + col, 2 * HEAD)] = grad_k.astype(bf16)
            out_ref[r, pl.ds(2 * width + col, 2 * HEAD)] = grad_v.astype(bf16)


def attend_back_call(counts, packed, grad_mixed, rows=256):
    total, width = grad_mixed.shape
    return pl.pallas_call(
        functools.partial(attend_back_kernel, seg=total // counts.shape[0]),
        grid_spec=pltpu.PrefetchScalarGridSpec(
            num_scalar_prefetch=1,
            grid=(total // rows,),
            in_specs=[
                pl.BlockSpec((rows, 3 * width), lambda i, n: (i, 0)),
                pl.BlockSpec((rows, width), lambda i, n: (i, 0)),
            ],
            out_specs=pl.BlockSpec((rows, 3 * width), lambda i, n: (i, 0)),
        ),
        out_shape=jax.ShapeDtypeStruct((total, 3 * width), bf16),
        compiler_params=pltpu.CompilerParams(vmem_limit_bytes=VMEM_CAP),
        cost_estimate=cost(16 * total * width * width, 16 << 20),
        name="attend_back",
    )(counts, packed, grad_mixed)


def whole(shape):
    return pl.BlockSpec(shape, lambda *i: (0,) * len(shape))


def rows_of(rows, cols):
    return pl.BlockSpec((rows, cols), lambda i, *n: (i, 0))


def finish_kernel(counts_ref, x_ref, mixed_ref, out_ref, up_ref, down_ref, rows_ref,
                  z1_ref, z2_ref, act_ref, slope_ref, hidden_ref, cls_ref, *, tile, seg):
    step = pl.program_id(0)
    rows, width = x_ref.shape
    z1 = x_ref[...].astype(f32) + dot(mixed_ref[...], out_ref[...])
    z1_ref[...] = z1
    first, _, _ = normalize(z1, rows_ref[0:1], rows_ref[2:3])
    low = first.astype(bf16)
    total = first
    for t in range(up_ref.shape[1] // tile):
        cols = pl.ds(t * tile, tile)
        act, slope = gelu_pair(dot(low, up_ref[:, cols]))
        act = act.astype(bf16)
        act_ref[:, cols] = act
        slope_ref[:, cols] = slope.astype(bf16)
        total = total + dot(act, down_ref[cols, :])
    z2_ref[...] = total
    normed = normalize(total, rows_ref[1:2], rows_ref[3:4])[0]
    at = lax.broadcasted_iota(jnp.int32, (seg, width), 0)
    for s in range(rows // seg):
        here = step * (rows // seg) + s
        block = normed[s * seg : (s + 1) * seg]
        cls_ref[pl.ds(here, 1), :] = block[0:1]
        hidden_ref[s * seg : (s + 1) * seg] = jnp.where(at < counts_ref[here], block, 0.0).astype(bf16)


def pack_kernel(wide_ref, *refs):
    small, o_ref = refs[:-1], refs[-1]
    cols = wide_ref.shape[1]
    o_ref[:, :cols] = wide_ref[...]
    turned, at = 0.0, 0
    for ref in small:
        count = ref.shape[0]
        shape = (count, 128)
        one = lax.broadcasted_iota(jnp.int32, shape, 1) == lax.broadcasted_iota(jnp.int32, shape, 0) + at
        turned = turned + dot_tn(ref[...], one.astype(bf16))
        at += count
    o_ref[:, cols:] = turned.astype(bf16)


def pack_call(wide, small):
    return pl.pallas_call(
        pack_kernel,
        out_shape=jax.ShapeDtypeStruct((wide.shape[0], wide.shape[1] + 128), bf16),
        name="pack",
    )(wide, *small)


def turn_kernel(w_ref, o_ref):
    o_ref[...] = w_ref[...].astype(f32).T


def turn_call(w, at):
    return pl.pallas_call(
        turn_kernel,
        grid=(1,),
        in_specs=[pl.BlockSpec((w.shape[0], 128), lambda i: (0, at))],
        out_specs=whole((128, w.shape[0])),
        out_shape=jax.ShapeDtypeStruct((128, w.shape[0]), f32),
        name="turn",
    )(w)


def up_out_specs(width, ff):
    return [
        pl.BlockSpec((width, width), lambda i, *n: (0, 3)),
        pl.BlockSpec((width, ff), lambda i, *n: (0, 0)),
    ]


def finish_call(counts, x, mixed, w_first, w_up, w_down, small, rows=256, tile=768):
    total, width = x.shape
    ff = w_down.shape[0]
    groups = counts.shape[0]
    narrow, wide = rows_of(rows, width), rows_of(rows, ff)
    return pl.pallas_call(
        functools.partial(finish_kernel, tile=tile, seg=total // groups),
        grid_spec=pltpu.PrefetchScalarGridSpec(
            num_scalar_prefetch=1,
            grid=(total // rows,),
            in_specs=[
                narrow, narrow,
                *up_out_specs(width, ff), whole(w_down.shape),
                whole(small.shape),
            ],
            out_specs=[narrow, narrow, wide, wide, narrow, whole((groups, width))],
        ),
        out_shape=[
            jax.ShapeDtypeStruct((total, width), f32),
            jax.ShapeDtypeStruct((total, width), f32),
            jax.ShapeDtypeStruct((total, ff), bf16),
            jax.ShapeDtypeStruct((total, ff), bf16),
            jax.ShapeDtypeStruct((total, width), bf16),
            jax.ShapeDtypeStruct((groups, width), f32),
        ],
        compiler_params=pltpu.CompilerParams(vmem_limit_bytes=VMEM_CAP),
        cost_estimate=cost(2 * total * width * (width + 2 * ff), 40 << 20),
        name="finish",
    )(counts, x, mixed, w_first, w_up, w_down, small)


def finish_back_kernel(counts_ref, cot_ref, cls_ref, z1_ref, z2_ref, slope_ref, out_ref, up_ref, down_ref,
                       rows_ref,
                       outer_ref, inner_ref, resid_ref, attended_ref, mixed_ref, low_ref, sums_ref, *, tile, seg):
    step = pl.program_id(0)
    rows, width = cot_ref.shape

    @pl.when(step == 0)
    def _():
        sums_ref[...] = jnp.zeros_like(sums_ref)

    at = lax.broadcasted_iota(jnp.int32, (seg, width), 0)
    parts = []
    for s in range(rows // seg):
        here = step * (rows // seg) + s
        block = cot_ref[s * seg : (s + 1) * seg].astype(f32)
        block = jnp.where(at == 0, cls_ref[pl.ds(here, 1), :], block)
        parts.append(jnp.where(at < counts_ref[here], block, 0.0))
    g = jnp.concatenate(parts, axis=0)
    _, unit_two, inv_two = normalize(z2_ref[...], rows_ref[1:2], rows_ref[3:4])
    grad_two = norm_back_rows(g, unit_two, inv_two, rows_ref[1:2])
    outer = grad_two.astype(bf16)
    outer_ref[...] = outer
    sums_ref[1:2] += jnp.sum(g * unit_two, axis=0, keepdims=True)
    sums_ref[3:4] += jnp.sum(g, axis=0, keepdims=True)
    first_grad = grad_two
    for t in range(up_ref.shape[1] // tile):
        cols = pl.ds(t * tile, tile)
        inner = (dot_nt(outer, down_ref[cols, :]) * slope_ref[:, cols].astype(f32)).astype(bf16)
        inner_ref[:, cols] = inner
        first_grad = first_grad + dot_nt(inner, up_ref[:, cols])
    first, unit_one, inv_one = normalize(z1_ref[...], rows_ref[0:1], rows_ref[2:3])
    low_ref[...] = first.astype(bf16)
    grad_one = norm_back_rows(first_grad, unit_one, inv_one, rows_ref[0:1])
    resid_ref[...] = grad_one
    sums_ref[0:1] += jnp.sum(first_grad * unit_one, axis=0, keepdims=True)
    sums_ref[2:3] += jnp.sum(first_grad, axis=0, keepdims=True)
    attended = grad_one.astype(bf16)
    attended_ref[...] = attended
    mixed_ref[...] = dot_nt(attended, out_ref[...]).astype(bf16)


def finish_back_call(counts, cot, cls_grad, z1, z2, slope, w_first, w_up, w_down, small, rows=256, tile=768):
    total, width = cot.shape
    ff = w_down.shape[0]
    groups = counts.shape[0]
    narrow, wide = rows_of(rows, width), rows_of(rows, ff)
    return pl.pallas_call(
        functools.partial(finish_back_kernel, tile=tile, seg=total // groups),
        grid_spec=pltpu.PrefetchScalarGridSpec(
            num_scalar_prefetch=1,
            grid=(total // rows,),
            in_specs=[
                narrow, whole((groups, width)), narrow, narrow, wide,
                *up_out_specs(width, ff), whole(w_down.shape),
                whole(small.shape),
            ],
            out_specs=[narrow, wide, narrow, narrow, narrow, narrow, whole((16, width))],
        ),
        out_shape=[
            jax.ShapeDtypeStruct((total, width), bf16),
            jax.ShapeDtypeStruct((total, ff), bf16),
            jax.ShapeDtypeStruct((total, width), f32),
            jax.ShapeDtypeStruct((total, width), bf16),
            jax.ShapeDtypeStruct((total, width), bf16),
            jax.ShapeDtypeStruct((total, width), bf16),
            jax.ShapeDtypeStruct((16, width), f32),
        ],
        compiler_params=pltpu.CompilerParams(vmem_limit_bytes=VMEM_CAP),
        cost_estimate=cost(2 * total * width * (width + 2 * ff), 40 << 20),
        name="finish_back",
    )(counts, cot, cls_grad, z1, z2, slope, w_first, w_up, w_down, small)


def row_blocks_kernel(ids_ref, a_ref, b_ref, *refs, count):
    extra, (mine_ref, send_ref, turned_ref) = refs[:-3], refs[-3:]
    c, f = ids_ref[0], ids_ref[1]
    half = turned_ref.shape[0] // 2
    unit = half // count

    def place(ref, value):
        for block in range(count):
            for h in range(2):
                to = pl.multiple_of((h ^ c) * half + (block ^ f) * unit, 16)
                ref[pl.ds(to, unit), :] = value[(block * 2 + h) * unit : (block * 2 + h + 1) * unit]

    @pl.when(pl.program_id(0) == 0)
    def _():
        place(turned_ref, a_ref[...].T)

    tile = b_ref.shape[1]
    result = dot(turned_ref[...], b_ref[...]).astype(bf16)
    mine_ref[:, :tile] = result[:half]
    send_ref[:, :tile] = result[half:]
    if extra:
        sums_ref, = extra
        low = sums_ref[...].astype(bf16)
        lanes = lax.broadcasted_iota(jnp.int32, (low.shape[0], 128), 1)
        eye = (lax.broadcasted_iota(jnp.int32, (low.shape[0], 128), 0) == lanes).astype(bf16)
        turned = dot_tn(low, eye).astype(bf16)
        for block in range(count):
            for h in range(2):
                value = turned[(block * 2 + h) * unit : (block * 2 + h + 1) * unit]
                to = pl.multiple_of((block ^ f) * unit, 16)

                @pl.when(h == c)
                def _():
                    mine_ref[pl.ds(to, unit), tile:] = value

                @pl.when(h != c)
                def _():
                    send_ref[pl.ds(to, unit), tile:] = value


def row_blocks_call(ids, a, b, count, sums=None, tile=768):
    total, width = a.shape
    cols = b.shape[1]
    full = cols if sums is None else cols + 128
    step = tile if sums is None else full
    out = pl.BlockSpec((width // 2, step), lambda i, n: (0, i))
    more = [] if sums is None else [sums]
    return pl.pallas_call(
        functools.partial(row_blocks_kernel, count=count),
        grid_spec=pltpu.PrefetchScalarGridSpec(
            num_scalar_prefetch=1,
            grid=(cols // tile,),
            in_specs=[whole(a.shape), pl.BlockSpec((total, tile), lambda i, n: (0, i))] + [whole(m.shape) for m in more],
            out_specs=[out, out],
            scratch_shapes=[pltpu.VMEM((width, total), bf16)],
        ),
        out_shape=[jax.ShapeDtypeStruct((width // 2, full), bf16)] * 2,
        compiler_params=pltpu.CompilerParams(vmem_limit_bytes=VMEM_CAP),
        cost_estimate=cost(2 * total * width * cols * 2, 16 << 20),
        name="row_blocks",
    )(ids, a, b, *more)


def wide_blocks_kernel(ids_ref, a_ref, b_ref, mine_ref, send_ref):
    c = ids_ref[0]
    half = b_ref.shape[1] // 2

    def rows_at(h):
        at = pl.multiple_of(h * half, 128)
        return dot_tn(b_ref[:, pl.ds(at, half)], a_ref[...]).astype(bf16)

    mine_ref[0] = rows_at(c)
    send_ref[0] = rows_at(1 - c)


def wide_blocks_call(ids, a, b, count):
    total, width = a.shape
    block = b.shape[1] // count
    out = pl.BlockSpec((1, block // 2, width), lambda i, n: (i ^ n[1], 0, 0))
    return pl.pallas_call(
        wide_blocks_kernel,
        grid_spec=pltpu.PrefetchScalarGridSpec(
            num_scalar_prefetch=1,
            grid=(count,),
            in_specs=[whole(a.shape), pl.BlockSpec((total, block), lambda i, n: (0, i))],
            out_specs=[out, out],
        ),
        out_shape=[jax.ShapeDtypeStruct((count, block // 2, width), bf16)] * 2,
        compiler_params=pltpu.CompilerParams(vmem_limit_bytes=VMEM_CAP),
        cost_estimate=cost(2 * total * width * b.shape[1] * 2, 16 << 20),
        name="wide_blocks",
    )(ids, a, b)


def token_grad_kernel(resid_ref, g_ref, w_ref, o_ref):
    o_ref[...] = (resid_ref[...] + dot_nt(g_ref[...], w_ref[...])).astype(bf16)


def token_grad_call(resid, g, w_qkv, rows=256):
    total, width = resid.shape
    return pl.pallas_call(
        token_grad_kernel,
        grid=(total // rows,),
        in_specs=[rows_of(rows, width), rows_of(rows, 3 * width), whole((width, 3 * width))],
        out_specs=rows_of(rows, width),
        out_shape=jax.ShapeDtypeStruct((total, width), bf16),
        compiler_params=pltpu.CompilerParams(vmem_limit_bytes=VMEM_CAP),
        cost_estimate=cost(12 * total * width * width, 16 << 20),
        name="token_grad",
    )(resid, g, w_qkv)


def cross_message(cse_qkv, cse_out, cse_up, cse_down, fsize, f):
    rows, width = cse_qkv.shape[0], cse_out.shape[1]
    ff = cse_up.shape[1]
    slim = width // fsize
    cols = jnp.concatenate(
        [
            cse_qkv.reshape(rows, 3, fsize, slim).transpose(2, 0, 1, 3).reshape(fsize, rows, 3 * slim),
            cse_up.reshape(rows, fsize, ff // fsize).transpose(1, 0, 2),
        ],
        axis=-1,
    )
    mine = in_order([part(cols, f, 0)] + [swap_f(part(cols, f ^ d, 0), d) for d in (1, 2, 3)])
    flat = mine.reshape(fsize * rows, -1)
    frows = cse_down.shape[0]
    out_flat = jnp.concatenate([cse_out[:, k * slim : (k + 1) * slim] for k in range(fsize)], axis=0)
    return jnp.concatenate([flat, cse_down, out_flat], axis=-1)


def unpack_kernel(m_ref, qkv_ref, out_ref, up_ref, down_ref, *, fsize):
    reps, frows, _ = m_ref.shape
    rows = frows // fsize
    width, a = qkv_ref.shape
    b, slim = a + up_ref.shape[1], width // fsize
    for r in range(reps):
        for k in range(fsize):
            at, here = k * reps * rows + r * rows, slice(k * rows, (k + 1) * rows)
            qkv_ref[at : at + rows, :] = m_ref[r, here, :a]
            up_ref[at : at + rows, :] = m_ref[r, here, a:b]
        down_ref[r * frows : (r + 1) * frows, :] = m_ref[r, :, b : b + width]
        out = [m_ref[r, k * rows : (k + 1) * rows, b + width :] for k in range(fsize)]
        out_ref[r * rows : (r + 1) * rows, :] = jnp.concatenate(out, axis=-1)


def cross_unpack(gathered, width, ff, fsize):
    reps, frows = gathered.shape[:2]
    slim = width // fsize
    if frows // fsize % 8:
        return cross_unpack_small(gathered, width, ff, fsize)
    shapes = [(width, 3 * slim), (slim, width), (width, ff // fsize), (ff // fsize, width)]
    return pl.pallas_call(
        functools.partial(unpack_kernel, fsize=fsize),
        out_shape=[jax.ShapeDtypeStruct(shape, bf16) for shape in shapes],
        compiler_params=pltpu.CompilerParams(vmem_limit_bytes=VMEM_CAP),
        name="unpack",
    )(gathered)


def cross_unpack_small(gathered, width, ff, fsize):
    slim = width // fsize
    reps, frows = gathered.shape[:2]
    rows = frows // fsize
    a, b = 3 * slim, 3 * slim + ff // fsize
    by_row = gathered[:, :, :b].reshape(reps, fsize, rows, b).transpose(1, 0, 2, 3).reshape(-1, b)
    qkv = by_row[:, :a]
    up = by_row[:, a:]
    down = gathered[:, :, b : b + width].reshape(-1, width)
    out = gathered[:, :, b + width :].reshape(reps, fsize, rows, slim).transpose(0, 2, 1, 3).reshape(-1, width)
    return qkv, out, up, down


def cross_block(cls_in, cotan, weights, gains, biases, fsize, f):
    qkv, out, up, down = weights
    segs, width = cls_in.shape
    slim = width // fsize
    heads = slim // HEAD
    packed = product(cls_in[None], qkv, "gsd,de->gse").astype(bf16)
    queries, keys, values = split_heads(packed, heads)
    every = jnp.ones((1, segs), jnp.bool_)
    mixed, log_total = attend(queries, keys, values, every)
    mixed = mixed.reshape(segs, slim)
    attended = sum_f(product(mixed, out, "sd,de->se"))
    first, unit_one, inv_one = normalize(cls_in.astype(f32) + attended, gains[0], biases[0])
    first_low = first.astype(bf16)
    activated, slope = gelu_pair(product(first_low, up, "sd,df->sf"))
    act_low = activated.astype(bf16)
    outer = sum_f(product(act_low, down, "sf,fd->sd"))
    cls_out, unit_two, inv_two = normalize(first + outer, gains[1], biases[1])

    grad_two, gain_two, bias_two = norm_back(cotan, unit_two, inv_two, gains[1])
    grad_outer = grad_two.astype(bf16)
    grad_inner = (product(grad_outer, down, "sd,fd->sf") * slope).astype(bf16)
    grad_first = grad_two + sum_f(product(grad_inner, up, "sf,df->sd"))
    grad_one, gain_one, bias_one = norm_back(grad_first, unit_one, inv_one, gains[0])
    grad_attended = grad_one.astype(bf16)
    grad_mixed = product(grad_attended, out, "se,de->sd").astype(bf16)
    grad_q, grad_k, grad_v = attend_back(
        queries, keys, values, every, log_total, grad_mixed.reshape(1, segs, heads, HEAD)
    )
    grad_packed = jnp.concatenate(
        [grad_q.reshape(segs, slim), grad_k.reshape(segs, slim), grad_v.reshape(segs, slim)], axis=-1
    ).astype(bf16)
    grad_in = grad_one + sum_f(product(grad_packed, qkv, "se,de->sd"))

    def own(value):
        return lax.dynamic_slice_in_dim(value, f * slim, slim, value.ndim - 1)

    sums = jnp.stack([gain_one, gain_two, bias_one, bias_two])
    pieces = {
        "packed": grad_packed,
        "inner": grad_inner,
        "act": act_low,
        "outer": grad_outer,
        "attended": grad_attended,
        "mixed": mixed,
        "own_in": own(cls_in),
        "own_low": own(first_low),
        "own_grad": own(grad_in).astype(bf16),
        "sums": jnp.pad(own(sums), ((0, segs - 4), (0, 0))).astype(bf16),
    }
    return cls_out, grad_in, pieces


def doc_message(spread, pieces, fsize, width):
    segs = spread.shape[1]
    slim = width // fsize
    qkv_cols = spread[:, :, : 3 * slim].reshape(fsize, segs, 3, slim).transpose(1, 2, 0, 3)
    parts = {"packed": qkv_cols.reshape(segs, 3 * width), "inner": spread[:, :, 3 * slim :].transpose(1, 0, 2).reshape(segs, -1)}
    parts = {**pieces, **parts}
    ends, at = {}, 0
    for name, value in parts.items():
        ends[name] = (at, at + value.shape[1])
        at += value.shape[1] + -value.shape[1] % 128
    parts = {k: jnp.pad(v, ((0, 0), (0, -v.shape[1] % 128))) for k, v in parts.items()}
    return jnp.concatenate(list(parts.values()), axis=-1), ends


def cross_grads(docs, ends, names):
    flat = docs.reshape(-1, docs.shape[-1])

    def cut(name):
        return flat[:, slice(*ends[name])]

    pairs = {"qkv": ("own_in", "packed"), "out": ("mixed", "attended"), "up": ("own_low", "inner"), "down": ("act", "outer")}
    grads = {k: product(cut(pairs[k][0]), cut(pairs[k][1]), "rd,re->de") for k in names if k in pairs}
    if "rest" in names:
        grads["positions"] = jnp.sum(docs[:, :, slice(*ends["own_grad"])].astype(f32), axis=0)
        sums = jnp.sum(docs[:, :4, slice(*ends["sums"])].astype(f32), axis=0)
        grads["gains"], grads["biases"] = sums[0:2], sums[2:4]
    return grads


def per_device(
    tokens, counts, cotangent,
    swe_qkv, swe_out, swe_up, swe_down, swe_gains, swe_biases,
    cse_qkv, cse_out, cse_up, cse_down, cse_gains, cse_biases, positions,
):
    docs_here, local_len, width = tokens.shape
    ff = swe_up.shape[1]
    seg_here = counts.shape[1]
    groups = docs_here * seg_here
    fsize = lax.axis_size("y") * lax.axis_size("x")
    f = lax.axis_index("y") * lax.axis_size("x") + lax.axis_index("x")
    c = lax.axis_index("c")
    ids = jnp.stack([c, f])
    segs = fsize * seg_here
    x = tokens.reshape(-1, width)
    cot = cotangent.reshape(-1, width)
    lens = counts.reshape(groups)

    small = [swe_gains, swe_biases, cse_gains, cse_biases, positions]
    count_small = sum(v.shape[0] for v in small)
    packed_up = pack_call(swe_up, small)
    w_up = lax.all_gather(packed_up, ("y", "x", "z", "c"), axis=0, tiled=True)
    first = RowGather(tie(jnp.concatenate([swe_qkv, swe_out], axis=-1), packed_up))
    first.far_z()
    down = RowGather(tie(swe_down, first.state))
    first.near_z()
    first.after(down.state)
    down.after(first.state)
    turned = first.state
    first.plane_first()
    down.far_z()
    message = cross_message(*tie((cse_qkv, cse_out, cse_up, cse_down), turned), fsize, f)
    down.after(first.state)
    first.after(down.state, message)
    first.plane_second()
    down.near_z()
    first.after(down.state)
    down.after(first.state)
    first.sibling()
    w_first = side_by_side(*first.state, c)
    down.plane_first(w_first)
    packed, mixed = attend_call(lens, x, tie(w_first, down.state))
    down.plane_second(packed)
    w_up = tie(w_up, packed, down.state)
    down.after(w_up)
    cross = lax.all_gather(tie(message, w_up), ("z", "c"), axis=0)
    down.sibling()
    w_down = side_by_side(*down.state, c)
    rows = turn_call(w_up, ff // 128)
    gains, biases, cross_gains, cross_biases, pos = (
        rows[0:2], rows[2:4], rows[4:6], rows[6:8], rows[8:count_small]
    )
    z1, z2, act, slope, hidden, cls_rows = finish_call(lens, x, mixed, w_first, w_up, w_down, rows)
    cross_w = cross_unpack(cross, width, ff, fsize)

    pos_here = lax.dynamic_slice_in_dim(pos, f * seg_here, seg_here, 0)
    cls_here = (cls_rows + pos_here).astype(bf16)
    cls_cot = cot.reshape(groups, -1, width)[:, 0]
    both = gather_f(jnp.concatenate([cls_here, cls_cot], axis=-1), cross_w).reshape(segs, 2 * width)
    cls_out, cls_grad, pieces = cross_block(
        both[:, :width], both[:, width:].astype(f32), cross_w, cross_gains, cross_biases, fsize, f,
    )
    cls_out = lax.dynamic_slice_in_dim(cls_out, f * seg_here, seg_here, 0)
    cls_here_grad = lax.dynamic_slice_in_dim(cls_grad, f * seg_here, seg_here, 0)

    spread = tie(jnp.concatenate([pieces["packed"], pieces["inner"]], axis=-1), cls_grad)
    outer, inner, resid, attended, grad_mixed, low, sums = finish_back_call(
        lens, cot, tie(cls_here_grad, spread), z1, z2, slope, w_first, w_up, w_down, rows
    )
    spread = gather_f(spread, outer)
    layer_out = hidden.reshape(groups, -1, width).at[:, 0].set(tie(cls_out.astype(bf16), outer))
    message, ends = doc_message(tie(spread, outer), pieces, fsize, width)
    docs = lax.all_gather(message, ("z", "c"), axis=0)
    red_down, red_up, red_qkv = RowReduce(), RowReduce(), RowReduce()
    g_down = wide_blocks_call(ids, tie(outer, message), act, fsize)
    g_out = row_blocks_call(ids, tie(mixed, g_down), attended, fsize, sums)
    red_down.core(g_down, g_out)
    red_down.chip()
    g_up = row_blocks_call(ids, tie(low, red_down.state), inner, fsize)
    red_down.plane_first(g_up)
    red_up.core(g_out, g_up)
    red_up.core(tie(g_up, red_down.state))
    red_up.chip()
    red_down.after(red_up.state)
    grad_packed = attend_back_call(lens, packed, tie(grad_mixed, red_up.state, red_down.state))
    red_down.plane_second(grad_packed)
    red_up.plane_first(grad_packed)
    red_down.after(grad_packed, red_up.state)
    red_up.after(red_down.state)
    g_qkv = row_blocks_call(ids, x, tie(grad_packed, red_up.state, red_down.state), fsize)
    red_up.plane_second(g_qkv)
    red_down.near_z(g_qkv)
    red_qkv.core(tie(g_qkv, red_up.state, red_down.state))
    red_qkv.chip_direct()
    red_down.far_z(red_qkv.state)
    red_up.near_z(red_qkv.state)
    red_up.after(red_qkv.state, red_down.state)
    red_down.after(red_up.state)
    token_grad = token_grad_call(tie(resid, red_qkv.state, red_down.state, red_up.state), grad_packed, w_first)
    others = cross_grads(tie(docs, token_grad), ends, ("up", "qkv"))
    red_qkv.plane_direct(token_grad, others)
    lead = red_qkv.state
    others |= cross_grads(tie(docs, lead), ends, ("down", "out", "rest"))
    red_down.back_far(token_grad, lead)
    red_up.far_z(token_grad, lead)
    red_qkv.near_z()
    lead = red_qkv.state
    red_down.back_near(lead)
    red_up.back_far(lead)
    red_qkv.far_z()
    lead = red_qkv.state
    red_down.back_core(lead)
    red_up.back_near(lead)
    red_qkv.back_far()
    lead = red_qkv.state
    red_up.back_core(lead)
    done_down = red_down.state.astype(f32)
    red_qkv.back_near()
    red_qkv.after(done_down, layer_out, others)
    red_qkv.back_core()
    done_up = red_up.state.astype(f32)
    done_qkv = red_qkv.state.astype(f32)
    pick = (jnp.arange(128)[None, :] == jnp.arange(4)[:, None]).astype(bf16)
    small_grads = product(pick, red_up.state[:, width : width + 128], "kc,rc->kr")
    return (
        layer_out.reshape(tokens.shape),
        token_grad.reshape(tokens.shape),
        done_qkv,
        done_up[:, :width],
        done_up[:, width + 128 :],
        done_down,
        small_grads[0:2],
        small_grads[2:4],
    ) + tuple(others[k] for k in ("qkv", "out", "up", "down", "gains", "biases", "positions"))


def solution(mesh):
    fsize, rsize = mesh.shape["fsdp"], mesh.shape["rep"]
    fine = Mesh(mesh.devices.reshape(2, fsize // 2, rsize // 2, 2), ("y", "x", "z", "c"))
    fs, rep = ("y", "x"), ("z", "c")
    every = fs + rep
    by_rows, by_cols = P(every, None), P(None, every)
    block = (by_rows,) * 4 + (by_cols,) * 2
    grads = (P(fs, None),) * 4 + (P(None, fs),) * 2
    return jax.shard_map(
        per_device,
        mesh=fine,
        in_specs=(P(rep, fs, None), P(rep, fs), P(rep, fs, None)) + block + block + (by_cols,),
        out_specs=(P(rep, fs, None),) * 2 + grads + grads + (P(None, fs),),
        check_vma=False,
    )
```

```python
import functools
import math

import jax
import jax.numpy as jnp
from jax import lax
from jax.experimental import pallas as pl
from jax.experimental.pallas import tpu as pltpu
from jax.sharding import Mesh
from jax.sharding import PartitionSpec as P

HEAD = 64
norm_eps = 1e-05
masked_score = -1000000000.0
bf16, f32 = jnp.bfloat16, jnp.float32
VMEM_CAP = 56 << 20


def tie(values, *after):
    return lax.optimization_barrier((values, after))[0]


def swap(value, axis, bit, then=()):
    size = lax.axis_size(axis)
    got = lax.ppermute(value, axis, [(i, i ^ bit) for i in range(size)])
    return tie(got, then) if then else got


def bit_of(axis, bit):
    return (lax.axis_index(axis) // bit) % 2


def join(mine, other, side, axis):
    first = side == 0
    return jnp.stack([jnp.where(first, mine, other), jnp.where(first, other, mine)], axis=axis)


def side_by_side(mine, other, side):
    both = jnp.concatenate([other, other], axis=-1)
    return lax.dynamic_update_slice_in_dim(both, mine, side * mine.shape[-1], axis=-1)


def part(value, side, axis):
    return lax.dynamic_index_in_dim(value, side, axis, keepdims=False)


def bits_down(size):
    return [1 << k for k in reversed(range(size.bit_length() - 1))]


class RowGather:
    def __init__(self, shard):
        rows, cols = shard.shape
        half = cols // 2
        c = lax.axis_index("c")
        keep = lax.dynamic_slice_in_dim(shard, c * half, half, 1)
        send = lax.dynamic_slice_in_dim(shard, (1 - c) * half, half, 1)
        self.state = join(keep, swap(send, "c", 1), c, 0).reshape(1, 2 * rows, half)

    def after(self, *others):
        self.state = tie(self.state, others)

    def far_z(self, *then):
        bits = bits_down(lax.axis_size("z"))
        for bit in bits[:-1]:
            self._along_z(bit, then)

    def near_z(self, *then):
        self._along_z(1, then)

    def _along_z(self, bit, then=()):
        got = self.state
        got = join(got, swap(got, "z", bit, then), bit_of("z", bit), 1)
        self.state = got.reshape((-1,) + got.shape[2:])

    def plane_first(self, *then):
        zhalf = self.state.shape[0] // 2
        one, two = self.state[:zhalf], self.state[zhalf:]
        got_one, got_two = swap(one, "x", 1, then), swap(two, "y", 1, then)
        self.state = join(one, got_one, lax.axis_index("x"), 0), join(two, got_two, lax.axis_index("y"), 0)

    def plane_second(self, *then):
        one, two = self.state
        got_one, got_two = swap(one, "y", 1, then), swap(two, "x", 1, then)
        one = join(one, got_one, lax.axis_index("y"), 0)
        two = join(two, got_two, lax.axis_index("x"), 1)
        both = jnp.concatenate([one, two], axis=2)
        self.state = both.reshape(-1, both.shape[-1])

    def sibling(self, *then):
        self.state = self.state, swap(self.state, "c", 1, then)


class RepGather:
    def __init__(self, message):
        self.state = message[None]

    far_z = RowGather.far_z
    near_z = RowGather.near_z
    after = RowGather.after

    def _along_z(self, bit, then=()):
        got = self.state
        got = join(got, swap(got, "z", bit, then), bit_of("z", bit), 1)
        self.state = got.reshape((-1,) + got.shape[2:])

    def sibling(self, *then):
        self.state = join(self.state, swap(self.state, "c", 1, then), lax.axis_index("c"), 1)


def swap_f(value, dist, then=()):
    count = lax.axis_size("y") * lax.axis_size("x")
    got = lax.ppermute(value, ("y", "x"), [(i, i ^ dist) for i in range(count)])
    return tie(got, then) if then else got


def in_order(parts):
    y, x = lax.axis_index("y"), lax.axis_index("x")
    row0 = [jnp.where(x == 0, parts[0], parts[1]), jnp.where(x == 0, parts[1], parts[0])]
    row1 = [jnp.where(x == 0, parts[2], parts[3]), jnp.where(x == 0, parts[3], parts[2])]
    top, low = jnp.stack(row0), jnp.stack(row1)
    return jnp.concatenate([jnp.where(y == 0, top, low), jnp.where(y == 0, low, top)])


def gather_f(value, *then):
    return in_order([value] + [swap_f(value, d, then) for d in (1, 2, 3)])


def sum_f(value):
    got = [value] + [swap_f(value, d) for d in (1, 2, 3)]
    return (got[0] + got[1]) + (got[2] + got[3])


def add(*terms):
    total = terms[0].astype(f32)
    for term in terms[1:]:
        total = total + term.astype(f32)
    return total.astype(bf16)


class RowReduce:
    def __init__(self):
        self.parts = []

    def after(self, *others):
        self.state = tie(self.state, others)

    def core(self, pair, *then):
        self.parts.append((pair[0], swap(pair[1], "c", 1, then)))

    def after_core(self, *others):
        self.parts = tie(self.parts, others)

    def chip_direct(self):
        count = lax.axis_size("y") * lax.axis_size("x")
        mine, got = (p.reshape((count, -1) + p.shape[-1:]) for p in self.parts[0])
        self.state = [add(mine[d], got[d]) for d in range(count)]

    def plane_direct(self, *then):
        got = [swap_f(self.state[d], d, then) for d in (1, 2, 3)]
        plane = add(self.state[0], *got)
        zsize = lax.axis_size("z")
        self.state = plane.reshape(zsize, plane.shape[0] // zsize, plane.shape[1])

    def chip(self):
        count = lax.axis_size("y") * lax.axis_size("x")

        def some(blocks, lower):
            out = []
            for d in blocks:
                cuts = []
                for mine, got in self.parts:
                    mine = mine.reshape((count, -1) + mine.shape[-1:])
                    got = got.reshape(mine.shape)
                    half = mine.shape[1] // 2
                    cut = slice(half, None) if lower else slice(None, half)
                    cuts.append(add(mine[d, cut], got[d, cut]))
                out.append(jnp.concatenate(cuts, axis=-1))
            return jnp.stack(out)

        self.state = some((0, 2), False), some((1, 3), False), some((0, 1), True), some((2, 3), True)

    def plane_first(self, *then):
        keep_upper, send_upper, keep_lower, send_lower = self.state
        got_upper, got_lower = swap(send_upper, "x", 1, then), swap(send_lower, "y", 1, then)
        self.state = (
            add(keep_upper[0], got_upper[0]), add(keep_upper[1], got_upper[1]),
            add(keep_lower[0], got_lower[0]), add(keep_lower[1], got_lower[1]),
        )

    def plane_second(self, *then):
        keep_upper, send_upper, keep_lower, send_lower = self.state
        got_upper, got_lower = swap(send_upper, "y", 1, then), swap(send_lower, "x", 1, then)
        plane = jnp.concatenate([add(keep_upper, got_upper), add(keep_lower, got_lower)], axis=0)
        zsize = lax.axis_size("z")
        self.state = plane.reshape(zsize, plane.shape[0] // zsize, plane.shape[1])

    def near_z(self, *then):
        self._along_z(1, then)

    def far_z(self, *then):
        for bit in reversed(bits_down(lax.axis_size("z"))[:-1]):
            self._along_z(bit, then)

    def _along_z(self, bit, then=()):
        side = bit_of("z", bit)
        pairs = self.state.reshape((-1, 2) + self.state.shape[1:])
        other = swap(part(pairs, 1 - side, 1), "z", bit, then)
        self.state = add(part(pairs, side, 1), other)

    def back_far(self, *then):
        self.back = RepGather(self.state[0])
        self.back.far_z(*then)
        self.state = self.back.state

    def back_near(self, *then):
        self.back.state = self.state
        self.back.near_z(*then)
        self.state = self.back.state

    def back_core(self, *then):
        mine = self.state.reshape(-1, self.state.shape[-1])
        both = join(mine, swap(mine, "c", 1, then), lax.axis_index("c"), 0)
        self.state = both.reshape(-1, both.shape[-1])


def product(left_op, right_op, einsum_form):
    return jnp.einsum(einsum_form, left_op, right_op, preferred_element_type=f32)


def normalize(summed_in, gain_row, bias_row):
    row_mean = jnp.mean(summed_in, axis=-1, keepdims=True)
    centered = summed_in - row_mean
    inv_dev = lax.rsqrt(jnp.mean(centered * centered, axis=-1, keepdims=True) + norm_eps)
    unit_rows = centered * inv_dev
    return (unit_rows * gain_row + bias_row, unit_rows, inv_dev)


def norm_back(upstream, unit_rows, inv_dev, gain_row):
    scaled = upstream * gain_row
    grad_in = inv_dev * (
        scaled
        - jnp.mean(scaled, axis=-1, keepdims=True)
        - unit_rows * jnp.mean(scaled * unit_rows, axis=-1, keepdims=True)
    )
    sums = tuple(range(upstream.ndim - 1))
    return (grad_in, jnp.sum(upstream * unit_rows, axis=sums), jnp.sum(upstream, axis=sums))


def gelu_pair(inner_pre):
    cumul = 0.5 * (1.0 + lax.erf(inner_pre * 0.7071067811865476))
    return (
        inner_pre * cumul,
        cumul + inner_pre * jnp.exp(-0.5 * inner_pre * inner_pre) * 0.3989422804014327,
    )


def masked_scores(query_rows, key_rows, key_mask):
    raw_scores = product(query_rows, key_rows, "gqhe,gkhe->ghqk") * (1.0 / math.sqrt(HEAD))
    return jnp.where(key_mask[:, None, None, :], raw_scores, masked_score)


def attend(query_rows, key_rows, value_rows, key_mask):
    scores = masked_scores(query_rows, key_rows, key_mask)
    row_max = jnp.max(scores, axis=-1, keepdims=True)
    log_total = row_max + jnp.log(jnp.sum(jnp.exp(scores - row_max), axis=-1, keepdims=True))
    softmax_w = jnp.exp(scores - log_total).astype(bf16)
    mixed_heads = product(softmax_w, value_rows, "ghqk,gkhe->gqhe").astype(bf16)
    return (mixed_heads, log_total)


def attend_back(query_rows, key_rows, value_rows, key_mask, log_total, grad_mixed):
    scores = masked_scores(query_rows, key_rows, key_mask)
    softmax_w = jnp.exp(scores - log_total)
    grad_value = product(softmax_w.astype(bf16), grad_mixed, "ghqk,gqhe->gkhe")
    grad_probs = product(grad_mixed, value_rows, "gqhe,gkhe->ghqk")
    grad_scores = (
        softmax_w * (grad_probs - jnp.sum(softmax_w * grad_probs, axis=-1, keepdims=True))
    ).astype(bf16)
    inv_root = 1.0 / math.sqrt(HEAD)
    grad_query = product(grad_scores, key_rows, "ghqk,gkhe->gqhe") * inv_root
    grad_key = product(grad_scores, query_rows, "ghqk,gqhe->gkhe") * inv_root
    return (grad_query, grad_key, grad_value)


def split_heads(packed, head_count):
    stacked = packed.reshape(packed.shape[0], packed.shape[1], 3, head_count, HEAD)
    return (stacked[:, :, 0], stacked[:, :, 1], stacked[:, :, 2])


def dot(a, b):
    return lax.dot_general(a, b, (((1,), (0,)), ((), ())), preferred_element_type=f32)


def dot_nt(a, b):
    return lax.dot_general(a, b, (((1,), (1,)), ((), ())), preferred_element_type=f32)


def dot_tn(a, b):
    return lax.dot_general(a, b, (((0,), (0,)), ((), ())), preferred_element_type=f32)


def norm_back_rows(upstream, unit_rows, inv_dev, gain_row):
    scaled = upstream * gain_row
    return inv_dev * (
        scaled
        - jnp.mean(scaled, axis=-1, keepdims=True)
        - unit_rows * jnp.mean(scaled * unit_rows, axis=-1, keepdims=True)
    )


def pair_of(value, low_half):
    zero = jnp.zeros_like(value)
    return jnp.concatenate([jnp.where(low_half, value, zero), jnp.where(low_half, zero, value)], axis=0)


def pair_probs(keys, queries_two, key_ok):
    scores = jnp.where(key_ok, dot_nt(keys, queries_two), masked_score)
    e = jnp.exp(scores - jnp.max(scores, axis=0, keepdims=True))
    return e * (1.0 / jnp.sum(e, axis=0, keepdims=True))


def cost(flops, moved):
    return pl.CostEstimate(flops=flops, bytes_accessed=moved, transcendentals=0)


def attend_kernel(counts_ref, x_ref, w_ref, packed_ref, mixed_ref, *, seg):
    step = pl.program_id(0)
    rows, width = x_ref.shape
    packed_ref[...] = dot(x_ref[...], w_ref[...]).astype(bf16)
    low_half = lax.broadcasted_iota(jnp.int32, (seg, 2 * HEAD), 1) < HEAD
    key_at = lax.broadcasted_iota(jnp.int32, (seg, 2 * seg), 0)
    for s in range(rows // seg):
        key_ok = key_at < counts_ref[step * (rows // seg) + s]
        r = pl.ds(s * seg, seg)
        for p in range(width // (2 * HEAD)):
            col = p * 2 * HEAD
            q = packed_ref[r, pl.ds(col, 2 * HEAD)] * jnp.asarray(HEAD**-0.5, bf16)
            k = packed_ref[r, pl.ds(width + col, 2 * HEAD)]
            v = packed_ref[r, pl.ds(2 * width + col, 2 * HEAD)]
            probs = pair_probs(k, pair_of(q, low_half), key_ok).astype(bf16)
            both = dot_tn(probs, v)
            mixed_ref[r, pl.ds(col, 2 * HEAD)] = jnp.where(low_half, both[:seg], both[seg:]).astype(bf16)


def attend_call(counts, x, w_qkv, rows=256):
    total, width = x.shape
    return pl.pallas_call(
        functools.partial(attend_kernel, seg=total // counts.shape[0]),
        grid_spec=pltpu.PrefetchScalarGridSpec(
            num_scalar_prefetch=1,
            grid=(total // rows,),
            in_specs=[
                pl.BlockSpec((rows, width), lambda i, n: (i, 0)),
                pl.BlockSpec((width, 3 * width), lambda i, n: (0, 0)),
            ],
            out_specs=[
                pl.BlockSpec((rows, 3 * width), lambda i, n: (i, 0)),
                pl.BlockSpec((rows, width), lambda i, n: (i, 0)),
            ],
        ),
        out_shape=[
            jax.ShapeDtypeStruct((total, 3 * width), bf16),
            jax.ShapeDtypeStruct((total, width), bf16),
        ],
        compiler_params=pltpu.CompilerParams(vmem_limit_bytes=VMEM_CAP),
        cost_estimate=cost(8 * total * width * width, 16 << 20),
        name="attend",
    )(counts, x, w_qkv)


def attend_back_kernel(counts_ref, packed_ref, grad_ref, out_ref, *, seg):
    step = pl.program_id(0)
    rows, width = grad_ref.shape
    low_half = lax.broadcasted_iota(jnp.int32, (seg, 2 * HEAD), 1) < HEAD
    key_at = lax.broadcasted_iota(jnp.int32, (seg, 2 * seg), 0)
    root = jnp.asarray(HEAD**-0.5, bf16)
    for s in range(rows // seg):
        key_ok = key_at < counts_ref[step * (rows // seg) + s]
        r = pl.ds(s * seg, seg)
        for p in range(width // (2 * HEAD)):
            col = p * 2 * HEAD
            q_two = pair_of(packed_ref[r, pl.ds(col, 2 * HEAD)] * root, low_half)
            k = packed_ref[r, pl.ds(width + col, 2 * HEAD)]
            v = packed_ref[r, pl.ds(2 * width + col, 2 * HEAD)]
            g_two = pair_of(grad_ref[r, pl.ds(col, 2 * HEAD)], low_half)
            probs = pair_probs(k, q_two, key_ok)
            grad_v = dot(probs.astype(bf16), g_two)
            grad_p = dot_nt(v, g_two)
            weighted = probs * grad_p
            grad_s = (weighted - probs * jnp.sum(weighted, axis=0, keepdims=True)).astype(bf16)
            grad_k = dot(grad_s, q_two)
            both = dot_tn(grad_s, k) * (HEAD**-0.5)
            out_ref[r, pl.ds(col, 2 * HEAD)] = jnp.where(low_half, both[:seg], both[seg:]).astype(bf16)
            out_ref[r, pl.ds(width + col, 2 * HEAD)] = grad_k.astype(bf16)
            out_ref[r, pl.ds(2 * width + col, 2 * HEAD)] = grad_v.astype(bf16)


def attend_back_call(counts, packed, grad_mixed, rows=256):
    total, width = grad_mixed.shape
    return pl.pallas_call(
        functools.partial(attend_back_kernel, seg=total // counts.shape[0]),
        grid_spec=pltpu.PrefetchScalarGridSpec(
            num_scalar_prefetch=1,
            grid=(total // rows,),
            in_specs=[
                pl.BlockSpec((rows, 3 * width), lambda i, n: (i, 0)),
                pl.BlockSpec((rows, width), lambda i, n: (i, 0)),
            ],
            out_specs=pl.BlockSpec((rows, 3 * width), lambda i, n: (i, 0)),
        ),
        out_shape=jax.ShapeDtypeStruct((total, 3 * width), bf16),
        compiler_params=pltpu.CompilerParams(vmem_limit_bytes=VMEM_CAP),
        cost_estimate=cost(16 * total * width * width, 16 << 20),
        name="attend_back",
    )(counts, packed, grad_mixed)


def whole(shape):
    return pl.BlockSpec(shape, lambda *i: (0,) * len(shape))


def rows_of(rows, cols):
    return pl.BlockSpec((rows, cols), lambda i, *n: (i, 0))


def finish_kernel(counts_ref, x_ref, mixed_ref, out_ref, up_ref, down_ref, rows_ref,
                  z1_ref, z2_ref, act_ref, slope_ref, hidden_ref, cls_ref, *, tile, seg):
    step = pl.program_id(0)
    rows, width = x_ref.shape
    z1 = x_ref[...].astype(f32) + dot(mixed_ref[...], out_ref[...])
    z1_ref[...] = z1
    first, _, _ = normalize(z1, rows_ref[0:1], rows_ref[2:3])
    low = first.astype(bf16)
    total = first
    for t in range(up_ref.shape[1] // tile):
        cols = pl.ds(t * tile, tile)
        act, slope = gelu_pair(dot(low, up_ref[:, cols]))
        act = act.astype(bf16)
        act_ref[:, cols] = act
        slope_ref[:, cols] = slope.astype(bf16)
        total = total + dot(act, down_ref[cols, :])
    z2_ref[...] = total
    normed = normalize(total, rows_ref[1:2], rows_ref[3:4])[0]
    at = lax.broadcasted_iota(jnp.int32, (seg, width), 0)
    for s in range(rows // seg):
        here = step * (rows // seg) + s
        block = normed[s * seg : (s + 1) * seg]
        cls_ref[pl.ds(here, 1), :] = block[0:1]
        hidden_ref[s * seg : (s + 1) * seg] = jnp.where(at < counts_ref[here], block, 0.0).astype(bf16)


def pack_kernel(wide_ref, *refs):
    small, o_ref = refs[:-1], refs[-1]
    cols = wide_ref.shape[1]
    o_ref[:, :cols] = wide_ref[...]
    turned, at = 0.0, 0
    for ref in small:
        count = ref.shape[0]
        shape = (count, 128)
        one = lax.broadcasted_iota(jnp.int32, shape, 1) == lax.broadcasted_iota(jnp.int32, shape, 0) + at
        turned = turned + dot_tn(ref[...], one.astype(bf16))
        at += count
    o_ref[:, cols:] = turned.astype(bf16)


def pack_call(wide, small):
    return pl.pallas_call(
        pack_kernel,
        out_shape=jax.ShapeDtypeStruct((wide.shape[0], wide.shape[1] + 128), bf16),
        name="pack",
    )(wide, *small)


def turn_kernel(w_ref, o_ref):
    o_ref[...] = w_ref[...].astype(f32).T


def turn_call(w, at):
    return pl.pallas_call(
        turn_kernel,
        grid=(1,),
        in_specs=[pl.BlockSpec((w.shape[0], 128), lambda i: (0, at))],
        out_specs=whole((128, w.shape[0])),
        out_shape=jax.ShapeDtypeStruct((128, w.shape[0]), f32),
        name="turn",
    )(w)


def up_out_specs(width, ff):
    return [
        pl.BlockSpec((width, width), lambda i, *n: (0, 3)),
        pl.BlockSpec((width, ff), lambda i, *n: (0, 0)),
    ]


def finish_call(counts, x, mixed, w_first, w_up, w_down, small, rows=256, tile=768):
    total, width = x.shape
    ff = w_down.shape[0]
    groups = counts.shape[0]
    narrow, wide = rows_of(rows, width), rows_of(rows, ff)
    return pl.pallas_call(
        functools.partial(finish_kernel, tile=tile, seg=total // groups),
        grid_spec=pltpu.PrefetchScalarGridSpec(
            num_scalar_prefetch=1,
            grid=(total // rows,),
            in_specs=[
                narrow, narrow,
                *up_out_specs(width, ff), whole(w_down.shape),
                whole(small.shape),
            ],
            out_specs=[narrow, narrow, wide, wide, narrow, whole((groups, width))],
        ),
        out_shape=[
            jax.ShapeDtypeStruct((total, width), f32),
            jax.ShapeDtypeStruct((total, width), f32),
            jax.ShapeDtypeStruct((total, ff), bf16),
            jax.ShapeDtypeStruct((total, ff), bf16),
            jax.ShapeDtypeStruct((total, width), bf16),
            jax.ShapeDtypeStruct((groups, width), f32),
        ],
        compiler_params=pltpu.CompilerParams(vmem_limit_bytes=VMEM_CAP),
        cost_estimate=cost(2 * total * width * (width + 2 * ff), 40 << 20),
        name="finish",
    )(counts, x, mixed, w_first, w_up, w_down, small)


def finish_back_kernel(counts_ref, cot_ref, cls_ref, z1_ref, z2_ref, slope_ref, out_ref, up_ref, down_ref,
                       rows_ref,
                       outer_ref, inner_ref, resid_ref, attended_ref, mixed_ref, low_ref, sums_ref, *, tile, seg):
    step = pl.program_id(0)
    rows, width = cot_ref.shape

    @pl.when(step == 0)
    def _():
        sums_ref[...] = jnp.zeros_like(sums_ref)

    at = lax.broadcasted_iota(jnp.int32, (seg, width), 0)
    parts = []
    for s in range(rows // seg):
        here = step * (rows // seg) + s
        block = cot_ref[s * seg : (s + 1) * seg].astype(f32)
        block = jnp.where(at == 0, cls_ref[pl.ds(here, 1), :], block)
        parts.append(jnp.where(at < counts_ref[here], block, 0.0))
    g = jnp.concatenate(parts, axis=0)
    _, unit_two, inv_two = normalize(z2_ref[...], rows_ref[1:2], rows_ref[3:4])
    grad_two = norm_back_rows(g, unit_two, inv_two, rows_ref[1:2])
    outer = grad_two.astype(bf16)
    outer_ref[...] = outer
    sums_ref[1:2] += jnp.sum(g * unit_two, axis=0, keepdims=True)
    sums_ref[3:4] += jnp.sum(g, axis=0, keepdims=True)
    first_grad = grad_two
    for t in range(up_ref.shape[1] // tile):
        cols = pl.ds(t * tile, tile)
        inner = (dot_nt(outer, down_ref[cols, :]) * slope_ref[:, cols].astype(f32)).astype(bf16)
        inner_ref[:, cols] = inner
        first_grad = first_grad + dot_nt(inner, up_ref[:, cols])
    first, unit_one, inv_one = normalize(z1_ref[...], rows_ref[0:1], rows_ref[2:3])
    low_ref[...] = first.astype(bf16)
    grad_one = norm_back_rows(first_grad, unit_one, inv_one, rows_ref[0:1])
    resid_ref[...] = grad_one
    sums_ref[0:1] += jnp.sum(first_grad * unit_one, axis=0, keepdims=True)
    sums_ref[2:3] += jnp.sum(first_grad, axis=0, keepdims=True)
    attended = grad_one.astype(bf16)
    attended_ref[...] = attended
    mixed_ref[...] = dot_nt(attended, out_ref[...]).astype(bf16)


def finish_back_call(counts, cot, cls_grad, z1, z2, slope, w_first, w_up, w_down, small, rows=256, tile=768):
    total, width = cot.shape
    ff = w_down.shape[0]
    groups = counts.shape[0]
    narrow, wide = rows_of(rows, width), rows_of(rows, ff)
    return pl.pallas_call(
        functools.partial(finish_back_kernel, tile=tile, seg=total // groups),
        grid_spec=pltpu.PrefetchScalarGridSpec(
            num_scalar_prefetch=1,
            grid=(total // rows,),
            in_specs=[
                narrow, whole((groups, width)), narrow, narrow, wide,
                *up_out_specs(width, ff), whole(w_down.shape),
                whole(small.shape),
            ],
            out_specs=[narrow, wide, narrow, narrow, narrow, narrow, whole((16, width))],
        ),
        out_shape=[
            jax.ShapeDtypeStruct((total, width), bf16),
            jax.ShapeDtypeStruct((total, ff), bf16),
            jax.ShapeDtypeStruct((total, width), f32),
            jax.ShapeDtypeStruct((total, width), bf16),
            jax.ShapeDtypeStruct((total, width), bf16),
            jax.ShapeDtypeStruct((total, width), bf16),
            jax.ShapeDtypeStruct((16, width), f32),
        ],
        compiler_params=pltpu.CompilerParams(vmem_limit_bytes=VMEM_CAP),
        cost_estimate=cost(2 * total * width * (width + 2 * ff), 40 << 20),
        name="finish_back",
    )(counts, cot, cls_grad, z1, z2, slope, w_first, w_up, w_down, small)


def row_blocks_kernel(ids_ref, a_ref, b_ref, *refs, count):
    extra, (mine_ref, send_ref, turned_ref) = refs[:-3], refs[-3:]
    c, f = ids_ref[0], ids_ref[1]
    half = turned_ref.shape[0] // 2
    unit = half // count

    def place(ref, value):
        for block in range(count):
            for h in range(2):
                to = pl.multiple_of((h ^ c) * half + (block ^ f) * unit, 16)
                ref[pl.ds(to, unit), :] = value[(block * 2 + h) * unit : (block * 2 + h + 1) * unit]

    @pl.when(pl.program_id(0) == 0)
    def _():
        place(turned_ref, a_ref[...].T)

    tile = b_ref.shape[1]
    result = dot(turned_ref[...], b_ref[...]).astype(bf16)
    mine_ref[:, :tile] = result[:half]
    send_ref[:, :tile] = result[half:]
    if extra:
        sums_ref, = extra
        low = sums_ref[...].astype(bf16)
        lanes = lax.broadcasted_iota(jnp.int32, (low.shape[0], 128), 1)
        eye = (lax.broadcasted_iota(jnp.int32, (low.shape[0], 128), 0) == lanes).astype(bf16)
        turned = dot_tn(low, eye).astype(bf16)
        for block in range(count):
            for h in range(2):
                value = turned[(block * 2 + h) * unit : (block * 2 + h + 1) * unit]
                to = pl.multiple_of((block ^ f) * unit, 16)

                @pl.when(h == c)
                def _():
                    mine_ref[pl.ds(to, unit), tile:] = value

                @pl.when(h != c)
                def _():
                    send_ref[pl.ds(to, unit), tile:] = value


def row_blocks_call(ids, a, b, count, sums=None, tile=768):
    total, width = a.shape
    cols = b.shape[1]
    full = cols if sums is None else cols + 128
    step = tile if sums is None else full
    out = pl.BlockSpec((width // 2, step), lambda i, n: (0, i))
    more = [] if sums is None else [sums]
    return pl.pallas_call(
        functools.partial(row_blocks_kernel, count=count),
        grid_spec=pltpu.PrefetchScalarGridSpec(
            num_scalar_prefetch=1,
            grid=(cols // tile,),
            in_specs=[whole(a.shape), pl.BlockSpec((total, tile), lambda i, n: (0, i))] + [whole(m.shape) for m in more],
            out_specs=[out, out],
            scratch_shapes=[pltpu.VMEM((width, total), bf16)],
        ),
        out_shape=[jax.ShapeDtypeStruct((width // 2, full), bf16)] * 2,
        compiler_params=pltpu.CompilerParams(vmem_limit_bytes=VMEM_CAP),
        cost_estimate=cost(2 * total * width * cols * 2, 16 << 20),
        name="row_blocks",
    )(ids, a, b, *more)


def wide_blocks_kernel(ids_ref, a_ref, b_ref, mine_ref, send_ref):
    c = ids_ref[0]
    half = b_ref.shape[1] // 2

    def rows_at(h):
        at = pl.multiple_of(h * half, 128)
        return dot_tn(b_ref[:, pl.ds(at, half)], a_ref[...]).astype(bf16)

    mine_ref[0] = rows_at(c)
    send_ref[0] = rows_at(1 - c)


def wide_blocks_call(ids, a, b, count):
    total, width = a.shape
    block = b.shape[1] // count
    out = pl.BlockSpec((1, block // 2, width), lambda i, n: (i ^ n[1], 0, 0))
    return pl.pallas_call(
        wide_blocks_kernel,
        grid_spec=pltpu.PrefetchScalarGridSpec(
            num_scalar_prefetch=1,
            grid=(count,),
            in_specs=[whole(a.shape), pl.BlockSpec((total, block), lambda i, n: (0, i))],
            out_specs=[out, out],
        ),
        out_shape=[jax.ShapeDtypeStruct((count, block // 2, width), bf16)] * 2,
        compiler_params=pltpu.CompilerParams(vmem_limit_bytes=VMEM_CAP),
        cost_estimate=cost(2 * total * width * b.shape[1] * 2, 16 << 20),
        name="wide_blocks",
    )(ids, a, b)


def token_grad_kernel(resid_ref, g_ref, w_ref, o_ref):
    o_ref[...] = (resid_ref[...] + dot_nt(g_ref[...], w_ref[...])).astype(bf16)


def token_grad_call(resid, g, w_qkv, rows=256):
    total, width = resid.shape
    return pl.pallas_call(
        token_grad_kernel,
        grid=(total // rows,),
        in_specs=[rows_of(rows, width), rows_of(rows, 3 * width), whole((width, 3 * width))],
        out_specs=rows_of(rows, width),
        out_shape=jax.ShapeDtypeStruct((total, width), bf16),
        compiler_params=pltpu.CompilerParams(vmem_limit_bytes=VMEM_CAP),
        cost_estimate=cost(12 * total * width * width, 16 << 20),
        name="token_grad",
    )(resid, g, w_qkv)


def cross_message(cse_qkv, cse_out, cse_up, cse_down, fsize, f):
    rows, width = cse_qkv.shape[0], cse_out.shape[1]
    ff = cse_up.shape[1]
    slim = width // fsize
    cols = jnp.concatenate(
        [
            cse_qkv.reshape(rows, 3, fsize, slim).transpose(2, 0, 1, 3).reshape(fsize, rows, 3 * slim),
            cse_up.reshape(rows, fsize, ff // fsize).transpose(1, 0, 2),
        ],
        axis=-1,
    )
    mine = in_order([part(cols, f, 0)] + [swap_f(part(cols, f ^ d, 0), d) for d in (1, 2, 3)])
    flat = mine.reshape(fsize * rows, -1)
    frows = cse_down.shape[0]
    out_flat = jnp.concatenate([cse_out[:, k * slim : (k + 1) * slim] for k in range(fsize)], axis=0)
    return jnp.concatenate([flat, cse_down, out_flat], axis=-1)


def unpack_kernel(m_ref, qkv_ref, out_ref, up_ref, down_ref, *, fsize):
    reps, frows, _ = m_ref.shape
    rows = frows // fsize
    width, a = qkv_ref.shape
    b, slim = a + up_ref.shape[1], width // fsize
    for r in range(reps):
        for k in range(fsize):
            at, here = k * reps * rows + r * rows, slice(k * rows, (k + 1) * rows)
            qkv_ref[at : at + rows, :] = m_ref[r, here, :a]
            up_ref[at : at + rows, :] = m_ref[r, here, a:b]
        down_ref[r * frows : (r + 1) * frows, :] = m_ref[r, :, b : b + width]
        out = [m_ref[r, k * rows : (k + 1) * rows, b + width :] for k in range(fsize)]
        out_ref[r * rows : (r + 1) * rows, :] = jnp.concatenate(out, axis=-1)


def cross_unpack(gathered, width, ff, fsize):
    reps, frows = gathered.shape[:2]
    slim = width // fsize
    if frows // fsize % 8:
        return cross_unpack_small(gathered, width, ff, fsize)
    shapes = [(width, 3 * slim), (slim, width), (width, ff // fsize), (ff // fsize, width)]
    return pl.pallas_call(
        functools.partial(unpack_kernel, fsize=fsize),
        out_shape=[jax.ShapeDtypeStruct(shape, bf16) for shape in shapes],
        compiler_params=pltpu.CompilerParams(vmem_limit_bytes=VMEM_CAP),
        name="unpack",
    )(gathered)


def cross_unpack_small(gathered, width, ff, fsize):
    slim = width // fsize
    reps, frows = gathered.shape[:2]
    rows = frows // fsize
    a, b = 3 * slim, 3 * slim + ff // fsize
    by_row = gathered[:, :, :b].reshape(reps, fsize, rows, b).transpose(1, 0, 2, 3).reshape(-1, b)
    qkv = by_row[:, :a]
    up = by_row[:, a:]
    down = gathered[:, :, b : b + width].reshape(-1, width)
    out = gathered[:, :, b + width :].reshape(reps, fsize, rows, slim).transpose(0, 2, 1, 3).reshape(-1, width)
    return qkv, out, up, down


def cross_block(cls_in, cotan, weights, gains, biases, fsize, f):
    qkv, out, up, down = weights
    segs, width = cls_in.shape
    slim = width // fsize
    heads = slim // HEAD
    packed = product(cls_in[None], qkv, "gsd,de->gse").astype(bf16)
    queries, keys, values = split_heads(packed, heads)
    every = jnp.ones((1, segs), jnp.bool_)
    mixed, log_total = attend(queries, keys, values, every)
    mixed = mixed.reshape(segs, slim)
    attended = sum_f(product(mixed, out, "sd,de->se"))
    first, unit_one, inv_one = normalize(cls_in.astype(f32) + attended, gains[0], biases[0])
    first_low = first.astype(bf16)
    activated, slope = gelu_pair(product(first_low, up, "sd,df->sf"))
    act_low = activated.astype(bf16)
    outer = sum_f(product(act_low, down, "sf,fd->sd"))
    cls_out, unit_two, inv_two = normalize(first + outer, gains[1], biases[1])

    grad_two, gain_two, bias_two = norm_back(cotan, unit_two, inv_two, gains[1])
    grad_outer = grad_two.astype(bf16)
    grad_inner = (product(grad_outer, down, "sd,fd->sf") * slope).astype(bf16)
    grad_first = grad_two + sum_f(product(grad_inner, up, "sf,df->sd"))
    grad_one, gain_one, bias_one = norm_back(grad_first, unit_one, inv_one, gains[0])
    grad_attended = grad_one.astype(bf16)
    grad_mixed = product(grad_attended, out, "se,de->sd").astype(bf16)
    grad_q, grad_k, grad_v = attend_back(
        queries, keys, values, every, log_total, grad_mixed.reshape(1, segs, heads, HEAD)
    )
    grad_packed = jnp.concatenate(
        [grad_q.reshape(segs, slim), grad_k.reshape(segs, slim), grad_v.reshape(segs, slim)], axis=-1
    ).astype(bf16)
    grad_in = grad_one + sum_f(product(grad_packed, qkv, "se,de->sd"))

    def own(value):
        return lax.dynamic_slice_in_dim(value, f * slim, slim, value.ndim - 1)

    sums = jnp.stack([gain_one, gain_two, bias_one, bias_two])
    pieces = {
        "packed": grad_packed,
        "inner": grad_inner,
        "act": act_low,
        "outer": grad_outer,
        "attended": grad_attended,
        "mixed": mixed,
        "own_in": own(cls_in),
        "own_low": own(first_low),
        "own_grad": own(grad_in).astype(bf16),
        "sums": jnp.pad(own(sums), ((0, segs - 4), (0, 0))).astype(bf16),
    }
    return cls_out, grad_in, pieces


def doc_message(spread, pieces, fsize, width):
    segs = spread.shape[1]
    slim = width // fsize
    qkv_cols = spread[:, :, : 3 * slim].reshape(fsize, segs, 3, slim).transpose(1, 2, 0, 3)
    parts = {"packed": qkv_cols.reshape(segs, 3 * width), "inner": spread[:, :, 3 * slim :].transpose(1, 0, 2).reshape(segs, -1)}
    parts = {**pieces, **parts}
    ends, at = {}, 0
    for name, value in parts.items():
        ends[name] = (at, at + value.shape[1])
        at += value.shape[1] + -value.shape[1] % 128
    parts = {k: jnp.pad(v, ((0, 0), (0, -v.shape[1] % 128))) for k, v in parts.items()}
    return jnp.concatenate(list(parts.values()), axis=-1), ends


def cross_grads(docs, ends, names):
    flat = docs.reshape(-1, docs.shape[-1])

    def cut(name):
        return flat[:, slice(*ends[name])]

    pairs = {"qkv": ("own_in", "packed"), "out": ("mixed", "attended"), "up": ("own_low", "inner"), "down": ("act", "outer")}
    grads = {k: product(cut(pairs[k][0]), cut(pairs[k][1]), "rd,re->de") for k in names if k in pairs}
    if "rest" in names:
        grads["positions"] = jnp.sum(docs[:, :, slice(*ends["own_grad"])].astype(f32), axis=0)
        sums = jnp.sum(docs[:, :4, slice(*ends["sums"])].astype(f32), axis=0)
        grads["gains"], grads["biases"] = sums[0:2], sums[2:4]
    return grads


def per_device(
    tokens, counts, cotangent,
    swe_qkv, swe_out, swe_up, swe_down, swe_gains, swe_biases,
    cse_qkv, cse_out, cse_up, cse_down, cse_gains, cse_biases, positions,
):
    docs_here, local_len, width = tokens.shape
    ff = swe_up.shape[1]
    seg_here = counts.shape[1]
    groups = docs_here * seg_here
    fsize = lax.axis_size("y") * lax.axis_size("x")
    f = lax.axis_index("y") * lax.axis_size("x") + lax.axis_index("x")
    c = lax.axis_index("c")
    ids = jnp.stack([c, f])
    segs = fsize * seg_here
    x = tokens.reshape(-1, width)
    cot = cotangent.reshape(-1, width)
    lens = counts.reshape(groups)

    small = [swe_gains, swe_biases, cse_gains, cse_biases, positions]
    count_small = sum(v.shape[0] for v in small)
    packed_up = pack_call(swe_up, small)
    w_up = lax.all_gather(packed_up, ("y", "x", "z", "c"), axis=0, tiled=True)
    first = RowGather(tie(jnp.concatenate([swe_qkv, swe_out], axis=-1), packed_up))
    first.far_z()
    down = RowGather(tie(swe_down, first.state))
    first.near_z()
    first.after(down.state)
    down.after(first.state)
    turned = first.state
    first.plane_first()
    down.far_z()
    message = cross_message(*tie((cse_qkv, cse_out, cse_up, cse_down), turned), fsize, f)
    down.after(first.state)
    first.after(down.state, message)
    first.plane_second()
    down.near_z()
    first.after(down.state)
    down.after(first.state)
    first.sibling()
    w_first = side_by_side(*first.state, c)
    down.plane_first(w_first)
    packed, mixed = attend_call(lens, x, tie(w_first, down.state))
    down.plane_second(packed)
    w_up = tie(w_up, packed, down.state)
    down.after(w_up)
    cross = lax.all_gather(tie(message, w_up), ("z", "c"), axis=0)
    down.sibling()
    w_down = side_by_side(*down.state, c)
    rows = turn_call(w_up, ff // 128)
    gains, biases, cross_gains, cross_biases, pos = (
        rows[0:2], rows[2:4], rows[4:6], rows[6:8], rows[8:count_small]
    )
    z1, z2, act, slope, hidden, cls_rows = finish_call(lens, x, mixed, w_first, w_up, w_down, rows)
    cross_w = cross_unpack(cross, width, ff, fsize)

    pos_here = lax.dynamic_slice_in_dim(pos, f * seg_here, seg_here, 0)
    cls_here = (cls_rows + pos_here).astype(bf16)
    cls_cot = cot.reshape(groups, -1, width)[:, 0]
    both = gather_f(jnp.concatenate([cls_here, cls_cot], axis=-1), cross_w).reshape(segs, 2 * width)
    cls_out, cls_grad, pieces = cross_block(
        both[:, :width], both[:, width:].astype(f32), cross_w, cross_gains, cross_biases, fsize, f,
    )
    cls_out = lax.dynamic_slice_in_dim(cls_out, f * seg_here, seg_here, 0)
    cls_here_grad = lax.dynamic_slice_in_dim(cls_grad, f * seg_here, seg_here, 0)

    spread = tie(jnp.concatenate([pieces["packed"], pieces["inner"]], axis=-1), cls_grad)
    outer, inner, resid, attended, grad_mixed, low, sums = finish_back_call(
        lens, cot, tie(cls_here_grad, spread), z1, z2, slope, w_first, w_up, w_down, rows
    )
    spread = gather_f(spread, outer)
    layer_out = hidden.reshape(groups, -1, width).at[:, 0].set(tie(cls_out.astype(bf16), outer))
    message, ends = doc_message(tie(spread, outer), pieces, fsize, width)
    docs = lax.all_gather(message, ("z", "c"), axis=0)
    red_down, red_up, red_qkv = RowReduce(), RowReduce(), RowReduce()
    g_down = wide_blocks_call(ids, tie(outer, message), act, fsize)
    g_out = row_blocks_call(ids, tie(mixed, g_down), attended, fsize, sums)
    red_down.core(g_down, g_out)
    red_down.chip()
    g_up = row_blocks_call(ids, tie(low, red_down.state), inner, fsize)
    red_down.plane_first(g_up)
    red_up.core(g_out, g_up)
    red_up.core(tie(g_up, red_down.state))
    red_up.chip()
    red_down.after(red_up.state)
    grad_packed = attend_back_call(lens, packed, tie(grad_mixed, red_up.state, red_down.state))
    red_down.plane_second(grad_packed)
    red_up.plane_first(grad_packed)
    red_down.after(grad_packed, red_up.state)
    red_up.after(red_down.state)
    g_qkv = row_blocks_call(ids, x, tie(grad_packed, red_up.state, red_down.state), fsize)
    red_up.plane_second(g_qkv)
    red_down.near_z(g_qkv)
    red_qkv.core(tie(g_qkv, red_up.state))
    red_qkv.chip_direct()
    token_grad = token_grad_call(tie(resid, red_qkv.state), grad_packed, w_first)
    red_down.far_z(token_grad)
    red_up.near_z(token_grad)
    others = cross_grads(tie(docs, token_grad), ends, ("up", "qkv"))
    red_qkv.plane_direct(token_grad, others)
    lead = red_qkv.state
    later = cross_grads(tie(docs, lead), ends, ("down", "out", "rest"))
    others |= later
    red_down.back_far(token_grad, lead)
    red_up.far_z(token_grad, lead)
    red_qkv.near_z(later)
    lead = red_qkv.state
    red_down.back_near(lead)
    red_up.back_far(lead)
    red_qkv.far_z()
    lead = red_qkv.state
    red_down.back_core(lead)
    red_up.back_near(lead)
    red_qkv.back_far()
    lead = red_qkv.state
    red_up.back_core(lead)
    done_down = red_down.state.astype(f32)
    red_qkv.back_near()
    red_qkv.after(done_down, layer_out, others)
    red_qkv.back_core()
    done_up = red_up.state.astype(f32)
    done_qkv = red_qkv.state.astype(f32)
    pick = (jnp.arange(128)[None, :] == jnp.arange(4)[:, None]).astype(bf16)
    small_grads = product(pick, red_up.state[:, width : width + 128], "kc,rc->kr")
    return (
        layer_out.reshape(tokens.shape),
        token_grad.reshape(tokens.shape),
        done_qkv,
        done_up[:, :width],
        done_up[:, width + 128 :],
        done_down,
        small_grads[0:2],
        small_grads[2:4],
    ) + tuple(others[k] for k in ("qkv", "out", "up", "down", "gains", "biases", "positions"))


def solution(mesh):
    fsize, rsize = mesh.shape["fsdp"], mesh.shape["rep"]
    fine = Mesh(mesh.devices.reshape(2, fsize // 2, rsize // 2, 2), ("y", "x", "z", "c"))
    fs, rep = ("y", "x"), ("z", "c")
    every = fs + rep
    by_rows, by_cols = P(every, None), P(None, every)
    block = (by_rows,) * 4 + (by_cols,) * 2
    grads = (P(fs, None),) * 4 + (P(None, fs),) * 2
    return jax.shard_map(
        per_device,
        mesh=fine,
        in_specs=(P(rep, fs, None), P(rep, fs), P(rep, fs, None)) + block + block + (by_cols,),
        out_specs=(P(rep, fs, None),) * 2 + grads + grads + (P(None, fs),),
        check_vma=False,
    )
```

```python
import functools
import math

import jax
import jax.numpy as jnp
from jax import lax
from jax.experimental import pallas as pl
from jax.experimental.pallas import tpu as pltpu
from jax.sharding import Mesh
from jax.sharding import PartitionSpec as P

HEAD = 64
norm_eps = 1e-05
masked_score = -1000000000.0
bf16, f32 = jnp.bfloat16, jnp.float32
VMEM_CAP = 56 << 20


def tie(values, *after):
    return lax.optimization_barrier((values, after))[0]


def swap(value, axis, bit, then=()):
    size = lax.axis_size(axis)
    got = lax.ppermute(value, axis, [(i, i ^ bit) for i in range(size)])
    return tie(got, then) if then else got


def bit_of(axis, bit):
    return (lax.axis_index(axis) // bit) % 2


def join(mine, other, side, axis):
    first = side == 0
    return jnp.stack([jnp.where(first, mine, other), jnp.where(first, other, mine)], axis=axis)


def side_by_side(mine, other, side):
    both = jnp.concatenate([other, other], axis=-1)
    return lax.dynamic_update_slice_in_dim(both, mine, side * mine.shape[-1], axis=-1)


def part(value, side, axis):
    return lax.dynamic_index_in_dim(value, side, axis, keepdims=False)


def bits_down(size):
    return [1 << k for k in reversed(range(size.bit_length() - 1))]


class RowGather:
    def __init__(self, shard):
        rows, cols = shard.shape
        half = cols // 2
        c = lax.axis_index("c")
        keep = lax.dynamic_slice_in_dim(shard, c * half, half, 1)
        send = lax.dynamic_slice_in_dim(shard, (1 - c) * half, half, 1)
        self.state = join(keep, swap(send, "c", 1), c, 0).reshape(1, 2 * rows, half)

    def after(self, *others):
        self.state = tie(self.state, others)

    def far_z(self, *then):
        bits = bits_down(lax.axis_size("z"))
        for bit in bits[:-1]:
            self._along_z(bit, then)

    def near_z(self, *then):
        self._along_z(1, then)

    def _along_z(self, bit, then=()):
        got = self.state
        got = join(got, swap(got, "z", bit, then), bit_of("z", bit), 1)
        self.state = got.reshape((-1,) + got.shape[2:])

    def plane_first(self, *then):
        zhalf = self.state.shape[0] // 2
        one, two = self.state[:zhalf], self.state[zhalf:]
        got_one, got_two = swap(one, "x", 1, then), swap(two, "y", 1, then)
        self.state = join(one, got_one, lax.axis_index("x"), 0), join(two, got_two, lax.axis_index("y"), 0)

    def plane_second(self, *then):
        one, two = self.state
        got_one, got_two = swap(one, "y", 1, then), swap(two, "x", 1, then)
        one = join(one, got_one, lax.axis_index("y"), 0)
        two = join(two, got_two, lax.axis_index("x"), 1)
        both = jnp.concatenate([one, two], axis=2)
        self.state = both.reshape(-1, both.shape[-1])

    def sibling(self, *then):
        self.state = self.state, swap(self.state, "c", 1, then)


class RepGather:
    def __init__(self, message):
        self.state = message[None]

    far_z = RowGather.far_z
    near_z = RowGather.near_z
    after = RowGather.after

    def _along_z(self, bit, then=()):
        got = self.state
        got = join(got, swap(got, "z", bit, then), bit_of("z", bit), 1)
        self.state = got.reshape((-1,) + got.shape[2:])

    def sibling(self, *then):
        self.state = join(self.state, swap(self.state, "c", 1, then), lax.axis_index("c"), 1)


def swap_f(value, dist, then=()):
    count = lax.axis_size("y") * lax.axis_size("x")
    got = lax.ppermute(value, ("y", "x"), [(i, i ^ dist) for i in range(count)])
    return tie(got, then) if then else got


def in_order(parts):
    y, x = lax.axis_index("y"), lax.axis_index("x")
    row0 = [jnp.where(x == 0, parts[0], parts[1]), jnp.where(x == 0, parts[1], parts[0])]
    row1 = [jnp.where(x == 0, parts[2], parts[3]), jnp.where(x == 0, parts[3], parts[2])]
    top, low = jnp.stack(row0), jnp.stack(row1)
    return jnp.concatenate([jnp.where(y == 0, top, low), jnp.where(y == 0, low, top)])


def gather_f(value, *then):
    return in_order([value] + [swap_f(value, d, then) for d in (1, 2, 3)])


def sum_f(value):
    got = [value] + [swap_f(value, d) for d in (1, 2, 3)]
    return (got[0] + got[1]) + (got[2] + got[3])


def add(*terms):
    total = terms[0].astype(f32)
    for term in terms[1:]:
        total = total + term.astype(f32)
    return total.astype(bf16)


class RowReduce:
    def __init__(self):
        self.parts = []

    def after(self, *others):
        self.state = tie(self.state, others)

    def core(self, pair, *then):
        self.parts.append((pair[0], swap(pair[1], "c", 1, then)))

    def after_core(self, *others):
        self.parts = tie(self.parts, others)

    def chip_direct(self):
        count = lax.axis_size("y") * lax.axis_size("x")
        mine, got = (p.reshape((count, -1) + p.shape[-1:]) for p in self.parts[0])
        self.state = [add(mine[d], got[d]) for d in range(count)]

    def plane_direct(self, *then):
        got = [swap_f(self.state[d], d, then) for d in (1, 2, 3)]
        plane = add(self.state[0], *got)
        zsize = lax.axis_size("z")
        self.state = plane.reshape(zsize, plane.shape[0] // zsize, plane.shape[1])

    def chip(self):
        count = lax.axis_size("y") * lax.axis_size("x")

        def some(blocks, lower):
            out = []
            for d in blocks:
                cuts = []
                for mine, got in self.parts:
                    mine = mine.reshape((count, -1) + mine.shape[-1:])
                    got = got.reshape(mine.shape)
                    half = mine.shape[1] // 2
                    cut = slice(half, None) if lower else slice(None, half)
                    cuts.append(add(mine[d, cut], got[d, cut]))
                out.append(jnp.concatenate(cuts, axis=-1))
            return jnp.stack(out)

        self.state = some((0, 2), False), some((1, 3), False), some((0, 1), True), some((2, 3), True)

    def plane_first(self, *then):
        keep_upper, send_upper, keep_lower, send_lower = self.state
        got_upper, got_lower = swap(send_upper, "x", 1, then), swap(send_lower, "y", 1, then)
        self.state = (
            add(keep_upper[0], got_upper[0]), add(keep_upper[1], got_upper[1]),
            add(keep_lower[0], got_lower[0]), add(keep_lower[1], got_lower[1]),
        )

    def plane_second(self, *then):
        keep_upper, send_upper, keep_lower, send_lower = self.state
        got_upper, got_lower = swap(send_upper, "y", 1, then), swap(send_lower, "x", 1, then)
        plane = jnp.concatenate([add(keep_upper, got_upper), add(keep_lower, got_lower)], axis=0)
        zsize = lax.axis_size("z")
        self.state = plane.reshape(zsize, plane.shape[0] // zsize, plane.shape[1])

    def near_z(self, *then):
        self._along_z(1, then)

    def far_z(self, *then):
        for bit in reversed(bits_down(lax.axis_size("z"))[:-1]):
            self._along_z(bit, then)

    def _along_z(self, bit, then=()):
        side = bit_of("z", bit)
        pairs = self.state.reshape((-1, 2) + self.state.shape[1:])
        other = swap(part(pairs, 1 - side, 1), "z", bit, then)
        self.state = add(part(pairs, side, 1), other)

    def back_far(self, *then):
        self.back = RepGather(self.state[0])
        self.back.far_z(*then)
        self.state = self.back.state

    def back_near(self, *then):
        self.back.state = self.state
        self.back.near_z(*then)
        self.state = self.back.state

    def back_core(self, *then):
        mine = self.state.reshape(-1, self.state.shape[-1])
        both = join(mine, swap(mine, "c", 1, then), lax.axis_index("c"), 0)
        self.state = both.reshape(-1, both.shape[-1])


def product(left_op, right_op, einsum_form):
    return jnp.einsum(einsum_form, left_op, right_op, preferred_element_type=f32)


def normalize(summed_in, gain_row, bias_row):
    row_mean = jnp.mean(summed_in, axis=-1, keepdims=True)
    centered = summed_in - row_mean
    inv_dev = lax.rsqrt(jnp.mean(centered * centered, axis=-1, keepdims=True) + norm_eps)
    unit_rows = centered * inv_dev
    return (unit_rows * gain_row + bias_row, unit_rows, inv_dev)


def norm_back(upstream, unit_rows, inv_dev, gain_row):
    scaled = upstream * gain_row
    grad_in = inv_dev * (
        scaled
        - jnp.mean(scaled, axis=-1, keepdims=True)
        - unit_rows * jnp.mean(scaled * unit_rows, axis=-1, keepdims=True)
    )
    sums = tuple(range(upstream.ndim - 1))
    return (grad_in, jnp.sum(upstream * unit_rows, axis=sums), jnp.sum(upstream, axis=sums))


def gelu_pair(inner_pre):
    cumul = 0.5 * (1.0 + lax.erf(inner_pre * 0.7071067811865476))
    return (
        inner_pre * cumul,
        cumul + inner_pre * jnp.exp(-0.5 * inner_pre * inner_pre) * 0.3989422804014327,
    )


def masked_scores(query_rows, key_rows, key_mask):
    raw_scores = product(query_rows, key_rows, "gqhe,gkhe->ghqk") * (1.0 / math.sqrt(HEAD))
    return jnp.where(key_mask[:, None, None, :], raw_scores, masked_score)


def attend(query_rows, key_rows, value_rows, key_mask):
    scores = masked_scores(query_rows, key_rows, key_mask)
    row_max = jnp.max(scores, axis=-1, keepdims=True)
    log_total = row_max + jnp.log(jnp.sum(jnp.exp(scores - row_max), axis=-1, keepdims=True))
    softmax_w = jnp.exp(scores - log_total).astype(bf16)
    mixed_heads = product(softmax_w, value_rows, "ghqk,gkhe->gqhe").astype(bf16)
    return (mixed_heads, log_total)


def attend_back(query_rows, key_rows, value_rows, key_mask, log_total, grad_mixed):
    scores = masked_scores(query_rows, key_rows, key_mask)
    softmax_w = jnp.exp(scores - log_total)
    grad_value = product(softmax_w.astype(bf16), grad_mixed, "ghqk,gqhe->gkhe")
    grad_probs = product(grad_mixed, value_rows, "gqhe,gkhe->ghqk")
    grad_scores = (
        softmax_w * (grad_probs - jnp.sum(softmax_w * grad_probs, axis=-1, keepdims=True))
    ).astype(bf16)
    inv_root = 1.0 / math.sqrt(HEAD)
    grad_query = product(grad_scores, key_rows, "ghqk,gkhe->gqhe") * inv_root
    grad_key = product(grad_scores, query_rows, "ghqk,gqhe->gkhe") * inv_root
    return (grad_query, grad_key, grad_value)


def split_heads(packed, head_count):
    stacked = packed.reshape(packed.shape[0], packed.shape[1], 3, head_count, HEAD)
    return (stacked[:, :, 0], stacked[:, :, 1], stacked[:, :, 2])


def dot(a, b):
    return lax.dot_general(a, b, (((1,), (0,)), ((), ())), preferred_element_type=f32)


def dot_nt(a, b):
    return lax.dot_general(a, b, (((1,), (1,)), ((), ())), preferred_element_type=f32)


def dot_tn(a, b):
    return lax.dot_general(a, b, (((0,), (0,)), ((), ())), preferred_element_type=f32)


def norm_back_rows(upstream, unit_rows, inv_dev, gain_row):
    scaled = upstream * gain_row
    return inv_dev * (
        scaled
        - jnp.mean(scaled, axis=-1, keepdims=True)
        - unit_rows * jnp.mean(scaled * unit_rows, axis=-1, keepdims=True)
    )


def pair_of(value, low_half):
    zero = jnp.zeros_like(value)
    return jnp.concatenate([jnp.where(low_half, value, zero), jnp.where(low_half, zero, value)], axis=0)


def pair_probs(keys, queries_two, key_ok):
    scores = jnp.where(key_ok, dot_nt(keys, queries_two), masked_score)
    e = jnp.exp(scores - jnp.max(scores, axis=0, keepdims=True))
    return e * (1.0 / jnp.sum(e, axis=0, keepdims=True))


def cost(flops, moved):
    return pl.CostEstimate(flops=flops, bytes_accessed=moved, transcendentals=0)


def attend_kernel(counts_ref, x_ref, w_ref, packed_ref, mixed_ref, *, seg):
    step = pl.program_id(0)
    rows, width = x_ref.shape
    packed_ref[...] = dot(x_ref[...], w_ref[...]).astype(bf16)
    low_half = lax.broadcasted_iota(jnp.int32, (seg, 2 * HEAD), 1) < HEAD
    key_at = lax.broadcasted_iota(jnp.int32, (seg, 2 * seg), 0)
    for s in range(rows // seg):
        key_ok = key_at < counts_ref[step * (rows // seg) + s]
        r = pl.ds(s * seg, seg)
        for p in range(width // (2 * HEAD)):
            col = p * 2 * HEAD
            q = packed_ref[r, pl.ds(col, 2 * HEAD)] * jnp.asarray(HEAD**-0.5, bf16)
            k = packed_ref[r, pl.ds(width + col, 2 * HEAD)]
            v = packed_ref[r, pl.ds(2 * width + col, 2 * HEAD)]
            probs = pair_probs(k, pair_of(q, low_half), key_ok).astype(bf16)
            both = dot_tn(probs, v)
            mixed_ref[r, pl.ds(col, 2 * HEAD)] = jnp.where(low_half, both[:seg], both[seg:]).astype(bf16)


def attend_call(counts, x, w_qkv, rows=256):
    total, width = x.shape
    return pl.pallas_call(
        functools.partial(attend_kernel, seg=total // counts.shape[0]),
        grid_spec=pltpu.PrefetchScalarGridSpec(
            num_scalar_prefetch=1,
            grid=(total // rows,),
            in_specs=[
                pl.BlockSpec((rows, width), lambda i, n: (i, 0)),
                pl.BlockSpec((width, 3 * width), lambda i, n: (0, 0)),
            ],
            out_specs=[
                pl.BlockSpec((rows, 3 * width), lambda i, n: (i, 0)),
                pl.BlockSpec((rows, width), lambda i, n: (i, 0)),
            ],
        ),
        out_shape=[
            jax.ShapeDtypeStruct((total, 3 * width), bf16),
            jax.ShapeDtypeStruct((total, width), bf16),
        ],
        compiler_params=pltpu.CompilerParams(vmem_limit_bytes=VMEM_CAP),
        cost_estimate=cost(8 * total * width * width, 16 << 20),
        name="attend",
    )(counts, x, w_qkv)


def attend_back_kernel(counts_ref, packed_ref, grad_ref, out_ref, *, seg):
    step = pl.program_id(0)
    rows, width = grad_ref.shape
    low_half = lax.broadcasted_iota(jnp.int32, (seg, 2 * HEAD), 1) < HEAD
    key_at = lax.broadcasted_iota(jnp.int32, (seg, 2 * seg), 0)
    root = jnp.asarray(HEAD**-0.5, bf16)
    for s in range(rows // seg):
        key_ok = key_at < counts_ref[step * (rows // seg) + s]
        r = pl.ds(s * seg, seg)
        for p in range(width // (2 * HEAD)):
            col = p * 2 * HEAD
            q_two = pair_of(packed_ref[r, pl.ds(col, 2 * HEAD)] * root, low_half)
            k = packed_ref[r, pl.ds(width + col, 2 * HEAD)]
            v = packed_ref[r, pl.ds(2 * width + col, 2 * HEAD)]
            g_two = pair_of(grad_ref[r, pl.ds(col, 2 * HEAD)], low_half)
            probs = pair_probs(k, q_two, key_ok)
            grad_v = dot(probs.astype(bf16), g_two)
            grad_p = dot_nt(v, g_two)
            weighted = probs * grad_p
            grad_s = (weighted - probs * jnp.sum(weighted, axis=0, keepdims=True)).astype(bf16)
            grad_k = dot(grad_s, q_two)
            both = dot_tn(grad_s, k) * (HEAD**-0.5)
            out_ref[r, pl.ds(col, 2 * HEAD)] = jnp.where(low_half, both[:seg], both[seg:]).astype(bf16)
            out_ref[r, pl.ds(width + col, 2 * HEAD)] = grad_k.astype(bf16)
            out_ref[r, pl.ds(2 * width + col, 2 * HEAD)] = grad_v.astype(bf16)


def attend_back_call(counts, packed, grad_mixed, rows=256):
    total, width = grad_mixed.shape
    return pl.pallas_call(
        functools.partial(attend_back_kernel, seg=total // counts.shape[0]),
        grid_spec=pltpu.PrefetchScalarGridSpec(
            num_scalar_prefetch=1,
            grid=(total // rows,),
            in_specs=[
                pl.BlockSpec((rows, 3 * width), lambda i, n: (i, 0)),
                pl.BlockSpec((rows, width), lambda i, n: (i, 0)),
            ],
            out_specs=pl.BlockSpec((rows, 3 * width), lambda i, n: (i, 0)),
        ),
        out_shape=jax.ShapeDtypeStruct((total, 3 * width), bf16),
        compiler_params=pltpu.CompilerParams(vmem_limit_bytes=VMEM_CAP),
        cost_estimate=cost(16 * total * width * width, 16 << 20),
        name="attend_back",
    )(counts, packed, grad_mixed)


def whole(shape):
    return pl.BlockSpec(shape, lambda *i: (0,) * len(shape))


def rows_of(rows, cols):
    return pl.BlockSpec((rows, cols), lambda i, *n: (i, 0))


def finish_kernel(counts_ref, x_ref, mixed_ref, out_ref, up_ref, down_ref, rows_ref,
                  z1_ref, z2_ref, act_ref, slope_ref, hidden_ref, cls_ref, *, tile, seg):
    step = pl.program_id(0)
    rows, width = x_ref.shape
    z1 = x_ref[...].astype(f32) + dot(mixed_ref[...], out_ref[...])
    z1_ref[...] = z1
    first, _, _ = normalize(z1, rows_ref[0:1], rows_ref[2:3])
    low = first.astype(bf16)
    total = first
    for t in range(up_ref.shape[1] // tile):
        cols = pl.ds(t * tile, tile)
        act, slope = gelu_pair(dot(low, up_ref[:, cols]))
        act = act.astype(bf16)
        act_ref[:, cols] = act
        slope_ref[:, cols] = slope.astype(bf16)
        total = total + dot(act, down_ref[cols, :])
    z2_ref[...] = total
    normed = normalize(total, rows_ref[1:2], rows_ref[3:4])[0]
    at = lax.broadcasted_iota(jnp.int32, (seg, width), 0)
    for s in range(rows // seg):
        here = step * (rows // seg) + s
        block = normed[s * seg : (s + 1) * seg]
        cls_ref[pl.ds(here, 1), :] = block[0:1]
        hidden_ref[s * seg : (s + 1) * seg] = jnp.where(at < counts_ref[here], block, 0.0).astype(bf16)


def pack_kernel(wide_ref, *refs):
    small, o_ref = refs[:-1], refs[-1]
    cols = wide_ref.shape[1]
    o_ref[:, :cols] = wide_ref[...]
    turned, at = 0.0, 0
    for ref in small:
        count = ref.shape[0]
        shape = (count, 128)
        one = lax.broadcasted_iota(jnp.int32, shape, 1) == lax.broadcasted_iota(jnp.int32, shape, 0) + at
        turned = turned + dot_tn(ref[...], one.astype(bf16))
        at += count
    o_ref[:, cols:] = turned.astype(bf16)


def pack_call(wide, small):
    return pl.pallas_call(
        pack_kernel,
        out_shape=jax.ShapeDtypeStruct((wide.shape[0], wide.shape[1] + 128), bf16),
        name="pack",
    )(wide, *small)


def turn_kernel(w_ref, o_ref):
    o_ref[...] = w_ref[...].astype(f32).T


def turn_call(w, at):
    return pl.pallas_call(
        turn_kernel,
        grid=(1,),
        in_specs=[pl.BlockSpec((w.shape[0], 128), lambda i: (0, at))],
        out_specs=whole((128, w.shape[0])),
        out_shape=jax.ShapeDtypeStruct((128, w.shape[0]), f32),
        name="turn",
    )(w)


def up_out_specs(width, ff):
    return [
        pl.BlockSpec((width, width), lambda i, *n: (0, 3)),
        pl.BlockSpec((width, ff), lambda i, *n: (0, 0)),
    ]


def finish_call(counts, x, mixed, w_first, w_up, w_down, small, rows=256, tile=768):
    total, width = x.shape
    ff = w_down.shape[0]
    groups = counts.shape[0]
    narrow, wide = rows_of(rows, width), rows_of(rows, ff)
    return pl.pallas_call(
        functools.partial(finish_kernel, tile=tile, seg=total // groups),
        grid_spec=pltpu.PrefetchScalarGridSpec(
            num_scalar_prefetch=1,
            grid=(total // rows,),
            in_specs=[
                narrow, narrow,
                *up_out_specs(width, ff), whole(w_down.shape),
                whole(small.shape),
            ],
            out_specs=[narrow, narrow, wide, wide, narrow, whole((groups, width))],
        ),
        out_shape=[
            jax.ShapeDtypeStruct((total, width), f32),
            jax.ShapeDtypeStruct((total, width), f32),
            jax.ShapeDtypeStruct((total, ff), bf16),
            jax.ShapeDtypeStruct((total, ff), bf16),
            jax.ShapeDtypeStruct((total, width), bf16),
            jax.ShapeDtypeStruct((groups, width), f32),
        ],
        compiler_params=pltpu.CompilerParams(vmem_limit_bytes=VMEM_CAP),
        cost_estimate=cost(2 * total * width * (width + 2 * ff), 40 << 20),
        name="finish",
    )(counts, x, mixed, w_first, w_up, w_down, small)


def finish_back_kernel(counts_ref, cot_ref, cls_ref, z1_ref, z2_ref, slope_ref, out_ref, up_ref, down_ref,
                       rows_ref,
                       outer_ref, inner_ref, resid_ref, attended_ref, mixed_ref, low_ref, sums_ref, *, tile, seg):
    step = pl.program_id(0)
    rows, width = cot_ref.shape

    @pl.when(step == 0)
    def _():
        sums_ref[...] = jnp.zeros_like(sums_ref)

    at = lax.broadcasted_iota(jnp.int32, (seg, width), 0)
    parts = []
    for s in range(rows // seg):
        here = step * (rows // seg) + s
        block = cot_ref[s * seg : (s + 1) * seg].astype(f32)
        block = jnp.where(at == 0, cls_ref[pl.ds(here, 1), :], block)
        parts.append(jnp.where(at < counts_ref[here], block, 0.0))
    g = jnp.concatenate(parts, axis=0)
    _, unit_two, inv_two = normalize(z2_ref[...], rows_ref[1:2], rows_ref[3:4])
    grad_two = norm_back_rows(g, unit_two, inv_two, rows_ref[1:2])
    outer = grad_two.astype(bf16)
    outer_ref[...] = outer
    sums_ref[1:2] += jnp.sum(g * unit_two, axis=0, keepdims=True)
    sums_ref[3:4] += jnp.sum(g, axis=0, keepdims=True)
    first_grad = grad_two
    for t in range(up_ref.shape[1] // tile):
        cols = pl.ds(t * tile, tile)
        inner = (dot_nt(outer, down_ref[cols, :]) * slope_ref[:, cols].astype(f32)).astype(bf16)
        inner_ref[:, cols] = inner
        first_grad = first_grad + dot_nt(inner, up_ref[:, cols])
    first, unit_one, inv_one = normalize(z1_ref[...], rows_ref[0:1], rows_ref[2:3])
    low_ref[...] = first.astype(bf16)
    grad_one = norm_back_rows(first_grad, unit_one, inv_one, rows_ref[0:1])
    resid_ref[...] = grad_one
    sums_ref[0:1] += jnp.sum(first_grad * unit_one, axis=0, keepdims=True)
    sums_ref[2:3] += jnp.sum(first_grad, axis=0, keepdims=True)
    attended = grad_one.astype(bf16)
    attended_ref[...] = attended
    mixed_ref[...] = dot_nt(attended, out_ref[...]).astype(bf16)


def finish_back_call(counts, cot, cls_grad, z1, z2, slope, w_first, w_up, w_down, small, rows=256, tile=768):
    total, width = cot.shape
    ff = w_down.shape[0]
    groups = counts.shape[0]
    narrow, wide = rows_of(rows, width), rows_of(rows, ff)
    return pl.pallas_call(
        functools.partial(finish_back_kernel, tile=tile, seg=total // groups),
        grid_spec=pltpu.PrefetchScalarGridSpec(
            num_scalar_prefetch=1,
            grid=(total // rows,),
            in_specs=[
                narrow, whole((groups, width)), narrow, narrow, wide,
                *up_out_specs(width, ff), whole(w_down.shape),
                whole(small.shape),
            ],
            out_specs=[narrow, wide, narrow, narrow, narrow, narrow, whole((16, width))],
        ),
        out_shape=[
            jax.ShapeDtypeStruct((total, width), bf16),
            jax.ShapeDtypeStruct((total, ff), bf16),
            jax.ShapeDtypeStruct((total, width), f32),
            jax.ShapeDtypeStruct((total, width), bf16),
            jax.ShapeDtypeStruct((total, width), bf16),
            jax.ShapeDtypeStruct((total, width), bf16),
            jax.ShapeDtypeStruct((16, width), f32),
        ],
        compiler_params=pltpu.CompilerParams(vmem_limit_bytes=VMEM_CAP),
        cost_estimate=cost(2 * total * width * (width + 2 * ff), 40 << 20),
        name="finish_back",
    )(counts, cot, cls_grad, z1, z2, slope, w_first, w_up, w_down, small)


def row_blocks_kernel(ids_ref, a_ref, b_ref, *refs, count):
    extra, (mine_ref, send_ref, turned_ref) = refs[:-3], refs[-3:]
    c, f = ids_ref[0], ids_ref[1]
    half = turned_ref.shape[0] // 2
    unit = half // count

    def place(ref, value):
        for block in range(count):
            for h in range(2):
                to = pl.multiple_of((h ^ c) * half + (block ^ f) * unit, 16)
                ref[pl.ds(to, unit), :] = value[(block * 2 + h) * unit : (block * 2 + h + 1) * unit]

    @pl.when(pl.program_id(0) == 0)
    def _():
        place(turned_ref, a_ref[...].T)

    tile = b_ref.shape[1]
    result = dot(turned_ref[...], b_ref[...]).astype(bf16)
    mine_ref[:, :tile] = result[:half]
    send_ref[:, :tile] = result[half:]
    if extra:
        sums_ref, = extra
        low = sums_ref[...].astype(bf16)
        lanes = lax.broadcasted_iota(jnp.int32, (low.shape[0], 128), 1)
        eye = (lax.broadcasted_iota(jnp.int32, (low.shape[0], 128), 0) == lanes).astype(bf16)
        turned = dot_tn(low, eye).astype(bf16)
        for block in range(count):
            for h in range(2):
                value = turned[(block * 2 + h) * unit : (block * 2 + h + 1) * unit]
                to = pl.multiple_of((block ^ f) * unit, 16)

                @pl.when(h == c)
                def _():
                    mine_ref[pl.ds(to, unit), tile:] = value

                @pl.when(h != c)
                def _():
                    send_ref[pl.ds(to, unit), tile:] = value


def row_blocks_call(ids, a, b, count, sums=None, tile=768):
    total, width = a.shape
    cols = b.shape[1]
    full = cols if sums is None else cols + 128
    step = tile if sums is None else full
    out = pl.BlockSpec((width // 2, step), lambda i, n: (0, i))
    more = [] if sums is None else [sums]
    return pl.pallas_call(
        functools.partial(row_blocks_kernel, count=count),
        grid_spec=pltpu.PrefetchScalarGridSpec(
            num_scalar_prefetch=1,
            grid=(cols // tile,),
            in_specs=[whole(a.shape), pl.BlockSpec((total, tile), lambda i, n: (0, i))] + [whole(m.shape) for m in more],
            out_specs=[out, out],
            scratch_shapes=[pltpu.VMEM((width, total), bf16)],
        ),
        out_shape=[jax.ShapeDtypeStruct((width // 2, full), bf16)] * 2,
        compiler_params=pltpu.CompilerParams(vmem_limit_bytes=VMEM_CAP),
        cost_estimate=cost(2 * total * width * cols * 2, 16 << 20),
        name="row_blocks",
    )(ids, a, b, *more)


def wide_blocks_kernel(ids_ref, a_ref, b_ref, mine_ref, send_ref):
    c = ids_ref[0]
    half = b_ref.shape[1] // 2

    def rows_at(h):
        at = pl.multiple_of(h * half, 128)
        return dot_tn(b_ref[:, pl.ds(at, half)], a_ref[...]).astype(bf16)

    mine_ref[0] = rows_at(c)
    send_ref[0] = rows_at(1 - c)


def wide_blocks_call(ids, a, b, count):
    total, width = a.shape
    block = b.shape[1] // count
    out = pl.BlockSpec((1, block // 2, width), lambda i, n: (i ^ n[1], 0, 0))
    return pl.pallas_call(
        wide_blocks_kernel,
        grid_spec=pltpu.PrefetchScalarGridSpec(
            num_scalar_prefetch=1,
            grid=(count,),
            in_specs=[whole(a.shape), pl.BlockSpec((total, block), lambda i, n: (0, i))],
            out_specs=[out, out],
        ),
        out_shape=[jax.ShapeDtypeStruct((count, block // 2, width), bf16)] * 2,
        compiler_params=pltpu.CompilerParams(vmem_limit_bytes=VMEM_CAP),
        cost_estimate=cost(2 * total * width * b.shape[1] * 2, 16 << 20),
        name="wide_blocks",
    )(ids, a, b)


def token_grad_kernel(resid_ref, g_ref, w_ref, o_ref):
    o_ref[...] = (resid_ref[...] + dot_nt(g_ref[...], w_ref[...])).astype(bf16)


def token_grad_call(resid, g, w_qkv, rows=256):
    total, width = resid.shape
    return pl.pallas_call(
        token_grad_kernel,
        grid=(total // rows,),
        in_specs=[rows_of(rows, width), rows_of(rows, 3 * width), whole((width, 3 * width))],
        out_specs=rows_of(rows, width),
        out_shape=jax.ShapeDtypeStruct((total, width), bf16),
        compiler_params=pltpu.CompilerParams(vmem_limit_bytes=VMEM_CAP),
        cost_estimate=cost(12 * total * width * width, 16 << 20),
        name="token_grad",
    )(resid, g, w_qkv)


def cross_message(cse_qkv, cse_out, cse_up, cse_down, fsize, f):
    rows, width = cse_qkv.shape[0], cse_out.shape[1]
    ff = cse_up.shape[1]
    slim = width // fsize
    cols = jnp.concatenate(
        [
            cse_qkv.reshape(rows, 3, fsize, slim).transpose(2, 0, 1, 3).reshape(fsize, rows, 3 * slim),
            cse_up.reshape(rows, fsize, ff // fsize).transpose(1, 0, 2),
        ],
        axis=-1,
    )
    mine = in_order([part(cols, f, 0)] + [swap_f(part(cols, f ^ d, 0), d) for d in (1, 2, 3)])
    flat = mine.reshape(fsize * rows, -1)
    frows = cse_down.shape[0]
    out_flat = jnp.concatenate([cse_out[:, k * slim : (k + 1) * slim] for k in range(fsize)], axis=0)
    return jnp.concatenate([flat, cse_down, out_flat], axis=-1)


def unpack_kernel(m_ref, qkv_ref, out_ref, up_ref, down_ref, *, fsize):
    reps, frows, _ = m_ref.shape
    rows = frows // fsize
    width, a = qkv_ref.shape
    b, slim = a + up_ref.shape[1], width // fsize
    for r in range(reps):
        for k in range(fsize):
            at, here = k * reps * rows + r * rows, slice(k * rows, (k + 1) * rows)
            qkv_ref[at : at + rows, :] = m_ref[r, here, :a]
            up_ref[at : at + rows, :] = m_ref[r, here, a:b]
        down_ref[r * frows : (r + 1) * frows, :] = m_ref[r, :, b : b + width]
        out = [m_ref[r, k * rows : (k + 1) * rows, b + width :] for k in range(fsize)]
        out_ref[r * rows : (r + 1) * rows, :] = jnp.concatenate(out, axis=-1)


def cross_unpack(gathered, width, ff, fsize):
    reps, frows = gathered.shape[:2]
    slim = width // fsize
    if frows // fsize % 8:
        return cross_unpack_small(gathered, width, ff, fsize)
    shapes = [(width, 3 * slim), (slim, width), (width, ff // fsize), (ff // fsize, width)]
    return pl.pallas_call(
        functools.partial(unpack_kernel, fsize=fsize),
        out_shape=[jax.ShapeDtypeStruct(shape, bf16) for shape in shapes],
        compiler_params=pltpu.CompilerParams(vmem_limit_bytes=VMEM_CAP),
        name="unpack",
    )(gathered)


def cross_unpack_small(gathered, width, ff, fsize):
    slim = width // fsize
    reps, frows = gathered.shape[:2]
    rows = frows // fsize
    a, b = 3 * slim, 3 * slim + ff // fsize
    by_row = gathered[:, :, :b].reshape(reps, fsize, rows, b).transpose(1, 0, 2, 3).reshape(-1, b)
    qkv = by_row[:, :a]
    up = by_row[:, a:]
    down = gathered[:, :, b : b + width].reshape(-1, width)
    out = gathered[:, :, b + width :].reshape(reps, fsize, rows, slim).transpose(0, 2, 1, 3).reshape(-1, width)
    return qkv, out, up, down


def cross_block(cls_in, cotan, weights, gains, biases, fsize, f):
    qkv, out, up, down = weights
    segs, width = cls_in.shape
    slim = width // fsize
    heads = slim // HEAD
    packed = product(cls_in[None], qkv, "gsd,de->gse").astype(bf16)
    queries, keys, values = split_heads(packed, heads)
    every = jnp.ones((1, segs), jnp.bool_)
    mixed, log_total = attend(queries, keys, values, every)
    mixed = mixed.reshape(segs, slim)
    attended = sum_f(product(mixed, out, "sd,de->se"))
    first, unit_one, inv_one = normalize(cls_in.astype(f32) + attended, gains[0], biases[0])
    first_low = first.astype(bf16)
    activated, slope = gelu_pair(product(first_low, up, "sd,df->sf"))
    act_low = activated.astype(bf16)
    outer = sum_f(product(act_low, down, "sf,fd->sd"))
    cls_out, unit_two, inv_two = normalize(first + outer, gains[1], biases[1])

    grad_two, gain_two, bias_two = norm_back(cotan, unit_two, inv_two, gains[1])
    grad_outer = grad_two.astype(bf16)
    grad_inner = (product(grad_outer, down, "sd,fd->sf") * slope).astype(bf16)
    grad_first = grad_two + sum_f(product(grad_inner, up, "sf,df->sd"))
    grad_one, gain_one, bias_one = norm_back(grad_first, unit_one, inv_one, gains[0])
    grad_attended = grad_one.astype(bf16)
    grad_mixed = product(grad_attended, out, "se,de->sd").astype(bf16)
    grad_q, grad_k, grad_v = attend_back(
        queries, keys, values, every, log_total, grad_mixed.reshape(1, segs, heads, HEAD)
    )
    grad_packed = jnp.concatenate(
        [grad_q.reshape(segs, slim), grad_k.reshape(segs, slim), grad_v.reshape(segs, slim)], axis=-1
    ).astype(bf16)
    grad_in = grad_one + sum_f(product(grad_packed, qkv, "se,de->sd"))

    def own(value):
        return lax.dynamic_slice_in_dim(value, f * slim, slim, value.ndim - 1)

    sums = jnp.stack([gain_one, gain_two, bias_one, bias_two])
    pieces = {
        "packed": grad_packed,
        "inner": grad_inner,
        "act": act_low,
        "outer": grad_outer,
        "attended": grad_attended,
        "mixed": mixed,
        "own_in": own(cls_in),
        "own_low": own(first_low),
        "own_grad": own(grad_in).astype(bf16),
        "sums": jnp.pad(own(sums), ((0, segs - 4), (0, 0))).astype(bf16),
    }
    return cls_out, grad_in, pieces


def doc_message(spread, pieces, fsize, width):
    segs = spread.shape[1]
    slim = width // fsize
    qkv_cols = spread[:, :, : 3 * slim].reshape(fsize, segs, 3, slim).transpose(1, 2, 0, 3)
    parts = {"packed": qkv_cols.reshape(segs, 3 * width), "inner": spread[:, :, 3 * slim :].transpose(1, 0, 2).reshape(segs, -1)}
    parts = {**pieces, **parts}
    ends, at = {}, 0
    for name, value in parts.items():
        ends[name] = (at, at + value.shape[1])
        at += value.shape[1] + -value.shape[1] % 128
    parts = {k: jnp.pad(v, ((0, 0), (0, -v.shape[1] % 128))) for k, v in parts.items()}
    return jnp.concatenate(list(parts.values()), axis=-1), ends


def cross_grads(docs, ends, names):
    flat = docs.reshape(-1, docs.shape[-1])

    def cut(name):
        return flat[:, slice(*ends[name])]

    pairs = {"qkv": ("own_in", "packed"), "out": ("mixed", "attended"), "up": ("own_low", "inner"), "down": ("act", "outer")}
    grads = {k: product(cut(pairs[k][0]), cut(pairs[k][1]), "rd,re->de") for k in names if k in pairs}
    if "rest" in names:
        grads["positions"] = jnp.sum(docs[:, :, slice(*ends["own_grad"])].astype(f32), axis=0)
        sums = jnp.sum(docs[:, :4, slice(*ends["sums"])].astype(f32), axis=0)
        grads["gains"], grads["biases"] = sums[0:2], sums[2:4]
    return grads


def per_device(
    tokens, counts, cotangent,
    swe_qkv, swe_out, swe_up, swe_down, swe_gains, swe_biases,
    cse_qkv, cse_out, cse_up, cse_down, cse_gains, cse_biases, positions,
):
    docs_here, local_len, width = tokens.shape
    ff = swe_up.shape[1]
    seg_here = counts.shape[1]
    groups = docs_here * seg_here
    fsize = lax.axis_size("y") * lax.axis_size("x")
    f = lax.axis_index("y") * lax.axis_size("x") + lax.axis_index("x")
    c = lax.axis_index("c")
    ids = jnp.stack([c, f])
    segs = fsize * seg_here
    x = tokens.reshape(-1, width)
    cot = cotangent.reshape(-1, width)
    lens = counts.reshape(groups)

    small = [swe_gains, swe_biases, cse_gains, cse_biases, positions]
    count_small = sum(v.shape[0] for v in small)
    packed_up = pack_call(swe_up, small)
    w_up = lax.all_gather(packed_up, ("y", "x", "z", "c"), axis=0, tiled=True)
    first = RowGather(tie(jnp.concatenate([swe_qkv, swe_out], axis=-1), packed_up))
    first.far_z()
    down = RowGather(tie(swe_down, first.state))
    first.near_z()
    first.after(down.state)
    down.after(first.state)
    turned = first.state
    first.plane_first()
    down.far_z()
    message = cross_message(*tie((cse_qkv, cse_out, cse_up, cse_down), turned), fsize, f)
    down.after(first.state)
    first.after(down.state, message)
    first.plane_second()
    down.near_z()
    first.after(down.state)
    down.after(first.state)
    first.sibling()
    w_first = side_by_side(*first.state, c)
    down.plane_first(w_first)
    packed, mixed = attend_call(lens, x, tie(w_first, down.state))
    down.plane_second(packed)
    w_up = tie(w_up, packed, down.state)
    down.after(w_up)
    cross = lax.all_gather(tie(message, w_up), ("z", "c"), axis=0)
    down.sibling()
    w_down = side_by_side(*down.state, c)
    rows = turn_call(w_up, ff // 128)
    gains, biases, cross_gains, cross_biases, pos = (
        rows[0:2], rows[2:4], rows[4:6], rows[6:8], rows[8:count_small]
    )
    z1, z2, act, slope, hidden, cls_rows = finish_call(lens, x, mixed, w_first, w_up, w_down, rows)
    cross_w = cross_unpack(cross, width, ff, fsize)

    pos_here = lax.dynamic_slice_in_dim(pos, f * seg_here, seg_here, 0)
    cls_here = (cls_rows + pos_here).astype(bf16)
    cls_cot = cot.reshape(groups, -1, width)[:, 0]
    both = gather_f(jnp.concatenate([cls_here, cls_cot], axis=-1), cross_w).reshape(segs, 2 * width)
    cls_out, cls_grad, pieces = cross_block(
        both[:, :width], both[:, width:].astype(f32), cross_w, cross_gains, cross_biases, fsize, f,
    )
    cls_out = lax.dynamic_slice_in_dim(cls_out, f * seg_here, seg_here, 0)
    cls_here_grad = lax.dynamic_slice_in_dim(cls_grad, f * seg_here, seg_here, 0)

    spread = tie(jnp.concatenate([pieces["packed"], pieces["inner"]], axis=-1), cls_grad)
    outer, inner, resid, attended, grad_mixed, low, sums = finish_back_call(
        lens, cot, tie(cls_here_grad, spread), z1, z2, slope, w_first, w_up, w_down, rows
    )
    spread = gather_f(spread, outer)
    message, ends = doc_message(tie(spread, outer), pieces, fsize, width)
    docs = lax.all_gather(message, ("z", "c"), axis=0)
    red_down, red_up, red_qkv = RowReduce(), RowReduce(), RowReduce()
    g_down = wide_blocks_call(ids, tie(outer, message), act, fsize)
    g_out = row_blocks_call(ids, tie(mixed, g_down), attended, fsize, sums)
    red_down.core(g_down, g_out)
    red_down.chip()
    g_up = row_blocks_call(ids, tie(low, red_down.state), inner, fsize)
    red_down.plane_first(g_up)
    red_up.core(g_out, g_up)
    red_up.core(tie(g_up, red_down.state))
    red_up.chip()
    red_down.after(red_up.state)
    grad_packed = attend_back_call(lens, packed, tie(grad_mixed, red_up.state, red_down.state))
    red_down.plane_second(grad_packed)
    red_up.plane_first(grad_packed)
    red_down.after(grad_packed, red_up.state)
    red_up.after(red_down.state)
    g_qkv = row_blocks_call(ids, x, tie(grad_packed, red_up.state, red_down.state), fsize)
    red_up.plane_second(g_qkv)
    red_down.near_z(g_qkv)
    red_qkv.core(tie(g_qkv, red_up.state))
    red_qkv.chip_direct()
    token_grad = token_grad_call(tie(resid, red_qkv.state), grad_packed, w_first)
    red_down.far_z(token_grad)
    red_up.near_z(token_grad)
    others = cross_grads(tie(docs, token_grad), ends, ("up", "qkv"))
    red_qkv.plane_direct(token_grad, others)
    lead = red_qkv.state
    later = cross_grads(tie(docs, lead), ends, ("down", "out", "rest"))
    others |= later
    red_down.back_far(token_grad, lead)
    red_up.far_z(token_grad, lead)
    red_qkv.near_z(later)
    lead = red_qkv.state
    layer_out = hidden.reshape(groups, -1, width).at[:, 0].set(tie(cls_out.astype(bf16), lead))
    red_down.back_near(lead)
    red_up.back_far(lead)
    red_qkv.far_z()
    lead = red_qkv.state
    red_down.back_core(lead)
    red_up.back_near(lead)
    red_qkv.back_far()
    lead = red_qkv.state
    red_up.back_core(lead)
    done_down = red_down.state.astype(f32)
    red_qkv.back_near()
    red_qkv.after(done_down, layer_out, others)
    red_qkv.back_core()
    done_up = red_up.state.astype(f32)
    done_qkv = red_qkv.state.astype(f32)
    pick = (jnp.arange(128)[None, :] == jnp.arange(4)[:, None]).astype(bf16)
    small_grads = product(pick, red_up.state[:, width : width + 128], "kc,rc->kr")
    return (
        layer_out.reshape(tokens.shape),
        token_grad.reshape(tokens.shape),
        done_qkv,
        done_up[:, :width],
        done_up[:, width + 128 :],
        done_down,
        small_grads[0:2],
        small_grads[2:4],
    ) + tuple(others[k] for k in ("qkv", "out", "up", "down", "gains", "biases", "positions"))


def solution(mesh):
    fsize, rsize = mesh.shape["fsdp"], mesh.shape["rep"]
    fine = Mesh(mesh.devices.reshape(2, fsize // 2, rsize // 2, 2), ("y", "x", "z", "c"))
    fs, rep = ("y", "x"), ("z", "c")
    every = fs + rep
    by_rows, by_cols = P(every, None), P(None, every)
    block = (by_rows,) * 4 + (by_cols,) * 2
    grads = (P(fs, None),) * 4 + (P(None, fs),) * 2
    return jax.shard_map(
        per_device,
        mesh=fine,
        in_specs=(P(rep, fs, None), P(rep, fs), P(rep, fs, None)) + block + block + (by_cols,),
        out_specs=(P(rep, fs, None),) * 2 + grads + grads + (P(None, fs),),
        check_vma=False,
    )
```
